512 devices in a mesh: row: 16 (over y, z_lo), col: 32 (over z_hi, x, core).
Axes of the slice: x: 4, y: 8, z: 8 (z_hi: 4, z_lo: 2; z = z_hi * 2 + z_lo), core: 2. Of those that a mesh axis runs over, the one named last changes fastest.
Arguments:
- tiles: bfloat16 [16, 32, 32, 256, 256], P('row', 'col'), may hold values from -6 to 6
- tile_ids: int32 [16, 32, 2, 32], P('row', 'col'), may hold values from 0 to 7, as said below
- tile_count: int32 [16, 32], P('row', 'col'), may hold values from 8 to 32
- query_degree: int32 [32768], P('row'), may hold values from 1 to 32
- product_degree: int32 [65536], P('col'), may hold values from 1 to 32
- panel: float32 [64, 65536], P(None, ('col', 'row')), may hold values from -6 to 6
Outputs:
- basis: float32 [64, 65536], P(None, ('col', 'row'))
The draws below stay inside these ranges and needn't reach their ends.
Inputs may be any that keep to these rules, and one draw needn't show every extreme that they name: `tile_ids`: on each device the 32 (tile row, tile column) pairs are distinct; tile row is below 8 and tile column below 8.
All inputs are finite; a program needn't handle non-finite values.
Results may differ from the reference program's by a relative error of at most 0.0042.
Values may be sent and summed in bfloat16 or wider, within the bound.
A program may use at most 64 MiB of HBM per device.

```python
import jax
import jax.numpy as jnp
from jax import lax

TS = 256
R = 64
QB = 8
PB = 8
KT = 32
ITERS = 2
NQ = 32768
NP = 65536
N_ROW = 16
N_COL = 32


def draw_degrees(key, length, stream):
    key = jax.random.fold_in(key, stream)
    first_key, second_key = jax.random.split(key)
    factor = jax.random.randint(first_key, (length,), 1, 5)
    exponent = jax.random.randint(second_key, (length,), 0, 4)
    degree = factor * jnp.left_shift(jnp.ones((length,), jnp.int32), exponent)
    return degree.at[0].set(32).at[1].set(1).astype(jnp.int32)


def draw_query_degree(key, part):
    return draw_degrees(key, NQ, 11)


def draw_product_degree(key, part):
    return draw_degrees(key, NP, 12)


def draw_tile_ids(key, part):
    key = jax.random.fold_in(key, 21)
    device_keys = jax.random.split(key, N_ROW * N_COL)

    def device_order(device_key):
        remaining = 1 + jax.random.permutation(device_key, QB * PB - 2)
        positions = jnp.concatenate([jnp.array([QB * PB - 1], jnp.int32), jnp.array([0], jnp.int32), remaining.astype(jnp.int32)])[:KT]
        return jnp.stack([positions // PB, positions % PB])
    return jax.vmap(device_order)(device_keys).reshape(N_ROW, N_COL, 2, KT).astype(jnp.int32)


def draw_tile_count(key, part):
    key = jax.random.fold_in(key, 31)
    lowest = max(2, KT // 4)
    counts = jax.random.randint(key, (N_ROW * N_COL,), lowest, KT + 1)
    return counts.at[0].set(KT).at[1].set(lowest).reshape(N_ROW, N_COL).astype(jnp.int32)


def steps_of(rng, shape, shards, smallest, largest):
    factor_of, own = 1.0, jax.random.fold_in(rng, 6)
    for dim, parts in shards:
        steps = jnp.exp(jax.random.uniform(jax.random.fold_in(own, dim), (parts,), jnp.float32, smallest / len(shards), largest / len(shards)))
        factor_of = factor_of * jnp.repeat(steps, shape[dim] // parts).reshape([-1 if axis == dim else 1 for axis in range(len(shape))])
    return factor_of


def scatter_about(key, extent, width, reach, cuts=(), kind=jnp.bfloat16):
    factor_of = steps_of(key, extent, cuts, -0.22, 0.18) if cuts else 1.0
    result = jax.random.normal(key, extent, jnp.float32) * width * factor_of
    return jnp.minimum(jnp.maximum(result, -reach), reach).astype(kind)


def setup_inputs(seed: int = 0) -> dict:
    key_list = jax.random.split(jax.random.key(seed), 7)
    return {
        "tiles": scatter_about(key_list[0], (N_ROW, N_COL, KT, TS, TS), 1.0, 6.0, ((0, 16), (1, 32))),
        "tile_ids": draw_tile_ids(jax.random.fold_in(key_list[6], 71), 0),
        "tile_count": draw_tile_count(jax.random.fold_in(key_list[6], 71), 0),
        "query_degree": draw_query_degree(jax.random.fold_in(key_list[6], 71), 0),
        "product_degree": draw_product_degree(jax.random.fold_in(key_list[6], 71), 0),
        "panel": scatter_about(key_list[5], (R, NP), 1.0, 6.0, ((1, 512),), jnp.float32),
    }


HIGH = lax.Precision.HIGHEST

def reference(tiles, tile_ids, tile_count, query_degree, product_degree, panel):
    qscale = 1.0 / jnp.sqrt(query_degree.astype(jnp.float32))
    pscale = 1.0 / jnp.sqrt(product_degree.astype(jnp.float32))
    live_slot = (jnp.arange(KT, dtype=jnp.int32)[None, None, :] < tile_count[:, :, None]).astype(jnp.float32)
    row_hot = (tile_ids[:, :, 0, :, None] == jnp.arange(QB, dtype=jnp.int32)).astype(jnp.float32) * live_slot[..., None]
    col_hot = (tile_ids[:, :, 1, :, None] == jnp.arange(PB, dtype=jnp.int32)).astype(jnp.float32) * live_slot[..., None]
    qgrid = qscale.reshape(N_ROW, 1, QB, TS)
    pgrid = pscale.reshape(N_COL, 1, PB, TS)
    current = panel
    for iteration in range(ITERS):
        scaled = (current * pscale[None, :]).astype(jnp.bfloat16).astype(jnp.float32)
        scaled_blocks = jnp.transpose(scaled.reshape(R, N_COL, PB, TS), (1, 0, 2, 3))

        def query_rows(inputs):
            tiles_r, rhot_r, chot_r = inputs

            def device_terms(running, items):
                tile_set, rhot, chot, block = items
                picked = jnp.einsum('kp,rpj->rkj', chot, block, precision=HIGH)
                products = jnp.einsum('rkj,kij->kri', picked, tile_set.astype(jnp.float32), precision=HIGH)
                return (running + jnp.einsum('kq,kri->rqi', rhot, products, precision=HIGH), None)
            running, unused = lax.scan(device_terms, jnp.zeros((R, QB, TS), jnp.float32), (tiles_r, rhot_r, chot_r, scaled_blocks))
            return running
        row_sums = lax.map(query_rows, (tiles, row_hot, col_hot))
        query_panel = (row_sums * qgrid).astype(jnp.bfloat16).astype(jnp.float32)

        def product_rows(running, items):
            tiles_r, rhot_r, chot_r, ublock = items

            def device_terms(inputs):
                tile_set, rhot, chot = inputs
                picked = jnp.einsum('kq,rqi->rki', rhot, ublock, precision=HIGH)
                products = jnp.einsum('rki,kij->krj', picked, tile_set.astype(jnp.float32), precision=HIGH)
                return jnp.einsum('kp,krj->rpj', chot, products, precision=HIGH)
            return (running + lax.map(device_terms, (tiles_r, rhot_r, chot_r)), None)
        col_sums, unused = lax.scan(product_rows, jnp.zeros((N_COL, R, PB, TS), jnp.float32), (tiles, row_hot, col_hot, query_panel))
        lifted = jnp.transpose(col_sums * pgrid, (1, 0, 2, 3)).reshape(R, N_COL * PB * TS)
        gram = jnp.einsum('ri,si->rs', lifted, lifted, precision=HIGH)
        lower = jnp.linalg.cholesky(gram)
        current = lax.linalg.triangular_solve(lower, lifted, left_side=True, lower=True)
    return current * jnp.sqrt(jnp.float32(NP))
```

```python
import functools
import math

import jax
import jax.numpy as jnp
from jax import lax
from jax.experimental import pallas as pl
from jax.experimental.pallas import tpu as pltpu
from jax.sharding import PartitionSpec as P

ITERS = 2


HIGH = lax.Precision.HIGHEST

AXES = ("row", "col")


def _device(axis, peer):
    if axis == "row":
        return (peer, lax.axis_index("col"))
    return (lax.axis_index("row"), peer)


def _exchange_kernel(x_ref, y_ref, buf, send_sems, recv_sems, *, axis, n, bcast):
    me = lax.axis_index(axis)
    barrier = pltpu.get_barrier_semaphore()

    def greet(k, carry):
        peer = lax.rem(me + k, n)
        pl.semaphore_signal(barrier, inc=1, device_id=_device(axis, peer),
                            device_id_type=pl.DeviceIdType.MESH)
        return carry

    lax.fori_loop(1, n, greet, 0)
    pl.semaphore_wait(barrier, n - 1)

    def source(peer):
        return x_ref.at[0] if bcast else x_ref.at[peer]

    def send(k, carry):
        peer = lax.rem(me + k, n)
        pltpu.make_async_remote_copy(
            src_ref=source(peer), dst_ref=buf.at[me],
            send_sem=send_sems.at[peer], recv_sem=recv_sems.at[me],
            device_id=_device(axis, peer), device_id_type=pl.DeviceIdType.MESH,
        ).start()
        return carry

    lax.fori_loop(1, n, send, 0)
    if bcast:
        y_ref[me] = x_ref[0]
    else:
        y_ref[me] = x_ref[me]

    def finish(k, carry):
        peer = lax.rem(me + k, n)
        pltpu.make_async_remote_copy(
            src_ref=source(peer), dst_ref=buf.at[me],
            send_sem=send_sems.at[peer], recv_sem=recv_sems.at[me],
            device_id=_device(axis, peer), device_id_type=pl.DeviceIdType.MESH,
        ).wait_send()
        pltpu.make_async_remote_copy(
            src_ref=source(peer), dst_ref=buf.at[peer],
            send_sem=send_sems.at[peer], recv_sem=recv_sems.at[peer],
            device_id=_device(axis, peer), device_id_type=pl.DeviceIdType.MESH,
        ).wait_recv()
        y_ref[peer] = buf[peer]
        return carry

    lax.fori_loop(1, n, finish, 0)


def exchange(x, axis, n, bcast, cid):
    chunk = x.shape[1:]
    nbytes = n * math.prod(chunk) * x.dtype.itemsize
    return pl.pallas_call(
        functools.partial(_exchange_kernel, axis=axis, n=n, bcast=bcast),
        out_shape=jax.ShapeDtypeStruct((n,) + chunk, x.dtype),
        in_specs=[pl.BlockSpec(memory_space=pltpu.VMEM)],
        out_specs=pl.BlockSpec(memory_space=pltpu.VMEM),
        scratch_shapes=[
            pltpu.VMEM((n,) + chunk, x.dtype),
            pltpu.SemaphoreType.DMA((n,)),
            pltpu.SemaphoreType.DMA((n,)),
        ],
        compiler_params=pltpu.CompilerParams(collective_id=cid, has_side_effects=True),
        cost_estimate=pl.CostEstimate(flops=0, transcendentals=0, bytes_accessed=3 * nbytes),
    )(x)


def orthonormal(lifted, gram):
    lower = jnp.linalg.cholesky(gram)
    return lax.linalg.triangular_solve(lower, lifted, left_side=True, lower=True)


def shards(tiles, tile_ids, tile_count, query_degree, product_degree, panel):
    tile_set = tiles[0, 0]
    slot_ids = tile_ids[0, 0]
    live_count = tile_count[0, 0]
    slots = tile_set.shape[0]
    side = tile_set.shape[1]
    width = panel.shape[0]
    query_tiles = query_degree.shape[0] // side
    product_tiles = product_degree.shape[0] // side
    n_row = lax.axis_size("row")
    n_col = lax.axis_size("col")
    live_slot = (jnp.arange(slots, dtype=jnp.int32) < live_count).astype(jnp.float32)
    row_hot = (slot_ids[0][:, None] == jnp.arange(query_tiles, dtype=jnp.int32)[None, :]).astype(
        jnp.float32
    ) * live_slot[:, None]
    col_hot = (slot_ids[1][:, None] == jnp.arange(product_tiles, dtype=jnp.int32)[None, :]).astype(
        jnp.float32
    ) * live_slot[:, None]
    qscale = 1.0 / jnp.sqrt(query_degree.astype(jnp.float32))
    pscale = 1.0 / jnp.sqrt(product_degree.astype(jnp.float32))
    row_at = lax.axis_index("row")
    col_at = lax.axis_index("col")
    share = panel.shape[1]
    block = pscale.shape[0]
    qchunk = query_degree.shape[0] // n_col
    my_pscale = lax.dynamic_slice_in_dim(pscale, row_at * share, share)
    my_qscale = lax.dynamic_slice_in_dim(qscale, col_at * qchunk, qchunk)
    root_count = math.sqrt(product_degree.shape[0] * n_col)

    scaled0 = (panel * my_pscale[None, :]).astype(jnp.bfloat16)
    gathered = exchange(scaled0[None], "row", n_row, True, 0)
    scaled_block = jnp.transpose(gathered, (1, 0, 2)).reshape(width, block)
    current = None
    for iteration in range(ITERS):
        if current is not None:
            scaled_block = (current * pscale[None, :]).astype(jnp.bfloat16)
        picked = jnp.take(scaled_block.reshape(width, product_tiles, side), slot_ids[1], axis=1)
        products = jnp.einsum("rkj,kij->kri", picked, tile_set, preferred_element_type=jnp.float32)
        partial_sum = jnp.einsum("kq,kri->rqi", row_hot, products, precision=HIGH).reshape(
            width, n_col, qchunk
        )
        pieces = exchange(jnp.transpose(partial_sum, (1, 0, 2)), "col", n_col, False, 1)
        query_share = jnp.sum(pieces, axis=0)
        rounded = (query_share * my_qscale[None, :]).astype(jnp.bfloat16)
        query_pieces = exchange(rounded[None], "col", n_col, True, 2)
        query_block = jnp.transpose(query_pieces, (1, 0, 2)).reshape(width, query_tiles * side)
        backward_picked = jnp.take(
            query_block.reshape(width, query_tiles, side), slot_ids[0], axis=1
        )
        backward_products = jnp.einsum(
            "rki,kij->krj", backward_picked, tile_set, preferred_element_type=jnp.float32
        )
        product_partial = jnp.einsum(
            "kp,krj->rpj", col_hot, backward_products, precision=HIGH
        ).reshape(width, n_row, share)
        product_pieces = exchange(jnp.transpose(product_partial, (1, 0, 2)), "row", n_row, False, 3)
        lifted_share = jnp.sum(product_pieces, axis=0) * my_pscale[None, :]
        lifted_pieces = exchange(lifted_share[None], "row", n_row, True, 4)
        lifted = jnp.transpose(lifted_pieces, (1, 0, 2)).reshape(width, block)
        gram_part = jnp.einsum("ri,si->rs", lifted, lifted, precision=HIGH)
        gram = jnp.sum(exchange(gram_part[None], "col", n_col, True, 5), axis=0)
        current = orthonormal(lifted, gram)
    mine = lax.dynamic_slice_in_dim(current, row_at * share, share, axis=1)
    return mine * root_count


def solution(mesh):
    in_specs = (
        P("row", "col", None, None, None),
        P("row", "col", None, None),
        P("row", "col"),
        P("row"),
        P("col"),
        P(None, ("col", "row")),
    )
    out_specs = P(None, ("col", "row"))
    return jax.shard_map(shards, mesh=mesh, in_specs=in_specs, out_specs=out_specs, check_vma=False)
```

```python
import functools
import math

import jax
import jax.numpy as jnp
from jax import lax
from jax.experimental import pallas as pl
from jax.experimental.pallas import tpu as pltpu
from jax.sharding import PartitionSpec as P

ITERS = 2


HIGH = lax.Precision.HIGHEST

AXES = ("row", "col")


def _device(axis, peer):
    if axis == "row":
        return (peer, lax.axis_index("col"))
    return (lax.axis_index("row"), peer)


def _staged_kernel(*refs, axis, factors, mode, has_scale, epilogue):
    if has_scale:
        x_ref, s_ref, y_ref = refs[:3]
        rest = refs[3:]
    else:
        x_ref, y_ref = refs[:2]
        s_ref = None
        rest = refs[2:]
    stages = len(factors)
    n_rs = stages if mode in ("reduce", "sum") else 0
    rbufs = rest[:n_rs]
    gbuf = rest[n_rs] if mode != "sum" else None
    sems = rest[-1]
    me = lax.axis_index(axis)
    strides = [math.prod(factors[:s]) for s in range(stages)]
    mine = [lax.rem(lax.div(me, strides[s]), factors[s]) for s in range(stages)]

    def peer_of(s, d):
        return me + (d - mine[s]) * strides[s]

    def other(s, k):
        return lax.rem(mine[s] + k, factors[s])

    barrier = pltpu.get_barrier_semaphore()
    for s in range(stages):
        for k in range(1, factors[s]):
            pl.semaphore_signal(barrier, inc=1, device_id=_device(axis, peer_of(s, other(s, k))),
                                device_id_type=pl.DeviceIdType.MESH)
    pl.semaphore_wait(barrier, sum(f - 1 for f in factors))

    def exchange_stage(kind, s, src_of, dst_of):
        copies = []
        for k in range(1, factors[s]):
            d = other(s, k)
            c = pltpu.make_async_remote_copy(
                src_ref=src_of(d), dst_ref=dst_of(mine[s]),
                send_sem=sems.at[kind, s, d], recv_sem=sems.at[kind + 1, s, mine[s]],
                device_id=_device(axis, peer_of(s, d)), device_id_type=pl.DeviceIdType.MESH,
            )
            c.start()
            copies.append((d, c))
        for d, c in copies:
            c.wait_send()
            pltpu.make_async_remote_copy(
                src_ref=src_of(d), dst_ref=dst_of(d),
                send_sem=sems.at[kind, s, d], recv_sem=sems.at[kind + 1, s, d],
                device_id=_device(axis, peer_of(s, d)), device_id_type=pl.DeviceIdType.MESH,
            ).wait_recv()

    if mode == "sum":
        acc = x_ref
        for s in range(stages):
            rb = rbufs[s]
            rb[mine[s]] = acc[...]
            exchange_stage(0, s, lambda d: acc, lambda d, rb=rb: rb.at[d])
            total = rb[0]
            for d in range(1, factors[s]):
                total = total + rb[d]
            if s == stages - 1:
                y_ref[...] = total
            else:
                rbufs[s + 1][mine[s + 1]] = total
                acc = rbufs[s + 1].at[mine[s + 1]]
        return

    if mode == "reduce":
        cur = x_ref
        for s in range(stages):
            lead = stages - 1 - s

            def src_of(d, cur=cur, lead=lead):
                return cur.at[(slice(None),) * lead + (d,)]

            rb = rbufs[s]
            exchange_stage(0, s, src_of, lambda d, rb=rb: rb.at[d])
            total = cur[(slice(None),) * lead + (mine[s],)]
            for k in range(1, factors[s]):
                total = total + rb[other(s, k)]
            rb[mine[s]] = total
            cur = rb.at[mine[s]]
        own = epilogue(cur[...], s_ref)
    else:
        own = x_ref[...]
    gbuf[tuple(mine[::-1])] = own.astype(gbuf.dtype)
    for s in reversed(range(stages)):
        lead = stages - 1 - s

        def view(d, s=s, lead=lead):
            return gbuf.at[(slice(None),) * lead + (d,) + tuple(mine[s - 1::-1] if s else ())]

        exchange_stage(2, s, lambda d, s=s: view(mine[s]), view)
    y_ref[...] = gbuf[...]


def staged(x, axis, factors, mode, cid, scale=None, epilogue=None, out_dtype=None):
    n = math.prod(factors)
    stages = len(factors)
    out_dtype = out_dtype or x.dtype
    if mode == "reduce":
        chunk = x.shape[1:]
        x = x.reshape(tuple(reversed(factors)) + chunk)
    else:
        chunk = x.shape
    scratch = []
    if mode in ("reduce", "sum"):
        for s in range(stages):
            rest = tuple(reversed(factors[s + 1:])) if mode == "reduce" else ()
            scratch.append(pltpu.VMEM((factors[s],) + rest + chunk, jnp.float32))
    if mode != "sum":
        scratch.append(pltpu.VMEM(tuple(reversed(factors)) + chunk, out_dtype))
    scratch.append(pltpu.SemaphoreType.DMA((4, stages, max(factors))))
    if mode == "sum":
        out_shape = chunk
    else:
        out_shape = tuple(reversed(factors)) + chunk
    args = (x,) if scale is None else (x, scale)
    nbytes = n * math.prod(chunk) * 4
    y = pl.pallas_call(
        functools.partial(_staged_kernel, axis=axis, factors=tuple(factors), mode=mode,
                          has_scale=scale is not None, epilogue=epilogue),
        out_shape=jax.ShapeDtypeStruct(out_shape, out_dtype),
        in_specs=[pl.BlockSpec(memory_space=pltpu.VMEM)] * len(args),
        out_specs=pl.BlockSpec(memory_space=pltpu.VMEM),
        scratch_shapes=scratch,
        compiler_params=pltpu.CompilerParams(collective_id=cid, has_side_effects=True),
        cost_estimate=pl.CostEstimate(flops=0, transcendentals=0, bytes_accessed=2 * nbytes),
    )(*args)
    if mode == "sum":
        return y
    return y.reshape((n,) + chunk)


COL_FACTORS = (2, 4, 4)
ROW_FACTORS = (2, 4, 2)


def _query_epilogue(total, s_ref):
    return (total * s_ref[...]).astype(jnp.bfloat16)


def _product_epilogue(total, s_ref):
    return total * s_ref[...]


def orthonormal(lifted, gram):
    lower = jnp.linalg.cholesky(gram)
    return lax.linalg.triangular_solve(lower, lifted, left_side=True, lower=True)


def shards(tiles, tile_ids, tile_count, query_degree, product_degree, panel):
    tile_set = tiles[0, 0]
    slot_ids = tile_ids[0, 0]
    live_count = tile_count[0, 0]
    slots = tile_set.shape[0]
    side = tile_set.shape[1]
    width = panel.shape[0]
    query_tiles = query_degree.shape[0] // side
    product_tiles = product_degree.shape[0] // side
    n_row = lax.axis_size("row")
    n_col = lax.axis_size("col")
    live_slot = (jnp.arange(slots, dtype=jnp.int32) < live_count).astype(jnp.float32)
    row_hot = (slot_ids[0][:, None] == jnp.arange(query_tiles, dtype=jnp.int32)[None, :]).astype(
        jnp.float32
    ) * live_slot[:, None]
    col_hot = (slot_ids[1][:, None] == jnp.arange(product_tiles, dtype=jnp.int32)[None, :]).astype(
        jnp.float32
    ) * live_slot[:, None]
    qscale = 1.0 / jnp.sqrt(query_degree.astype(jnp.float32))
    pscale = 1.0 / jnp.sqrt(product_degree.astype(jnp.float32))
    row_at = lax.axis_index("row")
    col_at = lax.axis_index("col")
    share = panel.shape[1]
    block = pscale.shape[0]
    qchunk = query_degree.shape[0] // n_col
    my_pscale = lax.dynamic_slice_in_dim(pscale, row_at * share, share)
    my_qscale = lax.dynamic_slice_in_dim(qscale, col_at * qchunk, qchunk)
    root_count = math.sqrt(product_degree.shape[0] * n_col)

    scaled0 = (panel * my_pscale[None, :]).astype(jnp.bfloat16)
    gathered = staged(scaled0, "row", ROW_FACTORS, "gather", 0)
    scaled_block = jnp.transpose(gathered, (1, 0, 2)).reshape(width, block)
    current = None
    for iteration in range(ITERS):
        if current is not None:
            scaled_block = (current * pscale[None, :]).astype(jnp.bfloat16)
        picked = jnp.take(scaled_block.reshape(width, product_tiles, side), slot_ids[1], axis=1)
        products = jnp.einsum("rkj,kij->kri", picked, tile_set, preferred_element_type=jnp.float32)
        partial_sum = jnp.einsum("kq,kri->rqi", row_hot, products, precision=HIGH).reshape(
            width, n_col, qchunk
        )
        query_pieces = staged(jnp.transpose(partial_sum, (1, 0, 2)), "col", COL_FACTORS, "reduce", 1,
                              scale=my_qscale[None, :], epilogue=_query_epilogue,
                              out_dtype=jnp.bfloat16)
        query_block = jnp.transpose(query_pieces, (1, 0, 2)).reshape(width, query_tiles * side)
        backward_picked = jnp.take(
            query_block.reshape(width, query_tiles, side), slot_ids[0], axis=1
        )
        backward_products = jnp.einsum(
            "rki,kij->krj", backward_picked, tile_set, preferred_element_type=jnp.float32
        )
        product_partial = jnp.einsum(
            "kp,krj->rpj", col_hot, backward_products, precision=HIGH
        ).reshape(width, n_row, share)
        lifted_pieces = staged(jnp.transpose(product_partial, (1, 0, 2)), "row", ROW_FACTORS, "reduce",
                               2, scale=my_pscale[None, :], epilogue=_product_epilogue)
        lifted = jnp.transpose(lifted_pieces, (1, 0, 2)).reshape(width, block)
        gram_part = jnp.einsum("ri,si->rs", lifted, lifted, precision=HIGH)
        gram = staged(gram_part, "col", COL_FACTORS, "sum", 3)
        current = orthonormal(lifted, gram)
    mine = lax.dynamic_slice_in_dim(current, row_at * share, share, axis=1)
    return mine * root_count


def solution(mesh):
    in_specs = (
        P("row", "col", None, None, None),
        P("row", "col", None, None),
        P("row", "col"),
        P("row"),
        P("col"),
        P(None, ("col", "row")),
    )
    out_specs = P(None, ("col", "row"))
    return jax.shard_map(shards, mesh=mesh, in_specs=in_specs, out_specs=out_specs, check_vma=False)
```

```python
import functools
import math

import jax
import jax.numpy as jnp
from jax import lax
from jax.experimental import pallas as pl
from jax.experimental.pallas import tpu as pltpu
from jax.sharding import PartitionSpec as P

ITERS = 2


HIGH = lax.Precision.HIGHEST

AXES = ("row", "col")


def _device(axis, peer):
    if axis == "row":
        return (peer, lax.axis_index("col"))
    return (lax.axis_index("row"), peer)


def _staged_kernel(*refs, axis, factors, mode, has_scale, epilogue):
    if has_scale:
        x_ref, s_ref, y_ref = refs[:3]
        rest = refs[3:]
    else:
        x_ref, y_ref = refs[:2]
        s_ref = None
        rest = refs[2:]
    stages = len(factors)
    n_rs = stages if mode in ("reduce", "sum") else 0
    rbufs = rest[:n_rs]
    gbuf = rest[n_rs] if mode != "sum" else None
    sems = rest[-1]
    me = lax.axis_index(axis)
    strides = [math.prod(factors[:s]) for s in range(stages)]
    mine = [lax.rem(lax.div(me, strides[s]), factors[s]) for s in range(stages)]

    def peer_of(s, d):
        return me + (d - mine[s]) * strides[s]

    def other(s, k):
        return lax.rem(mine[s] + k, factors[s])

    barrier = pltpu.get_barrier_semaphore()
    for s in range(stages):
        for k in range(1, factors[s]):
            pl.semaphore_signal(barrier, inc=1, device_id=_device(axis, peer_of(s, other(s, k))),
                                device_id_type=pl.DeviceIdType.MESH)
    pl.semaphore_wait(barrier, sum(f - 1 for f in factors))

    def exchange_stage(kind, s, src_of, dst_of):
        copies = []
        for k in range(1, factors[s]):
            d = other(s, k)
            c = pltpu.make_async_remote_copy(
                src_ref=src_of(d), dst_ref=dst_of(mine[s]),
                send_sem=sems.at[kind, s, d], recv_sem=sems.at[kind + 1, s, mine[s]],
                device_id=_device(axis, peer_of(s, d)), device_id_type=pl.DeviceIdType.MESH,
            )
            c.start()
            copies.append((d, c))
        for d, c in copies:
            c.wait_send()
            pltpu.make_async_remote_copy(
                src_ref=src_of(d), dst_ref=dst_of(d),
                send_sem=sems.at[kind, s, d], recv_sem=sems.at[kind + 1, s, d],
                device_id=_device(axis, peer_of(s, d)), device_id_type=pl.DeviceIdType.MESH,
            ).wait_recv()

    if mode == "sum":
        acc = x_ref
        for s in range(stages):
            rb = rbufs[s]
            rb[mine[s]] = acc[...]
            exchange_stage(0, s, lambda d: acc, lambda d, rb=rb: rb.at[d])
            total = rb[0]
            for d in range(1, factors[s]):
                total = total + rb[d]
            if s == stages - 1:
                y_ref[...] = total
            else:
                rbufs[s + 1][mine[s + 1]] = total
                acc = rbufs[s + 1].at[mine[s + 1]]
        return

    if mode == "reduce":
        cur = x_ref
        for s in range(stages):
            lead = stages - 1 - s

            def src_of(d, cur=cur, lead=lead):
                return cur.at[(slice(None),) * lead + (d,)]

            rb = rbufs[s]
            exchange_stage(0, s, src_of, lambda d, rb=rb: rb.at[d])
            total = cur[(slice(None),) * lead + (mine[s],)]
            for k in range(1, factors[s]):
                total = total + rb[other(s, k)]
            rb[mine[s]] = total
            cur = rb.at[mine[s]]
        own = epilogue(cur[...], s_ref)
    else:
        own = x_ref[...]
    gbuf[tuple(mine[::-1])] = own.astype(gbuf.dtype)
    for s in reversed(range(stages)):
        lead = stages - 1 - s

        def view(d, s=s, lead=lead):
            return gbuf.at[(slice(None),) * lead + (d,) + tuple(mine[s - 1::-1] if s else ())]

        exchange_stage(2, s, lambda d, s=s: view(mine[s]), view)
    y_ref[...] = gbuf[...]


def staged(x, axis, factors, mode, cid, scale=None, epilogue=None, out_dtype=None):
    n = math.prod(factors)
    stages = len(factors)
    out_dtype = out_dtype or x.dtype
    if mode == "reduce":
        chunk = x.shape[1:]
        x = x.reshape(tuple(reversed(factors)) + chunk)
    else:
        chunk = x.shape
    scratch = []
    if mode in ("reduce", "sum"):
        for s in range(stages):
            rest = tuple(reversed(factors[s + 1:])) if mode == "reduce" else ()
            scratch.append(pltpu.VMEM((factors[s],) + rest + chunk, jnp.float32))
    if mode != "sum":
        scratch.append(pltpu.VMEM(tuple(reversed(factors)) + chunk, out_dtype))
    scratch.append(pltpu.SemaphoreType.DMA((4, stages, max(factors))))
    if mode == "sum":
        out_shape = chunk
    else:
        out_shape = tuple(reversed(factors)) + chunk
    args = (x,) if scale is None else (x, scale)
    nbytes = n * math.prod(chunk) * 4
    y = pl.pallas_call(
        functools.partial(_staged_kernel, axis=axis, factors=tuple(factors), mode=mode,
                          has_scale=scale is not None, epilogue=epilogue),
        out_shape=jax.ShapeDtypeStruct(out_shape, out_dtype),
        in_specs=[pl.BlockSpec(memory_space=pltpu.VMEM)] * len(args),
        out_specs=pl.BlockSpec(memory_space=pltpu.VMEM),
        scratch_shapes=scratch,
        compiler_params=pltpu.CompilerParams(collective_id=cid, has_side_effects=True),
        cost_estimate=pl.CostEstimate(flops=0, transcendentals=0, bytes_accessed=2 * nbytes),
    )(*args)
    if mode == "sum":
        return y
    return y.reshape((n,) + chunk)


QUERY_FACTORS = (2, 4, 4)
GRAM_FACTORS = (4, 8)
ROW_FACTORS = (4, 4)


def _query_epilogue(total, s_ref):
    return (total * s_ref[...]).astype(jnp.bfloat16)


def _product_epilogue(total, s_ref):
    return total * s_ref[...]


def orthonormal(lifted, gram):
    lower = jnp.linalg.cholesky(gram)
    return lax.linalg.triangular_solve(lower, lifted, left_side=True, lower=True)


def shards(tiles, tile_ids, tile_count, query_degree, product_degree, panel):
    tile_set = tiles[0, 0]
    slot_ids = tile_ids[0, 0]
    live_count = tile_count[0, 0]
    slots = tile_set.shape[0]
    side = tile_set.shape[1]
    width = panel.shape[0]
    query_tiles = query_degree.shape[0] // side
    product_tiles = product_degree.shape[0] // side
    n_row = lax.axis_size("row")
    n_col = lax.axis_size("col")
    live_slot = (jnp.arange(slots, dtype=jnp.int32) < live_count).astype(jnp.float32)
    row_hot = (slot_ids[0][:, None] == jnp.arange(query_tiles, dtype=jnp.int32)[None, :]).astype(
        jnp.float32
    ) * live_slot[:, None]
    col_hot = (slot_ids[1][:, None] == jnp.arange(product_tiles, dtype=jnp.int32)[None, :]).astype(
        jnp.float32
    ) * live_slot[:, None]
    qscale = 1.0 / jnp.sqrt(query_degree.astype(jnp.float32))
    pscale = 1.0 / jnp.sqrt(product_degree.astype(jnp.float32))
    row_at = lax.axis_index("row")
    col_at = lax.axis_index("col")
    share = panel.shape[1]
    block = pscale.shape[0]
    qchunk = query_degree.shape[0] // n_col
    my_pscale = lax.dynamic_slice_in_dim(pscale, row_at * share, share)
    my_qscale = lax.dynamic_slice_in_dim(qscale, col_at * qchunk, qchunk)
    dense_qscale = jnp.concatenate([my_qscale, my_qscale])[None, :]
    root_count = math.sqrt(product_degree.shape[0] * n_col)

    scaled0 = (panel * my_pscale[None, :]).astype(jnp.bfloat16)
    gathered = staged(scaled0, "row", ROW_FACTORS, "gather", 0)
    scaled_block = jnp.transpose(gathered, (1, 0, 2)).reshape(width, block)
    current = None
    for iteration in range(ITERS):
        if current is not None:
            scaled_block = (current * pscale[None, :]).astype(jnp.bfloat16)
        picked = jnp.take(scaled_block.reshape(width, product_tiles, side), slot_ids[1], axis=1)
        products = jnp.einsum("rkj,kij->kri", picked, tile_set, preferred_element_type=jnp.float32)
        partial_sum = jnp.einsum("kq,kri->rqi", row_hot, products, precision=HIGH).reshape(
            width, n_col, qchunk
        )
        dense = jnp.transpose(partial_sum, (1, 0, 2)).reshape(n_col, width // 2, 2 * qchunk)
        query_pieces = staged(dense, "col", QUERY_FACTORS, "reduce", 1,
                              scale=dense_qscale, epilogue=_query_epilogue,
                              out_dtype=jnp.bfloat16).reshape(n_col, width, qchunk)
        query_block = jnp.transpose(query_pieces, (1, 0, 2)).reshape(width, query_tiles * side)
        backward_picked = jnp.take(
            query_block.reshape(width, query_tiles, side), slot_ids[0], axis=1
        )
        backward_products = jnp.einsum(
            "rki,kij->krj", backward_picked, tile_set, preferred_element_type=jnp.float32
        )
        product_partial = jnp.einsum(
            "kp,krj->rpj", col_hot, backward_products, precision=HIGH
        ).reshape(width, n_row, share)
        lifted_pieces = staged(jnp.transpose(product_partial, (1, 0, 2)), "row", ROW_FACTORS, "reduce",
                               2, scale=my_pscale[None, :], epilogue=_product_epilogue)
        lifted = jnp.transpose(lifted_pieces, (1, 0, 2)).reshape(width, block)
        gram_part = jnp.einsum("ri,si->rs", lifted, lifted, precision=HIGH)
        gram = staged(gram_part, "col", GRAM_FACTORS, "sum", 3)
        current = orthonormal(lifted, gram)
    mine = lax.dynamic_slice_in_dim(current, row_at * share, share, axis=1)
    return mine * root_count


def solution(mesh):
    in_specs = (
        P("row", "col", None, None, None),
        P("row", "col", None, None),
        P("row", "col"),
        P("row"),
        P("col"),
        P(None, ("col", "row")),
    )
    out_specs = P(None, ("col", "row"))
    return jax.shard_map(shards, mesh=mesh, in_specs=in_specs, out_specs=out_specs, check_vma=False)
```

```python
import functools
import math

import jax
import jax.numpy as jnp
from jax import lax
from jax.experimental import pallas as pl
from jax.experimental.pallas import tpu as pltpu
from jax.sharding import PartitionSpec as P

ITERS = 2


HIGH = lax.Precision.HIGHEST

AXES = ("row", "col")


def _device(axis, peer):
    if axis == "row":
        return (peer, lax.axis_index("col"))
    return (lax.axis_index("row"), peer)


def _staged_kernel(*refs, axis, factors, mode, has_scale, epilogue):
    if has_scale:
        x_ref, s_ref, y_ref = refs[:3]
        rest = refs[3:]
    else:
        x_ref, y_ref = refs[:2]
        s_ref = None
        rest = refs[2:]
    stages = len(factors)
    n_rs = stages if mode in ("reduce", "sum") else 0
    rbufs = rest[:n_rs]
    gbuf = rest[n_rs] if mode != "sum" else None
    sems = rest[-1]
    me = lax.axis_index(axis)
    strides = [math.prod(factors[:s]) for s in range(stages)]
    mine = [lax.rem(lax.div(me, strides[s]), factors[s]) for s in range(stages)]

    def peer_of(s, d):
        return me + (d - mine[s]) * strides[s]

    def other(s, k):
        return lax.rem(mine[s] + k, factors[s])

    barrier = pltpu.get_barrier_semaphore()
    for s in range(stages):
        for k in range(1, factors[s]):
            pl.semaphore_signal(barrier, inc=1, device_id=_device(axis, peer_of(s, other(s, k))),
                                device_id_type=pl.DeviceIdType.MESH)
    pl.semaphore_wait(barrier, sum(f - 1 for f in factors))

    def exchange_stage(kind, s, src_of, dst_of):
        copies = []
        for k in range(1, factors[s]):
            d = other(s, k)
            c = pltpu.make_async_remote_copy(
                src_ref=src_of(d), dst_ref=dst_of(mine[s]),
                send_sem=sems.at[kind, s, d], recv_sem=sems.at[kind + 1, s, mine[s]],
                device_id=_device(axis, peer_of(s, d)), device_id_type=pl.DeviceIdType.MESH,
            )
            c.start()
            copies.append((d, c))
        for d, c in copies:
            c.wait_send()
            pltpu.make_async_remote_copy(
                src_ref=src_of(d), dst_ref=dst_of(d),
                send_sem=sems.at[kind, s, d], recv_sem=sems.at[kind + 1, s, d],
                device_id=_device(axis, peer_of(s, d)), device_id_type=pl.DeviceIdType.MESH,
            ).wait_recv()

    if mode == "sum":
        acc = x_ref
        for s in range(stages):
            rb = rbufs[s]
            rb[mine[s]] = acc[...]
            exchange_stage(0, s, lambda d: acc, lambda d, rb=rb: rb.at[d])
            total = rb[0]
            for d in range(1, factors[s]):
                total = total + rb[d]
            if s == stages - 1:
                y_ref[...] = total
            else:
                rbufs[s + 1][mine[s + 1]] = total
                acc = rbufs[s + 1].at[mine[s + 1]]
        return

    if mode == "reduce":
        cur = x_ref
        for s in range(stages):
            lead = stages - 1 - s

            def src_of(d, cur=cur, lead=lead):
                return cur.at[(slice(None),) * lead + (d,)]

            rb = rbufs[s]
            exchange_stage(0, s, src_of, lambda d, rb=rb: rb.at[d])
            total = cur[(slice(None),) * lead + (mine[s],)]
            for k in range(1, factors[s]):
                total = total + rb[other(s, k)]
            rb[mine[s]] = total
            cur = rb.at[mine[s]]
        own = epilogue(cur[...], s_ref)
    else:
        own = x_ref[...]
    gbuf[tuple(mine[::-1])] = own.astype(gbuf.dtype)
    for s in reversed(range(stages)):
        lead = stages - 1 - s

        def view(d, s=s, lead=lead):
            return gbuf.at[(slice(None),) * lead + (d,) + tuple(mine[s - 1::-1] if s else ())]

        exchange_stage(2, s, lambda d, s=s: view(mine[s]), view)
    y_ref[...] = gbuf[...]


def staged(x, axis, factors, mode, cid, scale=None, epilogue=None, out_dtype=None):
    n = math.prod(factors)
    stages = len(factors)
    out_dtype = out_dtype or x.dtype
    if mode == "reduce":
        chunk = x.shape[1:]
        x = x.reshape(tuple(reversed(factors)) + chunk)
    else:
        chunk = x.shape
    scratch = []
    if mode in ("reduce", "sum"):
        for s in range(stages):
            rest = tuple(reversed(factors[s + 1:])) if mode == "reduce" else ()
            scratch.append(pltpu.VMEM((factors[s],) + rest + chunk, jnp.float32))
    if mode != "sum":
        scratch.append(pltpu.VMEM(tuple(reversed(factors)) + chunk, out_dtype))
    scratch.append(pltpu.SemaphoreType.DMA((4, stages, max(factors))))
    if mode == "sum":
        out_shape = chunk
    else:
        out_shape = tuple(reversed(factors)) + chunk
    args = (x,) if scale is None else (x, scale)
    nbytes = n * math.prod(chunk) * 4
    y = pl.pallas_call(
        functools.partial(_staged_kernel, axis=axis, factors=tuple(factors), mode=mode,
                          has_scale=scale is not None, epilogue=epilogue),
        out_shape=jax.ShapeDtypeStruct(out_shape, out_dtype),
        in_specs=[pl.BlockSpec(memory_space=pltpu.VMEM)] * len(args),
        out_specs=pl.BlockSpec(memory_space=pltpu.VMEM),
        scratch_shapes=scratch,
        compiler_params=pltpu.CompilerParams(collective_id=cid, has_side_effects=True),
        cost_estimate=pl.CostEstimate(flops=0, transcendentals=0, bytes_accessed=2 * nbytes),
    )(*args)
    if mode == "sum":
        return y
    return y.reshape((n,) + chunk)


QUERY_FACTORS = (2, 4, 4)
GRAM_FACTORS = (4, 8)
ROW_FACTORS = (4, 4)


def _query_epilogue(total, s_ref):
    return (total * s_ref[...]).astype(jnp.bfloat16)


def _product_epilogue(total, s_ref):
    return total * s_ref[...]


def _products_kernel(ids_ref, count_ref, src_ref, tiles_ref, out_ref, *, forward):
    out_ref[...] = jnp.zeros_like(out_ref)
    src_row, dst_row = (1, 0) if forward else (0, 1)

    def body(k, carry):
        @pl.when(k < count_ref[0])
        def _():
            x = src_ref[ids_ref[src_row, k]]
            t = tiles_ref[k]
            if forward:
                y = lax.dot_general(x, t, (((1,), (1,)), ((), ())),
                                    preferred_element_type=jnp.float32)
            else:
                y = jnp.dot(x, t, preferred_element_type=jnp.float32)
            d = ids_ref[dst_row, k]
            out_ref[d] = out_ref[d] + y

        return carry

    lax.fori_loop(0, tiles_ref.shape[0], body, 0)


def tile_products(slot_ids, live_count, src, tile_set, blocks, forward):
    slots, side, _ = tile_set.shape
    width = src.shape[1]
    return pl.pallas_call(
        functools.partial(_products_kernel, forward=forward),
        out_shape=jax.ShapeDtypeStruct((blocks, width, side), jnp.float32),
        in_specs=[
            pl.BlockSpec(memory_space=pltpu.SMEM),
            pl.BlockSpec(memory_space=pltpu.SMEM),
            pl.BlockSpec(memory_space=pltpu.VMEM),
            pl.BlockSpec(memory_space=pltpu.VMEM),
        ],
        out_specs=pl.BlockSpec(memory_space=pltpu.VMEM),
        cost_estimate=pl.CostEstimate(
            flops=2 * slots * width * side * side, transcendentals=0,
            bytes_accessed=slots * side * side * 2 + src.size * 2 + blocks * width * side * 4,
        ),
    )(slot_ids, live_count.reshape(1), src, tile_set)


def orthonormal(lifted, gram):
    lower = jnp.linalg.cholesky(gram)
    return lax.linalg.triangular_solve(lower, lifted, left_side=True, lower=True)


def shards(tiles, tile_ids, tile_count, query_degree, product_degree, panel):
    tile_set = tiles[0, 0]
    slot_ids = tile_ids[0, 0]
    live_count = tile_count[0, 0]
    side = tile_set.shape[1]
    width = panel.shape[0]
    query_tiles = query_degree.shape[0] // side
    product_tiles = product_degree.shape[0] // side
    n_row = lax.axis_size("row")
    n_col = lax.axis_size("col")
    qscale = (1.0 / jnp.sqrt(query_degree.astype(jnp.float32))).reshape(query_tiles, 1, side)
    pscale = (1.0 / jnp.sqrt(product_degree.astype(jnp.float32))).reshape(product_tiles, 1, side)
    row_at = lax.axis_index("row")
    col_at = lax.axis_index("col")
    share = panel.shape[1]
    block = product_degree.shape[0]
    q_per_tile = n_col // query_tiles
    p_per_tile = n_row // product_tiles
    my_qscale = lax.dynamic_index_in_dim(qscale, col_at // q_per_tile, keepdims=False)
    my_pscale = lax.dynamic_index_in_dim(pscale, row_at // p_per_tile, keepdims=False)
    root_count = math.sqrt(product_degree.shape[0] * n_col)

    panel_pscale = lax.dynamic_slice_in_dim(pscale.reshape(block), row_at * share, share)
    scaled0 = (panel * panel_pscale[None, :]).astype(jnp.bfloat16)
    gathered = staged(scaled0, "row", ROW_FACTORS, "gather", 0)
    per_tile = side // share
    scaled_tiles = jnp.transpose(
        gathered.reshape(product_tiles, per_tile, width, share), (0, 2, 1, 3)
    ).reshape(product_tiles, width, side)
    current = None
    for iteration in range(ITERS):
        if current is not None:
            scaled_tiles = (
                jnp.transpose(current.reshape(width, product_tiles, side), (1, 0, 2)) * pscale
            ).astype(jnp.bfloat16)
        partial_sum = tile_products(slot_ids, live_count, scaled_tiles, tile_set, query_tiles, True)
        query_tiles_panel = staged(
            partial_sum.reshape(n_col, width // q_per_tile, side), "col", QUERY_FACTORS, "reduce", 1,
            scale=my_qscale, epilogue=_query_epilogue, out_dtype=jnp.bfloat16,
        ).reshape(query_tiles, width, side)
        product_partial = tile_products(
            slot_ids, live_count, query_tiles_panel, tile_set, product_tiles, False
        )
        lifted_tiles = staged(
            product_partial.reshape(n_row, width // p_per_tile, side), "row", ROW_FACTORS, "reduce", 2,
            scale=my_pscale, epilogue=_product_epilogue,
        ).reshape(product_tiles, width, side)
        gram_part = jnp.einsum("pri,psi->rs", lifted_tiles, lifted_tiles, precision=HIGH)
        gram = staged(gram_part, "col", GRAM_FACTORS, "sum", 3)
        lifted = jnp.transpose(lifted_tiles, (1, 0, 2)).reshape(width, block)
        current = orthonormal(lifted, gram)
    mine = lax.dynamic_slice_in_dim(current, row_at * share, share, axis=1)
    return mine * root_count


def solution(mesh):
    in_specs = (
        P("row", "col", None, None, None),
        P("row", "col", None, None),
        P("row", "col"),
        P("row"),
        P("col"),
        P(None, ("col", "row")),
    )
    out_specs = P(None, ("col", "row"))
    return jax.shard_map(shards, mesh=mesh, in_specs=in_specs, out_specs=out_specs, check_vma=False)
```

```python
import functools
import math

import jax
import jax.numpy as jnp
from jax import lax
from jax.experimental import pallas as pl
from jax.experimental.pallas import tpu as pltpu
from jax.sharding import PartitionSpec as P

ITERS = 2


HIGH = lax.Precision.HIGHEST

AXES = ("row", "col")


def _device(axis, peer):
    if axis == "row":
        return (peer, lax.axis_index("col"))
    return (lax.axis_index("row"), peer)


def _staged_kernel(*refs, axis, factors, mode, has_scale, epilogue):
    if has_scale:
        x_ref, s_ref, y_ref = refs[:3]
        rest = refs[3:]
    else:
        x_ref, y_ref = refs[:2]
        s_ref = None
        rest = refs[2:]
    stages = len(factors)
    n_rs = stages if mode in ("reduce", "sum") else 0
    rbufs = rest[:n_rs]
    gbuf = rest[n_rs] if mode != "sum" else None
    sems = rest[-1]
    me = lax.axis_index(axis)
    strides = [math.prod(factors[:s]) for s in range(stages)]
    mine = [lax.rem(lax.div(me, strides[s]), factors[s]) for s in range(stages)]

    def peer_of(s, d):
        return me + (d - mine[s]) * strides[s]

    def other(s, k):
        return lax.rem(mine[s] + k, factors[s])

    def exchange_stage(kind, s, src_of, dst_of):
        copies = []
        for k in range(1, factors[s]):
            d = other(s, k)
            c = pltpu.make_async_remote_copy(
                src_ref=src_of(d), dst_ref=dst_of(mine[s]),
                send_sem=sems.at[kind, s, d], recv_sem=sems.at[kind + 1, s, mine[s]],
                device_id=_device(axis, peer_of(s, d)), device_id_type=pl.DeviceIdType.MESH,
            )
            c.start()
            copies.append((d, c))
        for d, c in copies:
            c.wait_send()
            pltpu.make_async_remote_copy(
                src_ref=src_of(d), dst_ref=dst_of(d),
                send_sem=sems.at[kind, s, d], recv_sem=sems.at[kind + 1, s, d],
                device_id=_device(axis, peer_of(s, d)), device_id_type=pl.DeviceIdType.MESH,
            ).wait_recv()

    if mode == "sum":
        acc = x_ref
        for s in range(stages):
            rb = rbufs[s]
            rb[mine[s]] = acc[...]
            exchange_stage(0, s, lambda d: acc, lambda d, rb=rb: rb.at[d])
            total = rb[0]
            for d in range(1, factors[s]):
                total = total + rb[d]
            if s == stages - 1:
                y_ref[...] = total
            else:
                rbufs[s + 1][mine[s + 1]] = total
                acc = rbufs[s + 1].at[mine[s + 1]]
        return

    if mode == "reduce":
        cur = x_ref
        for s in range(stages):
            lead = stages - 1 - s

            def src_of(d, cur=cur, lead=lead):
                return cur.at[(slice(None),) * lead + (d,)]

            rb = rbufs[s]
            exchange_stage(0, s, src_of, lambda d, rb=rb: rb.at[d])
            total = cur[(slice(None),) * lead + (mine[s],)]
            for k in range(1, factors[s]):
                total = total + rb[other(s, k)]
            rb[mine[s]] = total
            cur = rb.at[mine[s]]
        own = epilogue(cur[...], s_ref)
    else:
        own = x_ref[...]
    gbuf[tuple(mine[::-1])] = own.astype(gbuf.dtype)
    for s in reversed(range(stages)):
        lead = stages - 1 - s

        def view(d, s=s, lead=lead):
            return gbuf.at[(slice(None),) * lead + (d,) + tuple(mine[s - 1::-1] if s else ())]

        exchange_stage(2, s, lambda d, s=s: view(mine[s]), view)
    y_ref[...] = gbuf[...]


def staged(x, axis, factors, mode, cid, scale=None, epilogue=None, out_dtype=None):
    n = math.prod(factors)
    stages = len(factors)
    out_dtype = out_dtype or x.dtype
    if mode == "reduce":
        chunk = x.shape[1:]
        x = x.reshape(tuple(reversed(factors)) + chunk)
    else:
        chunk = x.shape
    scratch = []
    if mode in ("reduce", "sum"):
        for s in range(stages):
            rest = tuple(reversed(factors[s + 1:])) if mode == "reduce" else ()
            scratch.append(pltpu.VMEM((factors[s],) + rest + chunk, jnp.float32))
    if mode != "sum":
        scratch.append(pltpu.VMEM(tuple(reversed(factors)) + chunk, out_dtype))
    scratch.append(pltpu.SemaphoreType.DMA((4, stages, max(factors))))
    if mode == "sum":
        out_shape = chunk
    else:
        out_shape = tuple(reversed(factors)) + chunk
    args = (x,) if scale is None else (x, scale)
    nbytes = n * math.prod(chunk) * 4
    y = pl.pallas_call(
        functools.partial(_staged_kernel, axis=axis, factors=tuple(factors), mode=mode,
                          has_scale=scale is not None, epilogue=epilogue),
        out_shape=jax.ShapeDtypeStruct(out_shape, out_dtype),
        in_specs=[pl.BlockSpec(memory_space=pltpu.VMEM)] * len(args),
        out_specs=pl.BlockSpec(memory_space=pltpu.VMEM),
        scratch_shapes=scratch,
        compiler_params=pltpu.CompilerParams(has_side_effects=True),
        cost_estimate=pl.CostEstimate(flops=0, transcendentals=0, bytes_accessed=2 * nbytes),
    )(*args)
    if mode == "sum":
        return y
    return y.reshape((n,) + chunk)


QUERY_FACTORS = (2, 4, 4)
GRAM_FACTORS = (4, 8)
ROW_FACTORS = (4, 4)


def _query_epilogue(total, s_ref):
    return (total * s_ref[...]).astype(jnp.bfloat16)


def _product_epilogue(total, s_ref):
    return total * s_ref[...]


GROUP = 4


def _products_kernel(ids_ref, count_ref, src_ref, tiles_hbm, out_ref, tiles, sems, *, forward):
    slots = tiles.shape[0]
    groups = slots // GROUP

    def fetch(g):
        return pltpu.make_async_copy(
            tiles_hbm.at[pl.ds(g * GROUP, GROUP)], tiles.at[pl.ds(g * GROUP, GROUP)], sems.at[g]
        )

    for g in range(groups):
        fetch(g).start()
    out_ref[...] = jnp.zeros_like(out_ref)
    src_row, dst_row = (1, 0) if forward else (0, 1)

    def body(k, carry):
        @pl.when(k < count_ref[0])
        def _():
            x = src_ref[ids_ref[src_row, k]]
            t = tiles[k]
            if forward:
                y = lax.dot_general(x, t, (((1,), (1,)), ((), ())),
                                    preferred_element_type=jnp.float32)
            else:
                y = jnp.dot(x, t, preferred_element_type=jnp.float32)
            d = ids_ref[dst_row, k]
            out_ref[d] = out_ref[d] + y

        return carry

    for g in range(groups):
        fetch(g).wait()
        lax.fori_loop(g * GROUP, (g + 1) * GROUP, body, 0)


def tile_products(slot_ids, live_count, src, tile_set, blocks, forward):
    slots, side, _ = tile_set.shape
    width = src.shape[1]
    return pl.pallas_call(
        functools.partial(_products_kernel, forward=forward),
        out_shape=jax.ShapeDtypeStruct((blocks, width, side), jnp.float32),
        in_specs=[
            pl.BlockSpec(memory_space=pltpu.SMEM),
            pl.BlockSpec(memory_space=pltpu.SMEM),
            pl.BlockSpec(memory_space=pltpu.VMEM),
            pl.BlockSpec(memory_space=pl.ANY),
        ],
        out_specs=pl.BlockSpec(memory_space=pltpu.VMEM),
        scratch_shapes=[
            pltpu.VMEM(tile_set.shape, tile_set.dtype),
            pltpu.SemaphoreType.DMA((slots // GROUP,)),
        ],
        cost_estimate=pl.CostEstimate(
            flops=2 * slots * width * side * side, transcendentals=0,
            bytes_accessed=slots * side * side * 2 + src.size * 2 + blocks * width * side * 4,
        ),
    )(slot_ids, live_count.reshape(1), src, tile_set)


def orthonormal(lifted, gram):
    lower = jnp.linalg.cholesky(gram)
    return lax.linalg.triangular_solve(lower, lifted, left_side=True, lower=True)


def shards(tiles, tile_ids, tile_count, query_degree, product_degree, panel):
    tile_set = tiles[0, 0]
    slot_ids = tile_ids[0, 0]
    live_count = tile_count[0, 0]
    side = tile_set.shape[1]
    width = panel.shape[0]
    query_tiles = query_degree.shape[0] // side
    product_tiles = product_degree.shape[0] // side
    n_row = lax.axis_size("row")
    n_col = lax.axis_size("col")
    qscale = (1.0 / jnp.sqrt(query_degree.astype(jnp.float32))).reshape(query_tiles, 1, side)
    pscale = (1.0 / jnp.sqrt(product_degree.astype(jnp.float32))).reshape(product_tiles, 1, side)
    row_at = lax.axis_index("row")
    col_at = lax.axis_index("col")
    share = panel.shape[1]
    block = product_degree.shape[0]
    q_per_tile = n_col // query_tiles
    p_per_tile = n_row // product_tiles
    my_qscale = lax.dynamic_index_in_dim(qscale, col_at // q_per_tile, keepdims=False)
    my_pscale = lax.dynamic_index_in_dim(pscale, row_at // p_per_tile, keepdims=False)
    root_count = math.sqrt(product_degree.shape[0] * n_col)

    panel_pscale = lax.dynamic_slice_in_dim(pscale.reshape(block), row_at * share, share)
    scaled0 = (panel * panel_pscale[None, :]).astype(jnp.bfloat16)
    gathered = staged(scaled0, "row", ROW_FACTORS, "gather", 0)
    per_tile = side // share
    scaled_tiles = jnp.transpose(
        gathered.reshape(product_tiles, per_tile, width, share), (0, 2, 1, 3)
    ).reshape(product_tiles, width, side)
    current = None
    for iteration in range(ITERS):
        if current is not None:
            scaled_tiles = (
                jnp.transpose(current.reshape(width, product_tiles, side), (1, 0, 2)) * pscale
            ).astype(jnp.bfloat16)
        partial_sum = tile_products(slot_ids, live_count, scaled_tiles, tile_set, query_tiles, True)
        query_tiles_panel = staged(
            partial_sum.reshape(n_col, width // q_per_tile, side), "col", QUERY_FACTORS, "reduce", 1,
            scale=my_qscale, epilogue=_query_epilogue, out_dtype=jnp.bfloat16,
        ).reshape(query_tiles, width, side)
        product_partial = tile_products(
            slot_ids, live_count, query_tiles_panel, tile_set, product_tiles, False
        )
        lifted_tiles = staged(
            product_partial.reshape(n_row, width // p_per_tile, side), "row", ROW_FACTORS, "reduce", 2,
            scale=my_pscale, epilogue=_product_epilogue,
        ).reshape(product_tiles, width, side)
        gram_part = jnp.einsum("pri,psi->rs", lifted_tiles, lifted_tiles, precision=HIGH)
        gram = staged(gram_part, "col", GRAM_FACTORS, "sum", 3)
        lifted = jnp.transpose(lifted_tiles, (1, 0, 2)).reshape(width, block)
        current = orthonormal(lifted, gram)
    mine = lax.dynamic_slice_in_dim(current, row_at * share, share, axis=1)
    return mine * root_count


def solution(mesh):
    in_specs = (
        P("row", "col", None, None, None),
        P("row", "col", None, None),
        P("row", "col"),
        P("row"),
        P("col"),
        P(None, ("col", "row")),
    )
    out_specs = P(None, ("col", "row"))
    return jax.shard_map(shards, mesh=mesh, in_specs=in_specs, out_specs=out_specs, check_vma=False)
```

```python
import functools
import math

import jax
import jax.numpy as jnp
from jax import lax
from jax.experimental import pallas as pl
from jax.experimental.pallas import tpu as pltpu
from jax.sharding import PartitionSpec as P

ITERS = 2


HIGH = lax.Precision.HIGHEST

AXES = ("row", "col")


def _device(axis, peer):
    if axis == "row":
        return (peer, lax.axis_index("col"))
    return (lax.axis_index("row"), peer)


def _staged_kernel(*refs, axis, factors, mode, has_scale, epilogue):
    if has_scale:
        x_ref, s_ref, y_ref = refs[:3]
        rest = refs[3:]
    else:
        x_ref, y_ref = refs[:2]
        s_ref = None
        rest = refs[2:]
    stages = len(factors)
    n_rs = stages if mode in ("reduce", "sum") else 0
    rbufs = rest[:n_rs]
    gbuf = rest[n_rs] if mode != "sum" else None
    sems = rest[-1]
    me = lax.axis_index(axis)
    strides = [math.prod(factors[:s]) for s in range(stages)]
    mine = [lax.rem(lax.div(me, strides[s]), factors[s]) for s in range(stages)]

    def peer_of(s, d):
        return me + (d - mine[s]) * strides[s]

    def other(s, k):
        return lax.rem(mine[s] + k, factors[s])

    barrier = pltpu.get_barrier_semaphore()
    for s in range(stages):
        for k in range(1, factors[s]):
            pl.semaphore_signal(barrier, inc=1, device_id=_device(axis, peer_of(s, other(s, k))),
                                device_id_type=pl.DeviceIdType.MESH)
    pl.semaphore_wait(barrier, sum(f - 1 for f in factors))

    def exchange_stage(kind, s, src_of, dst_of):
        copies = []
        for k in range(1, factors[s]):
            d = other(s, k)
            c = pltpu.make_async_remote_copy(
                src_ref=src_of(d), dst_ref=dst_of(mine[s]),
                send_sem=sems.at[kind, s, d], recv_sem=sems.at[kind + 1, s, mine[s]],
                device_id=_device(axis, peer_of(s, d)), device_id_type=pl.DeviceIdType.MESH,
            )
            c.start()
            copies.append((d, c))
        for d, c in copies:
            c.wait_send()
            pltpu.make_async_remote_copy(
                src_ref=src_of(d), dst_ref=dst_of(d),
                send_sem=sems.at[kind, s, d], recv_sem=sems.at[kind + 1, s, d],
                device_id=_device(axis, peer_of(s, d)), device_id_type=pl.DeviceIdType.MESH,
            ).wait_recv()

    if mode == "sum":
        acc = x_ref
        for s in range(stages):
            rb = rbufs[s]
            rb[mine[s]] = acc[...]
            exchange_stage(0, s, lambda d: acc, lambda d, rb=rb: rb.at[d])
            total = rb[0]
            for d in range(1, factors[s]):
                total = total + rb[d]
            if s == stages - 1:
                y_ref[...] = total
            else:
                rbufs[s + 1][mine[s + 1]] = total
                acc = rbufs[s + 1].at[mine[s + 1]]
        return

    if mode == "reduce":
        cur = x_ref
        for s in range(stages):
            lead = stages - 1 - s

            def src_of(d, cur=cur, lead=lead):
                return cur.at[(slice(None),) * lead + (d,)]

            rb = rbufs[s]
            exchange_stage(0, s, src_of, lambda d, rb=rb: rb.at[d])
            total = cur[(slice(None),) * lead + (mine[s],)]
            for k in range(1, factors[s]):
                total = total + rb[other(s, k)]
            rb[mine[s]] = total
            cur = rb.at[mine[s]]
        own = epilogue(cur[...], s_ref)
    else:
        own = x_ref[...]
    gbuf[tuple(mine[::-1])] = own.astype(gbuf.dtype)
    for s in reversed(range(stages)):
        lead = stages - 1 - s

        def view(d, s=s, lead=lead):
            return gbuf.at[(slice(None),) * lead + (d,) + tuple(mine[s - 1::-1] if s else ())]

        exchange_stage(2, s, lambda d, s=s: view(mine[s]), view)
    y_ref[...] = gbuf[...]


def staged(x, axis, factors, mode, cid, scale=None, epilogue=None, out_dtype=None):
    n = math.prod(factors)
    stages = len(factors)
    out_dtype = out_dtype or x.dtype
    if mode == "reduce":
        chunk = x.shape[1:]
        x = x.reshape(tuple(reversed(factors)) + chunk)
    else:
        chunk = x.shape
    scratch = []
    if mode in ("reduce", "sum"):
        for s in range(stages):
            rest = tuple(reversed(factors[s + 1:])) if mode == "reduce" else ()
            scratch.append(pltpu.VMEM((factors[s],) + rest + chunk, jnp.float32))
    if mode != "sum":
        scratch.append(pltpu.VMEM(tuple(reversed(factors)) + chunk, out_dtype))
    scratch.append(pltpu.SemaphoreType.DMA((4, stages, max(factors))))
    if mode == "sum":
        out_shape = chunk
    else:
        out_shape = tuple(reversed(factors)) + chunk
    args = (x,) if scale is None else (x, scale)
    nbytes = n * math.prod(chunk) * 4
    y = pl.pallas_call(
        functools.partial(_staged_kernel, axis=axis, factors=tuple(factors), mode=mode,
                          has_scale=scale is not None, epilogue=epilogue),
        out_shape=jax.ShapeDtypeStruct(out_shape, out_dtype),
        in_specs=[pl.BlockSpec(memory_space=pltpu.VMEM)] * len(args),
        out_specs=pl.BlockSpec(memory_space=pltpu.VMEM),
        scratch_shapes=scratch,
        compiler_params=pltpu.CompilerParams(collective_id=cid, has_side_effects=True),
        cost_estimate=pl.CostEstimate(flops=0, transcendentals=0, bytes_accessed=2 * nbytes),
    )(*args)
    if mode == "sum":
        return y
    return y.reshape((n,) + chunk)


QUERY_FACTORS = (2, 4, 4)
GRAM_FACTORS = (4, 8)
ROW_FACTORS = (4, 4)


def _query_epilogue(total, s_ref):
    return (total * s_ref[...]).astype(jnp.bfloat16)


def _product_epilogue(total, s_ref):
    return total * s_ref[...]


GROUP = 4


def _products_kernel(ids_ref, count_ref, src_ref, tiles_hbm, out_ref, tiles, sems, *, forward):
    slots = tiles.shape[0]
    groups = slots // GROUP

    def fetch(g):
        return pltpu.make_async_copy(
            tiles_hbm.at[pl.ds(g * GROUP, GROUP)], tiles.at[pl.ds(g * GROUP, GROUP)], sems.at[g]
        )

    for g in range(groups):
        fetch(g).start()
    out_ref[...] = jnp.zeros_like(out_ref)
    src_row, dst_row = (1, 0) if forward else (0, 1)
    count = count_ref[0]
    for g in range(groups):
        fetch(g).wait()
        ys = []
        for k in range(g * GROUP, (g + 1) * GROUP):
            x = src_ref[ids_ref[src_row, k]]
            t = tiles[k]
            if forward:
                y = lax.dot_general(x, t, (((1,), (1,)), ((), ())),
                                    preferred_element_type=jnp.float32)
            else:
                y = jnp.dot(x, t, preferred_element_type=jnp.float32)
            ys.append(jnp.where(k < count, y, 0.0))
        for k, y in zip(range(g * GROUP, (g + 1) * GROUP), ys):
            d = ids_ref[dst_row, k]
            out_ref[d] = out_ref[d] + y


def tile_products(slot_ids, live_count, src, tile_set, blocks, forward):
    slots, side, _ = tile_set.shape
    width = src.shape[1]
    return pl.pallas_call(
        functools.partial(_products_kernel, forward=forward),
        out_shape=jax.ShapeDtypeStruct((blocks, width, side), jnp.float32),
        in_specs=[
            pl.BlockSpec(memory_space=pltpu.SMEM),
            pl.BlockSpec(memory_space=pltpu.SMEM),
            pl.BlockSpec(memory_space=pltpu.VMEM),
            pl.BlockSpec(memory_space=pl.ANY),
        ],
        out_specs=pl.BlockSpec(memory_space=pltpu.VMEM),
        scratch_shapes=[
            pltpu.VMEM(tile_set.shape, tile_set.dtype),
            pltpu.SemaphoreType.DMA((slots // GROUP,)),
        ],
        cost_estimate=pl.CostEstimate(
            flops=2 * slots * width * side * side, transcendentals=0,
            bytes_accessed=slots * side * side * 2 + src.size * 2 + blocks * width * side * 4,
        ),
    )(slot_ids, live_count.reshape(1), src, tile_set)


def orthonormal(lifted, gram):
    lower = jnp.linalg.cholesky(gram)
    return lax.linalg.triangular_solve(lower, lifted, left_side=True, lower=True)


def shards(tiles, tile_ids, tile_count, query_degree, product_degree, panel):
    tile_set = tiles[0, 0]
    slot_ids = tile_ids[0, 0]
    live_count = tile_count[0, 0]
    side = tile_set.shape[1]
    width = panel.shape[0]
    query_tiles = query_degree.shape[0] // side
    product_tiles = product_degree.shape[0] // side
    n_row = lax.axis_size("row")
    n_col = lax.axis_size("col")
    qscale = (1.0 / jnp.sqrt(query_degree.astype(jnp.float32))).reshape(query_tiles, 1, side)
    pscale = (1.0 / jnp.sqrt(product_degree.astype(jnp.float32))).reshape(product_tiles, 1, side)
    row_at = lax.axis_index("row")
    col_at = lax.axis_index("col")
    share = panel.shape[1]
    block = product_degree.shape[0]
    q_per_tile = n_col // query_tiles
    p_per_tile = n_row // product_tiles
    my_qscale = lax.dynamic_index_in_dim(qscale, col_at // q_per_tile, keepdims=False)
    my_pscale = lax.dynamic_index_in_dim(pscale, row_at // p_per_tile, keepdims=False)
    root_count = math.sqrt(product_degree.shape[0] * n_col)

    panel_pscale = lax.dynamic_slice_in_dim(pscale.reshape(block), row_at * share, share)
    scaled0 = (panel * panel_pscale[None, :]).astype(jnp.bfloat16)
    gathered = staged(scaled0, "row", ROW_FACTORS, "gather", 0)
    per_tile = side // share
    scaled_tiles = jnp.transpose(
        gathered.reshape(product_tiles, per_tile, width, share), (0, 2, 1, 3)
    ).reshape(product_tiles, width, side)
    current = None
    for iteration in range(ITERS):
        if current is not None:
            scaled_tiles = (
                jnp.transpose(current.reshape(width, product_tiles, side), (1, 0, 2)) * pscale
            ).astype(jnp.bfloat16)
        partial_sum = tile_products(slot_ids, live_count, scaled_tiles, tile_set, query_tiles, True)
        query_tiles_panel = staged(
            partial_sum.reshape(n_col, width // q_per_tile, side), "col", QUERY_FACTORS, "reduce", 1,
            scale=my_qscale, epilogue=_query_epilogue, out_dtype=jnp.bfloat16,
        ).reshape(query_tiles, width, side)
        product_partial = tile_products(
            slot_ids, live_count, query_tiles_panel, tile_set, product_tiles, False
        )
        lifted_tiles = staged(
            product_partial.reshape(n_row, width // p_per_tile, side), "row", ROW_FACTORS, "reduce", 2,
            scale=my_pscale, epilogue=_product_epilogue,
        ).reshape(product_tiles, width, side)
        gram_part = jnp.einsum("pri,psi->rs", lifted_tiles, lifted_tiles, precision=HIGH)
        gram = staged(gram_part, "col", GRAM_FACTORS, "sum", 3)
        lifted = jnp.transpose(lifted_tiles, (1, 0, 2)).reshape(width, block)
        current = orthonormal(lifted, gram)
    mine = lax.dynamic_slice_in_dim(current, row_at * share, share, axis=1)
    return mine * root_count


def solution(mesh):
    in_specs = (
        P("row", "col", None, None, None),
        P("row", "col", None, None),
        P("row", "col"),
        P("row"),
        P("col"),
        P(None, ("col", "row")),
    )
    out_specs = P(None, ("col", "row"))
    return jax.shard_map(shards, mesh=mesh, in_specs=in_specs, out_specs=out_specs, check_vma=False)
```

```python
import functools
import math

import jax
import jax.numpy as jnp
from jax import lax
from jax.experimental import pallas as pl
from jax.experimental.pallas import tpu as pltpu
from jax.sharding import PartitionSpec as P

ITERS = 2


HIGH = lax.Precision.HIGHEST

AXES = ("row", "col")


def _device(axis, peer):
    if axis == "row":
        return (peer, lax.axis_index("col"))
    return (lax.axis_index("row"), peer)


class _Plan:
    def __init__(self, axis, factors):
        self.axis = axis
        self.factors = tuple(factors)
        self.stages = len(factors)
        self.me = lax.axis_index(axis)
        self.strides = [math.prod(factors[:s]) for s in range(self.stages)]
        self.mine = [lax.rem(lax.div(self.me, self.strides[s]), factors[s])
                     for s in range(self.stages)]

    def peer(self, s, d):
        return _device(self.axis, self.me + (d - self.mine[s]) * self.strides[s])

    def other(self, s, k):
        return lax.rem(self.mine[s] + k, self.factors[s])

    def peers(self):
        return [self.peer(s, self.other(s, k)) for s in range(self.stages)
                for k in range(1, self.factors[s])]


def _barrier(plans):
    barrier = pltpu.get_barrier_semaphore()
    count = 0
    for plan in plans:
        for dev in plan.peers():
            pl.semaphore_signal(barrier, inc=1, device_id=dev, device_id_type=pl.DeviceIdType.MESH)
            count += 1
    pl.semaphore_wait(barrier, count)


def _exchange(plan, sems, kind, s, src_of, dst_of):
    copies = []
    mine = plan.mine[s]
    for k in range(1, plan.factors[s]):
        d = plan.other(s, k)
        c = pltpu.make_async_remote_copy(
            src_ref=src_of(d), dst_ref=dst_of(mine),
            send_sem=sems.at[kind, s, d], recv_sem=sems.at[kind + 1, s, mine],
            device_id=plan.peer(s, d), device_id_type=pl.DeviceIdType.MESH,
        )
        c.start()
        copies.append((d, c))
    for d, c in copies:
        c.wait_send()
        pltpu.make_async_remote_copy(
            src_ref=src_of(d), dst_ref=dst_of(d),
            send_sem=sems.at[kind, s, d], recv_sem=sems.at[kind + 1, s, d],
            device_id=plan.peer(s, d), device_id_type=pl.DeviceIdType.MESH,
        ).wait_recv()


def _reduce_scatter(plan, sems, kind, x_ref, rbufs):
    cur = x_ref
    for s in range(plan.stages):
        lead = plan.stages - 1 - s

        def src_of(d, cur=cur, lead=lead):
            return cur.at[(slice(None),) * lead + (d,)]

        rb = rbufs[s]
        _exchange(plan, sems, kind, s, src_of, lambda d, rb=rb: rb.at[d])
        total = cur[(slice(None),) * lead + (plan.mine[s],)]
        for k in range(1, plan.factors[s]):
            total = total + rb[plan.other(s, k)]
        rb[plan.mine[s]] = total
        cur = rb.at[plan.mine[s]]
    return cur


def _all_gather(plan, sems, kind, gbuf, own):
    mine = plan.mine
    gbuf[tuple(mine[::-1])] = own.astype(gbuf.dtype)
    for s in reversed(range(plan.stages)):
        lead = plan.stages - 1 - s

        def view(d, s=s, lead=lead):
            return gbuf.at[(slice(None),) * lead + (d,) + tuple(mine[s - 1::-1] if s else ())]

        _exchange(plan, sems, kind, s, lambda d, s=s: view(mine[s]), view)


def _sum(plan, sems, kind, value, rbufs):
    for s in range(plan.stages):
        rb = rbufs[s]
        rb[plan.mine[s]] = value
        src = rb.at[plan.mine[s]]
        _exchange(plan, sems, kind, s, lambda d, src=src: src, lambda d, rb=rb: rb.at[d])
        value = rb[0]
        for d in range(1, plan.factors[s]):
            value = value + rb[d]
    return value


def _staged_kernel(*refs, axis, factors, mode, has_scale, epilogue):
    if has_scale:
        x_ref, s_ref, y_ref = refs[:3]
        rest = refs[3:]
    else:
        x_ref, y_ref = refs[:2]
        s_ref = None
        rest = refs[2:]
    plan = _Plan(axis, factors)
    n_rs = plan.stages if mode in ("reduce", "sum") else 0
    rbufs = rest[:n_rs]
    gbuf = rest[n_rs] if mode != "sum" else None
    sems = rest[-1]
    _barrier([plan])
    if mode == "sum":
        y_ref[...] = _sum(plan, sems, 0, x_ref[...], rbufs)
        return
    if mode == "reduce":
        own = epilogue(_reduce_scatter(plan, sems, 0, x_ref, rbufs)[...], s_ref)
    else:
        own = x_ref[...]
    _all_gather(plan, sems, 2, gbuf, own)
    y_ref[...] = gbuf[...]


def _digits(j, factors):
    return tuple((j // math.prod(factors[:s])) % factors[s] for s in reversed(range(len(factors))))


def _product_gram_kernel(x_ref, s_ref, y_ref, g_ref, *rest, row_factors, col_factors):
    rows = _Plan("row", row_factors)
    cols = _Plan("col", col_factors)
    rbufs = rest[:rows.stages]
    gbuf = rest[rows.stages]
    cbufs = rest[rows.stages + 1:rows.stages + 1 + cols.stages]
    sems = rest[-1]
    _barrier([rows, cols])
    own = _reduce_scatter(rows, sems, 0, x_ref, rbufs)[...] * s_ref[...]
    _all_gather(rows, sems, 2, gbuf, own)
    y_ref[...] = gbuf[...]
    n = math.prod(row_factors)
    per = y_ref.shape[-2]
    width = g_ref.shape[0]
    gram = None
    for p in range(n * per // width):
        parts = [y_ref[_digits(p * width // per + i, row_factors)] for i in range(width // per)]
        block = jnp.concatenate(parts, axis=0)
        term = lax.dot_general(block, block, (((1,), (1,)), ((), ())), precision=HIGH,
                               preferred_element_type=jnp.float32)
        gram = term if gram is None else gram + term
    g_ref[...] = _sum(cols, sems, 4, gram, cbufs)


def product_gram(x, scale, row_factors, col_factors, cid, width):
    n = math.prod(row_factors)
    chunk = x.shape[1:]
    x = x.reshape(tuple(reversed(row_factors)) + chunk)
    scratch = []
    for s in range(len(row_factors)):
        scratch.append(pltpu.VMEM((row_factors[s],) + tuple(reversed(row_factors[s + 1:])) + chunk,
                                  jnp.float32))
    scratch.append(pltpu.VMEM(tuple(reversed(row_factors)) + chunk, jnp.float32))
    for s in range(len(col_factors)):
        scratch.append(pltpu.VMEM((col_factors[s], width, width), jnp.float32))
    scratch.append(pltpu.SemaphoreType.DMA((6, max(len(row_factors), len(col_factors)),
                                            max(row_factors + col_factors))))
    nbytes = n * math.prod(chunk) * 4
    y, g = pl.pallas_call(
        functools.partial(_product_gram_kernel, row_factors=tuple(row_factors),
                          col_factors=tuple(col_factors)),
        out_shape=(jax.ShapeDtypeStruct(tuple(reversed(row_factors)) + chunk, jnp.float32),
                   jax.ShapeDtypeStruct((width, width), jnp.float32)),
        in_specs=[pl.BlockSpec(memory_space=pltpu.VMEM)] * 2,
        out_specs=(pl.BlockSpec(memory_space=pltpu.VMEM), pl.BlockSpec(memory_space=pltpu.VMEM)),
        scratch_shapes=scratch,
        compiler_params=pltpu.CompilerParams(collective_id=cid, has_side_effects=True),
        cost_estimate=pl.CostEstimate(flops=0, transcendentals=0, bytes_accessed=2 * nbytes),
    )(x, scale)
    return y.reshape((n,) + chunk), g


def staged(x, axis, factors, mode, cid, scale=None, epilogue=None, out_dtype=None):
    n = math.prod(factors)
    stages = len(factors)
    out_dtype = out_dtype or x.dtype
    if mode == "reduce":
        chunk = x.shape[1:]
        x = x.reshape(tuple(reversed(factors)) + chunk)
    else:
        chunk = x.shape
    scratch = []
    if mode in ("reduce", "sum"):
        for s in range(stages):
            rest = tuple(reversed(factors[s + 1:])) if mode == "reduce" else ()
            scratch.append(pltpu.VMEM((factors[s],) + rest + chunk, jnp.float32))
    if mode != "sum":
        scratch.append(pltpu.VMEM(tuple(reversed(factors)) + chunk, out_dtype))
    scratch.append(pltpu.SemaphoreType.DMA((4, stages, max(factors))))
    if mode == "sum":
        out_shape = chunk
    else:
        out_shape = tuple(reversed(factors)) + chunk
    args = (x,) if scale is None else (x, scale)
    nbytes = n * math.prod(chunk) * 4
    y = pl.pallas_call(
        functools.partial(_staged_kernel, axis=axis, factors=tuple(factors), mode=mode,
                          has_scale=scale is not None, epilogue=epilogue),
        out_shape=jax.ShapeDtypeStruct(out_shape, out_dtype),
        in_specs=[pl.BlockSpec(memory_space=pltpu.VMEM)] * len(args),
        out_specs=pl.BlockSpec(memory_space=pltpu.VMEM),
        scratch_shapes=scratch,
        compiler_params=pltpu.CompilerParams(collective_id=cid, has_side_effects=True),
        cost_estimate=pl.CostEstimate(flops=0, transcendentals=0, bytes_accessed=2 * nbytes),
    )(*args)
    if mode == "sum":
        return y
    return y.reshape((n,) + chunk)


QUERY_FACTORS = (2, 4, 4)
GRAM_FACTORS = (4, 8)
ROW_FACTORS = (4, 4)


def _query_epilogue(total, s_ref):
    return (total * s_ref[...]).astype(jnp.bfloat16)


def _product_epilogue(total, s_ref):
    return total * s_ref[...]


GROUP = 8


def _products_kernel(ids_ref, count_ref, src_ref, tiles_hbm, out_ref, tiles, sems, *, forward):
    slots = tiles.shape[0]
    groups = slots // GROUP

    def fetch(g):
        return pltpu.make_async_copy(
            tiles_hbm.at[pl.ds(g * GROUP, GROUP)], tiles.at[pl.ds(g * GROUP, GROUP)], sems.at[g]
        )

    for g in range(groups):
        fetch(g).start()
    out_ref[...] = jnp.zeros_like(out_ref)
    src_row, dst_row = (1, 0) if forward else (0, 1)
    count = count_ref[0]
    for g in range(groups):
        fetch(g).wait()
        ys = []
        for k in range(g * GROUP, (g + 1) * GROUP):
            x = src_ref[ids_ref[src_row, k]]
            t = tiles[k]
            if forward:
                y = lax.dot_general(x, t, (((1,), (1,)), ((), ())),
                                    preferred_element_type=jnp.float32)
            else:
                y = jnp.dot(x, t, preferred_element_type=jnp.float32)
            ys.append(jnp.where(k < count, y, 0.0))
        for k, y in zip(range(g * GROUP, (g + 1) * GROUP), ys):
            d = ids_ref[dst_row, k]
            out_ref[d] = out_ref[d] + y


def tile_products(slot_ids, live_count, src, tile_set, blocks, forward):
    slots, side, _ = tile_set.shape
    width = src.shape[1]
    return pl.pallas_call(
        functools.partial(_products_kernel, forward=forward),
        out_shape=jax.ShapeDtypeStruct((blocks, width, side), jnp.float32),
        in_specs=[
            pl.BlockSpec(memory_space=pltpu.SMEM),
            pl.BlockSpec(memory_space=pltpu.SMEM),
            pl.BlockSpec(memory_space=pltpu.VMEM),
            pl.BlockSpec(memory_space=pl.ANY),
        ],
        out_specs=pl.BlockSpec(memory_space=pltpu.VMEM),
        scratch_shapes=[
            pltpu.VMEM(tile_set.shape, tile_set.dtype),
            pltpu.SemaphoreType.DMA((slots // GROUP,)),
        ],
        cost_estimate=pl.CostEstimate(
            flops=2 * slots * width * side * side, transcendentals=0,
            bytes_accessed=slots * side * side * 2 + src.size * 2 + blocks * width * side * 4,
        ),
    )(slot_ids, live_count.reshape(1), src, tile_set)


def orthonormal(lifted, gram):
    lower = jnp.linalg.cholesky(gram)
    return lax.linalg.triangular_solve(lower, lifted, left_side=True, lower=True)


def shards(tiles, tile_ids, tile_count, query_degree, product_degree, panel):
    tile_set = tiles[0, 0]
    slot_ids = tile_ids[0, 0]
    live_count = tile_count[0, 0]
    side = tile_set.shape[1]
    width = panel.shape[0]
    query_tiles = query_degree.shape[0] // side
    product_tiles = product_degree.shape[0] // side
    n_row = lax.axis_size("row")
    n_col = lax.axis_size("col")
    qscale = (1.0 / jnp.sqrt(query_degree.astype(jnp.float32))).reshape(query_tiles, 1, side)
    pscale = (1.0 / jnp.sqrt(product_degree.astype(jnp.float32))).reshape(product_tiles, 1, side)
    row_at = lax.axis_index("row")
    col_at = lax.axis_index("col")
    share = panel.shape[1]
    block = product_degree.shape[0]
    q_per_tile = n_col // query_tiles
    p_per_tile = n_row // product_tiles
    my_qscale = lax.dynamic_index_in_dim(qscale, col_at // q_per_tile, keepdims=False)
    my_pscale = lax.dynamic_index_in_dim(pscale, row_at // p_per_tile, keepdims=False)
    root_count = math.sqrt(product_degree.shape[0] * n_col)

    panel_pscale = lax.dynamic_slice_in_dim(pscale.reshape(block), row_at * share, share)
    scaled0 = (panel * panel_pscale[None, :]).astype(jnp.bfloat16)
    gathered = staged(scaled0, "row", ROW_FACTORS, "gather", 0)
    per_tile = side // share
    scaled_tiles = jnp.transpose(
        gathered.reshape(product_tiles, per_tile, width, share), (0, 2, 1, 3)
    ).reshape(product_tiles, width, side)
    current = None
    for iteration in range(ITERS):
        if current is not None:
            scaled_tiles = (
                jnp.transpose(current.reshape(width, product_tiles, side), (1, 0, 2)) * pscale
            ).astype(jnp.bfloat16)
        partial_sum = tile_products(slot_ids, live_count, scaled_tiles, tile_set, query_tiles, True)
        query_tiles_panel = staged(
            partial_sum.reshape(n_col, width // q_per_tile, side), "col", QUERY_FACTORS, "reduce", 1,
            scale=my_qscale, epilogue=_query_epilogue, out_dtype=jnp.bfloat16,
        ).reshape(query_tiles, width, side)
        product_partial = tile_products(
            slot_ids, live_count, query_tiles_panel, tile_set, product_tiles, False
        )
        lifted_pieces, gram = product_gram(
            product_partial.reshape(n_row, width // p_per_tile, side), my_pscale, ROW_FACTORS,
            GRAM_FACTORS, 2, width,
        )
        lifted_tiles = lifted_pieces.reshape(product_tiles, width, side)
        lifted = jnp.transpose(lifted_tiles, (1, 0, 2)).reshape(width, block)
        current = orthonormal(lifted, gram)
    mine = lax.dynamic_slice_in_dim(current, row_at * share, share, axis=1)
    return mine * root_count


def solution(mesh):
    in_specs = (
        P("row", "col", None, None, None),
        P("row", "col", None, None),
        P("row", "col"),
        P("row"),
        P("col"),
        P(None, ("col", "row")),
    )
    out_specs = P(None, ("col", "row"))
    return jax.shard_map(shards, mesh=mesh, in_specs=in_specs, out_specs=out_specs, check_vma=False)
```

```python
import functools
import math

import jax
import jax.numpy as jnp
from jax import lax
from jax.experimental import pallas as pl
from jax.experimental.pallas import tpu as pltpu
from jax.sharding import PartitionSpec as P

ITERS = 2


HIGH = lax.Precision.HIGHEST

AXES = ("row", "col")


def _device(axis, peer):
    if axis == "row":
        return (peer, lax.axis_index("col"))
    return (lax.axis_index("row"), peer)


class _Plan:
    def __init__(self, axis, factors):
        self.axis = axis
        self.factors = tuple(factors)
        self.stages = len(factors)
        self.me = lax.axis_index(axis)
        self.strides = [math.prod(factors[:s]) for s in range(self.stages)]
        self.mine = [lax.rem(lax.div(self.me, self.strides[s]), factors[s])
                     for s in range(self.stages)]

    def peer(self, s, d):
        return _device(self.axis, self.me + (d - self.mine[s]) * self.strides[s])

    def other(self, s, k):
        return lax.rem(self.mine[s] + k, self.factors[s])

    def peers(self):
        return [self.peer(s, self.other(s, k)) for s in range(self.stages)
                for k in range(1, self.factors[s])]


def _barrier(plans):
    barrier = pltpu.get_barrier_semaphore()
    count = 0
    for plan in plans:
        for dev in plan.peers():
            pl.semaphore_signal(barrier, inc=1, device_id=dev, device_id_type=pl.DeviceIdType.MESH)
            count += 1
    pl.semaphore_wait(barrier, count)


def _exchange(plan, sems, kind, s, src_of, dst_of):
    copies = []
    mine = plan.mine[s]
    for k in range(1, plan.factors[s]):
        d = plan.other(s, k)
        c = pltpu.make_async_remote_copy(
            src_ref=src_of(d), dst_ref=dst_of(mine),
            send_sem=sems.at[kind, s, d], recv_sem=sems.at[kind + 1, s, mine],
            device_id=plan.peer(s, d), device_id_type=pl.DeviceIdType.MESH,
        )
        c.start()
        copies.append((d, c))
    for d, c in copies:
        c.wait_send()
        pltpu.make_async_remote_copy(
            src_ref=src_of(d), dst_ref=dst_of(d),
            send_sem=sems.at[kind, s, d], recv_sem=sems.at[kind + 1, s, d],
            device_id=plan.peer(s, d), device_id_type=pl.DeviceIdType.MESH,
        ).wait_recv()


def _reduce_scatter(plan, sems, kind, x_ref, rbufs):
    cur = x_ref
    for s in range(plan.stages):
        lead = plan.stages - 1 - s

        def src_of(d, cur=cur, lead=lead):
            return cur.at[(slice(None),) * lead + (d,)]

        rb = rbufs[s]
        _exchange(plan, sems, kind, s, src_of, lambda d, rb=rb: rb.at[d])
        total = cur[(slice(None),) * lead + (plan.mine[s],)]
        for k in range(1, plan.factors[s]):
            total = total + rb[plan.other(s, k)]
        rb[plan.mine[s]] = total
        cur = rb.at[plan.mine[s]]
    return cur


def _all_gather(plan, sems, kind, gbuf, own):
    mine = plan.mine
    gbuf[tuple(mine[::-1])] = own.astype(gbuf.dtype)
    for s in reversed(range(plan.stages)):
        lead = plan.stages - 1 - s

        def view(d, s=s, lead=lead):
            return gbuf.at[(slice(None),) * lead + (d,) + tuple(mine[s - 1::-1] if s else ())]

        _exchange(plan, sems, kind, s, lambda d, s=s: view(mine[s]), view)


def _sum(plan, sems, kind, value, rbufs):
    for s in range(plan.stages):
        rb = rbufs[s]
        rb[plan.mine[s]] = value
        src = rb.at[plan.mine[s]]
        _exchange(plan, sems, kind, s, lambda d, src=src: src, lambda d, rb=rb: rb.at[d])
        value = rb[0]
        for d in range(1, plan.factors[s]):
            value = value + rb[d]
    return value


def _staged_kernel(*refs, axis, factors, mode, has_scale, epilogue):
    if has_scale:
        x_ref, s_ref, y_ref = refs[:3]
        rest = refs[3:]
    else:
        x_ref, y_ref = refs[:2]
        s_ref = None
        rest = refs[2:]
    plan = _Plan(axis, factors)
    n_rs = plan.stages if mode in ("reduce", "sum") else 0
    rbufs = rest[:n_rs]
    gbuf = rest[n_rs] if mode != "sum" else None
    sems = rest[-1]
    _barrier([plan])
    if mode == "sum":
        y_ref[...] = _sum(plan, sems, 0, x_ref[...], rbufs)
        return
    if mode == "reduce":
        own = epilogue(_reduce_scatter(plan, sems, 0, x_ref, rbufs)[...], s_ref)
    else:
        own = x_ref[...]
    _all_gather(plan, sems, 2, gbuf, own)
    y_ref[...] = gbuf[...]


def _digits(j, factors):
    return tuple((j // math.prod(factors[:s])) % factors[s] for s in reversed(range(len(factors))))


def _product_gram_kernel(x_ref, s_ref, y_ref, g_ref, *rest, row_factors, col_factors):
    rows = _Plan("row", row_factors)
    cols = _Plan("col", col_factors)
    rbufs = rest[:rows.stages]
    gbuf = rest[rows.stages]
    cbufs = rest[rows.stages + 1:rows.stages + 1 + cols.stages]
    sems = rest[-1]
    _barrier([rows, cols])
    own = _reduce_scatter(rows, sems, 0, x_ref, rbufs)[...] * s_ref[...]
    _all_gather(rows, sems, 2, gbuf, own)
    y_ref[...] = gbuf[...]
    n = math.prod(row_factors)
    per = y_ref.shape[-2]
    width = g_ref.shape[0]
    gram = None
    for p in range(n * per // width):
        parts = [y_ref[_digits(p * width // per + i, row_factors)] for i in range(width // per)]
        block = jnp.concatenate(parts, axis=0)
        term = lax.dot_general(block, block, (((1,), (1,)), ((), ())), precision=HIGH,
                               preferred_element_type=jnp.float32)
        gram = term if gram is None else gram + term
    g_ref[...] = _sum(cols, sems, 4, gram, cbufs)


def product_gram(x, scale, row_factors, col_factors, cid, width):
    n = math.prod(row_factors)
    chunk = x.shape[1:]
    x = x.reshape(tuple(reversed(row_factors)) + chunk)
    scratch = []
    for s in range(len(row_factors)):
        scratch.append(pltpu.VMEM((row_factors[s],) + tuple(reversed(row_factors[s + 1:])) + chunk,
                                  jnp.float32))
    scratch.append(pltpu.VMEM(tuple(reversed(row_factors)) + chunk, jnp.float32))
    for s in range(len(col_factors)):
        scratch.append(pltpu.VMEM((col_factors[s], width, width), jnp.float32))
    scratch.append(pltpu.SemaphoreType.DMA((6, max(len(row_factors), len(col_factors)),
                                            max(row_factors + col_factors))))
    nbytes = n * math.prod(chunk) * 4
    y, g = pl.pallas_call(
        functools.partial(_product_gram_kernel, row_factors=tuple(row_factors),
                          col_factors=tuple(col_factors)),
        out_shape=(jax.ShapeDtypeStruct(tuple(reversed(row_factors)) + chunk, jnp.float32),
                   jax.ShapeDtypeStruct((width, width), jnp.float32)),
        in_specs=[pl.BlockSpec(memory_space=pltpu.VMEM)] * 2,
        out_specs=(pl.BlockSpec(memory_space=pltpu.VMEM), pl.BlockSpec(memory_space=pltpu.VMEM)),
        scratch_shapes=scratch,
        compiler_params=pltpu.CompilerParams(collective_id=cid, has_side_effects=True),
        cost_estimate=pl.CostEstimate(flops=0, transcendentals=0, bytes_accessed=2 * nbytes),
    )(x, scale)
    return y.reshape((n,) + chunk), g


def staged(x, axis, factors, mode, cid, scale=None, epilogue=None, out_dtype=None):
    n = math.prod(factors)
    stages = len(factors)
    out_dtype = out_dtype or x.dtype
    if mode == "reduce":
        chunk = x.shape[1:]
        x = x.reshape(tuple(reversed(factors)) + chunk)
    else:
        chunk = x.shape
    scratch = []
    if mode in ("reduce", "sum"):
        for s in range(stages):
            rest = tuple(reversed(factors[s + 1:])) if mode == "reduce" else ()
            scratch.append(pltpu.VMEM((factors[s],) + rest + chunk, jnp.float32))
    if mode != "sum":
        scratch.append(pltpu.VMEM(tuple(reversed(factors)) + chunk, out_dtype))
    scratch.append(pltpu.SemaphoreType.DMA((4, stages, max(factors))))
    if mode == "sum":
        out_shape = chunk
    else:
        out_shape = tuple(reversed(factors)) + chunk
    args = (x,) if scale is None else (x, scale)
    nbytes = n * math.prod(chunk) * 4
    y = pl.pallas_call(
        functools.partial(_staged_kernel, axis=axis, factors=tuple(factors), mode=mode,
                          has_scale=scale is not None, epilogue=epilogue),
        out_shape=jax.ShapeDtypeStruct(out_shape, out_dtype),
        in_specs=[pl.BlockSpec(memory_space=pltpu.VMEM)] * len(args),
        out_specs=pl.BlockSpec(memory_space=pltpu.VMEM),
        scratch_shapes=scratch,
        compiler_params=pltpu.CompilerParams(collective_id=cid, has_side_effects=True),
        cost_estimate=pl.CostEstimate(flops=0, transcendentals=0, bytes_accessed=2 * nbytes),
    )(*args)
    if mode == "sum":
        return y
    return y.reshape((n,) + chunk)


QUERY_FACTORS = (2, 4, 4)
GRAM_FACTORS = (4, 8)
ROW_FACTORS = (4, 4)


def _query_epilogue(total, s_ref):
    return (total * s_ref[...]).astype(jnp.bfloat16)


def _product_epilogue(total, s_ref):
    return total * s_ref[...]


GROUP = 8


def _products_kernel(ids_ref, count_ref, src_ref, tiles_hbm, out_ref, tiles, sems, *, forward):
    slots = tiles.shape[0]
    groups = slots // GROUP

    def fetch(g):
        return pltpu.make_async_copy(
            tiles_hbm.at[pl.ds(g * GROUP, GROUP)], tiles.at[pl.ds(g * GROUP, GROUP)], sems.at[g]
        )

    for g in range(groups):
        fetch(g).start()
    out_ref[...] = jnp.zeros_like(out_ref)
    src_row, dst_row = (1, 0) if forward else (0, 1)
    count = count_ref[0]
    for g in range(groups):
        fetch(g).wait()
        ys = []
        for k in range(g * GROUP, (g + 1) * GROUP):
            x = src_ref[ids_ref[src_row, k]]
            t = tiles[k]
            if forward:
                y = lax.dot_general(x, t, (((1,), (1,)), ((), ())),
                                    preferred_element_type=jnp.float32)
            else:
                y = jnp.dot(x, t, preferred_element_type=jnp.float32)
            ys.append(jnp.where(k < count, y, 0.0))
        for k, y in zip(range(g * GROUP, (g + 1) * GROUP), ys):
            d = ids_ref[dst_row, k]
            out_ref[d] = out_ref[d] + y


def tile_products(slot_ids, live_count, src, tile_set, blocks, forward):
    slots, side, _ = tile_set.shape
    width = src.shape[1]
    return pl.pallas_call(
        functools.partial(_products_kernel, forward=forward),
        out_shape=jax.ShapeDtypeStruct((blocks, width, side), jnp.float32),
        in_specs=[
            pl.BlockSpec(memory_space=pltpu.SMEM),
            pl.BlockSpec(memory_space=pltpu.SMEM),
            pl.BlockSpec(memory_space=pltpu.VMEM),
            pl.BlockSpec(memory_space=pl.ANY),
        ],
        out_specs=pl.BlockSpec(memory_space=pltpu.VMEM),
        scratch_shapes=[
            pltpu.VMEM(tile_set.shape, tile_set.dtype),
            pltpu.SemaphoreType.DMA((slots // GROUP,)),
        ],
        cost_estimate=pl.CostEstimate(
            flops=2 * slots * width * side * side, transcendentals=0,
            bytes_accessed=slots * side * side * 2 + src.size * 2 + blocks * width * side * 4,
        ),
    )(slot_ids, live_count.reshape(1), src, tile_set)


def lower_inverse(gram):
    lower = jnp.linalg.cholesky(gram)
    eye = jnp.eye(gram.shape[0], dtype=gram.dtype)
    return lax.linalg.triangular_solve(lower, eye, left_side=True, lower=True)


def shards(tiles, tile_ids, tile_count, query_degree, product_degree, panel):
    tile_set = tiles[0, 0]
    slot_ids = tile_ids[0, 0]
    live_count = tile_count[0, 0]
    side = tile_set.shape[1]
    width = panel.shape[0]
    query_tiles = query_degree.shape[0] // side
    product_tiles = product_degree.shape[0] // side
    n_row = lax.axis_size("row")
    n_col = lax.axis_size("col")
    qscale = (1.0 / jnp.sqrt(query_degree.astype(jnp.float32))).reshape(query_tiles, 1, side)
    pscale = (1.0 / jnp.sqrt(product_degree.astype(jnp.float32))).reshape(product_tiles, 1, side)
    row_at = lax.axis_index("row")
    col_at = lax.axis_index("col")
    share = panel.shape[1]
    block = product_degree.shape[0]
    q_per_tile = n_col // query_tiles
    p_per_tile = n_row // product_tiles
    my_qscale = lax.dynamic_index_in_dim(qscale, col_at // q_per_tile, keepdims=False)
    my_pscale = lax.dynamic_index_in_dim(pscale, row_at // p_per_tile, keepdims=False)
    root_count = math.sqrt(product_degree.shape[0] * n_col)

    panel_pscale = lax.dynamic_slice_in_dim(pscale.reshape(block), row_at * share, share)
    scaled0 = (panel * panel_pscale[None, :]).astype(jnp.bfloat16)
    gathered = staged(scaled0, "row", ROW_FACTORS, "gather", 0)
    per_tile = side // share
    scaled_tiles = jnp.transpose(
        gathered.reshape(product_tiles, per_tile, width, share), (0, 2, 1, 3)
    ).reshape(product_tiles, width, side)
    for iteration in range(ITERS):
        if iteration:
            current_tiles = jnp.einsum("rs,psi->pri", inverse, lifted_tiles, precision=HIGH)
            scaled_tiles = (current_tiles * pscale).astype(jnp.bfloat16)
        partial_sum = tile_products(slot_ids, live_count, scaled_tiles, tile_set, query_tiles, True)
        query_tiles_panel = staged(
            partial_sum.reshape(n_col, width // q_per_tile, side), "col", QUERY_FACTORS, "reduce", 1,
            scale=my_qscale, epilogue=_query_epilogue, out_dtype=jnp.bfloat16,
        ).reshape(query_tiles, width, side)
        product_partial = tile_products(
            slot_ids, live_count, query_tiles_panel, tile_set, product_tiles, False
        )
        lifted_pieces, gram = product_gram(
            product_partial.reshape(n_row, width // p_per_tile, side), my_pscale, ROW_FACTORS,
            GRAM_FACTORS, 2, width,
        )
        lifted_tiles = lifted_pieces.reshape(product_tiles, width, side)
        inverse = lower_inverse(gram)
    my_tile = lax.dynamic_index_in_dim(lifted_tiles, row_at // per_tile, keepdims=False)
    my_lifted = lax.dynamic_slice_in_dim(my_tile, (row_at % per_tile) * share, share, axis=1)
    return jnp.einsum("rs,si->ri", inverse, my_lifted, precision=HIGH) * root_count


def solution(mesh):
    in_specs = (
        P("row", "col", None, None, None),
        P("row", "col", None, None),
        P("row", "col"),
        P("row"),
        P("col"),
        P(None, ("col", "row")),
    )
    out_specs = P(None, ("col", "row"))
    return jax.shard_map(shards, mesh=mesh, in_specs=in_specs, out_specs=out_specs, check_vma=False)
```

```python
import functools
import math

import jax
import jax.numpy as jnp
from jax import lax
from jax.experimental import pallas as pl
from jax.experimental.pallas import tpu as pltpu
from jax.sharding import PartitionSpec as P

ITERS = 2


HIGH = lax.Precision.HIGHEST

AXES = ("row", "col")


def _device(axis, peer):
    if axis == "row":
        return (peer, lax.axis_index("col"))
    return (lax.axis_index("row"), peer)


class _Plan:
    def __init__(self, axis, factors):
        self.axis = axis
        self.factors = tuple(factors)
        self.stages = len(factors)
        self.me = lax.axis_index(axis)
        self.strides = [math.prod(factors[:s]) for s in range(self.stages)]
        self.mine = [lax.rem(lax.div(self.me, self.strides[s]), factors[s])
                     for s in range(self.stages)]

    def peer(self, s, d):
        return _device(self.axis, self.me + (d - self.mine[s]) * self.strides[s])

    def other(self, s, k):
        return lax.rem(self.mine[s] + k, self.factors[s])

    def peers(self):
        return [self.peer(s, self.other(s, k)) for s in range(self.stages)
                for k in range(1, self.factors[s])]


def _barrier(plans):
    barrier = pltpu.get_barrier_semaphore()
    count = 0
    for plan in plans:
        for dev in plan.peers():
            pl.semaphore_signal(barrier, inc=1, device_id=dev, device_id_type=pl.DeviceIdType.MESH)
            count += 1
    pl.semaphore_wait(barrier, count)


def _exchange(plan, sems, kind, s, src_of, dst_of, pending):
    copies = []
    mine = plan.mine[s]
    for k in range(1, plan.factors[s]):
        d = plan.other(s, k)
        c = pltpu.make_async_remote_copy(
            src_ref=src_of(d), dst_ref=dst_of(mine),
            send_sem=sems.at[kind, s, d], recv_sem=sems.at[kind + 1, s, mine],
            device_id=plan.peer(s, d), device_id_type=pl.DeviceIdType.MESH,
        )
        c.start()
        copies.append((d, c))
    pending.extend(c for _, c in copies)
    for d, c in copies:
        pltpu.make_async_remote_copy(
            src_ref=src_of(d), dst_ref=dst_of(d),
            send_sem=sems.at[kind, s, d], recv_sem=sems.at[kind + 1, s, d],
            device_id=plan.peer(s, d), device_id_type=pl.DeviceIdType.MESH,
        ).wait_recv()


def _reduce_scatter(plan, sems, kind, x_ref, rbufs, pending):
    cur = x_ref
    for s in range(plan.stages):
        lead = plan.stages - 1 - s

        def src_of(d, cur=cur, lead=lead):
            return cur.at[(slice(None),) * lead + (d,)]

        rb = rbufs[s]
        _exchange(plan, sems, kind, s, src_of, lambda d, rb=rb: rb.at[d], pending)
        total = cur[(slice(None),) * lead + (plan.mine[s],)]
        for k in range(1, plan.factors[s]):
            total = total + rb[plan.other(s, k)]
        rb[plan.mine[s]] = total
        cur = rb.at[plan.mine[s]]
    return cur


def _all_gather(plan, sems, kind, gbuf, own, pending):
    mine = plan.mine
    gbuf[tuple(mine[::-1])] = own.astype(gbuf.dtype)
    for s in reversed(range(plan.stages)):
        lead = plan.stages - 1 - s

        def view(d, s=s, lead=lead):
            return gbuf.at[(slice(None),) * lead + (d,) + tuple(mine[s - 1::-1] if s else ())]

        _exchange(plan, sems, kind, s, lambda d, s=s: view(mine[s]), view, pending)


def _sum(plan, sems, kind, value, rbufs, pending):
    for s in range(plan.stages):
        rb = rbufs[s]
        rb[plan.mine[s]] = value
        src = rb.at[plan.mine[s]]
        _exchange(plan, sems, kind, s, lambda d, src=src: src, lambda d, rb=rb: rb.at[d], pending)
        value = rb[0]
        for d in range(1, plan.factors[s]):
            value = value + rb[d]
    return value


def _staged_kernel(*refs, axis, factors, mode, has_scale, epilogue):
    if has_scale:
        x_ref, s_ref, y_ref = refs[:3]
        rest = refs[3:]
    else:
        x_ref, y_ref = refs[:2]
        s_ref = None
        rest = refs[2:]
    plan = _Plan(axis, factors)
    n_rs = plan.stages if mode in ("reduce", "sum") else 0
    rbufs = rest[:n_rs]
    gbuf = rest[n_rs] if mode != "sum" else None
    sems = rest[-1]
    _barrier([plan])
    pending = []
    if mode == "sum":
        y_ref[...] = _sum(plan, sems, 0, x_ref[...], rbufs, pending)
    else:
        if mode == "reduce":
            own = epilogue(_reduce_scatter(plan, sems, 0, x_ref, rbufs, pending)[...], s_ref)
        else:
            own = x_ref[...]
        _all_gather(plan, sems, 2, gbuf, own, pending)
        y_ref[...] = gbuf[...]
    for c in pending:
        c.wait_send()


def _digits(j, factors):
    return tuple((j // math.prod(factors[:s])) % factors[s] for s in reversed(range(len(factors))))


def _product_gram_kernel(x_ref, s_ref, y_ref, g_ref, *rest, row_factors, col_factors):
    rows = _Plan("row", row_factors)
    cols = _Plan("col", col_factors)
    rbufs = rest[:rows.stages]
    gbuf = rest[rows.stages]
    cbufs = rest[rows.stages + 1:rows.stages + 1 + cols.stages]
    sems = rest[-1]
    _barrier([rows, cols])
    pending = []
    own = _reduce_scatter(rows, sems, 0, x_ref, rbufs, pending)[...] * s_ref[...]
    _all_gather(rows, sems, 2, gbuf, own, pending)
    y_ref[...] = gbuf[...]
    n = math.prod(row_factors)
    per = y_ref.shape[-2]
    width = g_ref.shape[0]
    gram = None
    for p in range(n * per // width):
        parts = [y_ref[_digits(p * width // per + i, row_factors)] for i in range(width // per)]
        block = jnp.concatenate(parts, axis=0)
        term = lax.dot_general(block, block, (((1,), (1,)), ((), ())), precision=HIGH,
                               preferred_element_type=jnp.float32)
        gram = term if gram is None else gram + term
    g_ref[...] = _sum(cols, sems, 4, gram, cbufs, pending)
    for c in pending:
        c.wait_send()


def product_gram(x, scale, row_factors, col_factors, cid, width):
    n = math.prod(row_factors)
    chunk = x.shape[1:]
    x = x.reshape(tuple(reversed(row_factors)) + chunk)
    scratch = []
    for s in range(len(row_factors)):
        scratch.append(pltpu.VMEM((row_factors[s],) + tuple(reversed(row_factors[s + 1:])) + chunk,
                                  jnp.float32))
    scratch.append(pltpu.VMEM(tuple(reversed(row_factors)) + chunk, jnp.float32))
    for s in range(len(col_factors)):
        scratch.append(pltpu.VMEM((col_factors[s], width, width), jnp.float32))
    scratch.append(pltpu.SemaphoreType.DMA((6, max(len(row_factors), len(col_factors)),
                                            max(row_factors + col_factors))))
    nbytes = n * math.prod(chunk) * 4
    y, g = pl.pallas_call(
        functools.partial(_product_gram_kernel, row_factors=tuple(row_factors),
                          col_factors=tuple(col_factors)),
        out_shape=(jax.ShapeDtypeStruct(tuple(reversed(row_factors)) + chunk, jnp.float32),
                   jax.ShapeDtypeStruct((width, width), jnp.float32)),
        in_specs=[pl.BlockSpec(memory_space=pltpu.VMEM)] * 2,
        out_specs=(pl.BlockSpec(memory_space=pltpu.VMEM), pl.BlockSpec(memory_space=pltpu.VMEM)),
        scratch_shapes=scratch,
        compiler_params=pltpu.CompilerParams(collective_id=cid, has_side_effects=True),
        cost_estimate=pl.CostEstimate(flops=0, transcendentals=0, bytes_accessed=2 * nbytes),
    )(x, scale)
    return y.reshape((n,) + chunk), g


def staged(x, axis, factors, mode, cid, scale=None, epilogue=None, out_dtype=None):
    n = math.prod(factors)
    stages = len(factors)
    out_dtype = out_dtype or x.dtype
    if mode == "reduce":
        chunk = x.shape[1:]
        x = x.reshape(tuple(reversed(factors)) + chunk)
    else:
        chunk = x.shape
    scratch = []
    if mode in ("reduce", "sum"):
        for s in range(stages):
            rest = tuple(reversed(factors[s + 1:])) if mode == "reduce" else ()
            scratch.append(pltpu.VMEM((factors[s],) + rest + chunk, jnp.float32))
    if mode != "sum":
        scratch.append(pltpu.VMEM(tuple(reversed(factors)) + chunk, out_dtype))
    scratch.append(pltpu.SemaphoreType.DMA((4, stages, max(factors))))
    if mode == "sum":
        out_shape = chunk
    else:
        out_shape = tuple(reversed(factors)) + chunk
    args = (x,) if scale is None else (x, scale)
    nbytes = n * math.prod(chunk) * 4
    y = pl.pallas_call(
        functools.partial(_staged_kernel, axis=axis, factors=tuple(factors), mode=mode,
                          has_scale=scale is not None, epilogue=epilogue),
        out_shape=jax.ShapeDtypeStruct(out_shape, out_dtype),
        in_specs=[pl.BlockSpec(memory_space=pltpu.VMEM)] * len(args),
        out_specs=pl.BlockSpec(memory_space=pltpu.VMEM),
        scratch_shapes=scratch,
        compiler_params=pltpu.CompilerParams(collective_id=cid, has_side_effects=True),
        cost_estimate=pl.CostEstimate(flops=0, transcendentals=0, bytes_accessed=2 * nbytes),
    )(*args)
    if mode == "sum":
        return y
    return y.reshape((n,) + chunk)


QUERY_FACTORS = (2, 4, 4)
GRAM_FACTORS = (4, 8)
ROW_FACTORS = (4, 4)


def _query_epilogue(total, s_ref):
    return (total * s_ref[...]).astype(jnp.bfloat16)


def _product_epilogue(total, s_ref):
    return total * s_ref[...]


GROUP = 8


def _products_kernel(ids_ref, count_ref, src_ref, tiles_hbm, out_ref, tiles, sems, *, forward):
    slots = tiles.shape[0]
    groups = slots // GROUP

    def fetch(g):
        return pltpu.make_async_copy(
            tiles_hbm.at[pl.ds(g * GROUP, GROUP)], tiles.at[pl.ds(g * GROUP, GROUP)], sems.at[g]
        )

    for g in range(groups):
        fetch(g).start()
    out_ref[...] = jnp.zeros_like(out_ref)
    src_row, dst_row = (1, 0) if forward else (0, 1)
    count = count_ref[0]
    for g in range(groups):
        fetch(g).wait()
        ys = []
        for k in range(g * GROUP, (g + 1) * GROUP):
            x = src_ref[ids_ref[src_row, k]]
            t = tiles[k]
            if forward:
                y = lax.dot_general(x, t, (((1,), (1,)), ((), ())),
                                    preferred_element_type=jnp.float32)
            else:
                y = jnp.dot(x, t, preferred_element_type=jnp.float32)
            ys.append(jnp.where(k < count, y, 0.0))
        for k, y in zip(range(g * GROUP, (g + 1) * GROUP), ys):
            d = ids_ref[dst_row, k]
            out_ref[d] = out_ref[d] + y


def tile_products(slot_ids, live_count, src, tile_set, blocks, forward):
    slots, side, _ = tile_set.shape
    width = src.shape[1]
    return pl.pallas_call(
        functools.partial(_products_kernel, forward=forward),
        out_shape=jax.ShapeDtypeStruct((blocks, width, side), jnp.float32),
        in_specs=[
            pl.BlockSpec(memory_space=pltpu.SMEM),
            pl.BlockSpec(memory_space=pltpu.SMEM),
            pl.BlockSpec(memory_space=pltpu.VMEM),
            pl.BlockSpec(memory_space=pl.ANY),
        ],
        out_specs=pl.BlockSpec(memory_space=pltpu.VMEM),
        scratch_shapes=[
            pltpu.VMEM(tile_set.shape, tile_set.dtype),
            pltpu.SemaphoreType.DMA((slots // GROUP,)),
        ],
        cost_estimate=pl.CostEstimate(
            flops=2 * slots * width * side * side, transcendentals=0,
            bytes_accessed=slots * side * side * 2 + src.size * 2 + blocks * width * side * 4,
        ),
    )(slot_ids, live_count.reshape(1), src, tile_set)


def lower_inverse(gram):
    lower = jnp.linalg.cholesky(gram)
    eye = jnp.eye(gram.shape[0], dtype=gram.dtype)
    return lax.linalg.triangular_solve(lower, eye, left_side=True, lower=True)


def shards(tiles, tile_ids, tile_count, query_degree, product_degree, panel):
    tile_set = tiles[0, 0]
    slot_ids = tile_ids[0, 0]
    live_count = tile_count[0, 0]
    side = tile_set.shape[1]
    width = panel.shape[0]
    query_tiles = query_degree.shape[0] // side
    product_tiles = product_degree.shape[0] // side
    n_row = lax.axis_size("row")
    n_col = lax.axis_size("col")
    qscale = (1.0 / jnp.sqrt(query_degree.astype(jnp.float32))).reshape(query_tiles, 1, side)
    pscale = (1.0 / jnp.sqrt(product_degree.astype(jnp.float32))).reshape(product_tiles, 1, side)
    row_at = lax.axis_index("row")
    col_at = lax.axis_index("col")
    share = panel.shape[1]
    block = product_degree.shape[0]
    q_per_tile = n_col // query_tiles
    p_per_tile = n_row // product_tiles
    my_qscale = lax.dynamic_index_in_dim(qscale, col_at // q_per_tile, keepdims=False)
    my_pscale = lax.dynamic_index_in_dim(pscale, row_at // p_per_tile, keepdims=False)
    root_count = math.sqrt(product_degree.shape[0] * n_col)

    panel_pscale = lax.dynamic_slice_in_dim(pscale.reshape(block), row_at * share, share)
    scaled0 = (panel * panel_pscale[None, :]).astype(jnp.bfloat16)
    gathered = staged(scaled0, "row", ROW_FACTORS, "gather", 0)
    per_tile = side // share
    scaled_tiles = jnp.transpose(
        gathered.reshape(product_tiles, per_tile, width, share), (0, 2, 1, 3)
    ).reshape(product_tiles, width, side)
    for iteration in range(ITERS):
        if iteration:
            current_tiles = jnp.einsum("rs,psi->pri", inverse, lifted_tiles, precision=HIGH)
            scaled_tiles = (current_tiles * pscale).astype(jnp.bfloat16)
        partial_sum = tile_products(slot_ids, live_count, scaled_tiles, tile_set, query_tiles, True)
        query_tiles_panel = staged(
            partial_sum.reshape(n_col, width // q_per_tile, side), "col", QUERY_FACTORS, "reduce", 1,
            scale=my_qscale, epilogue=_query_epilogue, out_dtype=jnp.bfloat16,
        ).reshape(query_tiles, width, side)
        product_partial = tile_products(
            slot_ids, live_count, query_tiles_panel, tile_set, product_tiles, False
        )
        lifted_pieces, gram = product_gram(
            product_partial.reshape(n_row, width // p_per_tile, side), my_pscale, ROW_FACTORS,
            GRAM_FACTORS, 2, width,
        )
        lifted_tiles = lifted_pieces.reshape(product_tiles, width, side)
        inverse = lower_inverse(gram)
    my_tile = lax.dynamic_index_in_dim(lifted_tiles, row_at // per_tile, keepdims=False)
    my_lifted = lax.dynamic_slice_in_dim(my_tile, (row_at % per_tile) * share, share, axis=1)
    return jnp.einsum("rs,si->ri", inverse, my_lifted, precision=HIGH) * root_count


def solution(mesh):
    in_specs = (
        P("row", "col", None, None, None),
        P("row", "col", None, None),
        P("row", "col"),
        P("row"),
        P("col"),
        P(None, ("col", "row")),
    )
    out_specs = P(None, ("col", "row"))
    return jax.shard_map(shards, mesh=mesh, in_specs=in_specs, out_specs=out_specs, check_vma=False)
```

```python
import functools
import math

import jax
import jax.numpy as jnp
from jax import lax
from jax.experimental import pallas as pl
from jax.experimental.pallas import tpu as pltpu
from jax.sharding import PartitionSpec as P

ITERS = 2


HIGH = lax.Precision.HIGHEST

AXES = ("row", "col")


def _device(axis, peer):
    if axis == "row":
        return (peer, lax.axis_index("col"))
    return (lax.axis_index("row"), peer)


class _Plan:
    def __init__(self, axis, factors):
        self.axis = axis
        self.factors = tuple(factors)
        self.stages = len(factors)
        self.me = lax.axis_index(axis)
        self.strides = [math.prod(factors[:s]) for s in range(self.stages)]
        self.mine = [lax.rem(lax.div(self.me, self.strides[s]), factors[s])
                     for s in range(self.stages)]

    def peer(self, s, d):
        return _device(self.axis, self.me + (d - self.mine[s]) * self.strides[s])

    def other(self, s, k):
        return lax.rem(self.mine[s] + k, self.factors[s])

    def peers(self):
        return [self.peer(s, self.other(s, k)) for s in range(self.stages)
                for k in range(1, self.factors[s])]


def _barrier(plans):
    barrier = pltpu.get_barrier_semaphore()
    count = 0
    for plan in plans:
        for dev in plan.peers():
            pl.semaphore_signal(barrier, inc=1, device_id=dev, device_id_type=pl.DeviceIdType.MESH)
            count += 1
    pl.semaphore_wait(barrier, count)


def _exchange(plan, sems, kind, s, src_of, dst_of, pending):
    copies = []
    mine = plan.mine[s]
    for k in range(1, plan.factors[s]):
        d = plan.other(s, k)
        c = pltpu.make_async_remote_copy(
            src_ref=src_of(d), dst_ref=dst_of(mine),
            send_sem=sems.at[kind, s, d], recv_sem=sems.at[kind + 1, s, mine],
            device_id=plan.peer(s, d), device_id_type=pl.DeviceIdType.MESH,
        )
        c.start()
        copies.append((d, c))
    pending.extend(c for _, c in copies)
    for d, c in copies:
        pltpu.make_async_remote_copy(
            src_ref=src_of(d), dst_ref=dst_of(d),
            send_sem=sems.at[kind, s, d], recv_sem=sems.at[kind + 1, s, d],
            device_id=plan.peer(s, d), device_id_type=pl.DeviceIdType.MESH,
        ).wait_recv()


def _reduce_scatter(plan, sems, kind, x_ref, rbufs, pending):
    cur = x_ref
    for s in range(plan.stages):
        lead = plan.stages - 1 - s

        def src_of(d, cur=cur, lead=lead):
            return cur.at[(slice(None),) * lead + (d,)]

        rb = rbufs[s]
        _exchange(plan, sems, kind, s, src_of, lambda d, rb=rb: rb.at[d], pending)
        total = cur[(slice(None),) * lead + (plan.mine[s],)]
        for k in range(1, plan.factors[s]):
            total = total + rb[plan.other(s, k)]
        rb[plan.mine[s]] = total
        cur = rb.at[plan.mine[s]]
    return cur


def _all_gather(plan, sems, kind, gbuf, own, pending):
    mine = plan.mine
    gbuf[tuple(mine[::-1])] = own.astype(gbuf.dtype)
    for s in reversed(range(plan.stages)):
        lead = plan.stages - 1 - s

        def view(d, s=s, lead=lead):
            return gbuf.at[(slice(None),) * lead + (d,) + tuple(mine[s - 1::-1] if s else ())]

        _exchange(plan, sems, kind, s, lambda d, s=s: view(mine[s]), view, pending)


def _sum(plan, sems, kind, value, rbufs, pending):
    for s in range(plan.stages):
        rb = rbufs[s]
        rb[plan.mine[s]] = value
        src = rb.at[plan.mine[s]]
        _exchange(plan, sems, kind, s, lambda d, src=src: src, lambda d, rb=rb: rb.at[d], pending)
        value = rb[0]
        for d in range(1, plan.factors[s]):
            value = value + rb[d]
    return value


def _staged_kernel(*refs, axis, factors, mode, has_scale, epilogue):
    if has_scale:
        x_ref, s_ref, y_ref = refs[:3]
        rest = refs[3:]
    else:
        x_ref, y_ref = refs[:2]
        s_ref = None
        rest = refs[2:]
    plan = _Plan(axis, factors)
    n_rs = plan.stages if mode in ("reduce", "sum") else 0
    rbufs = rest[:n_rs]
    gbuf = rest[n_rs] if mode != "sum" else None
    sems = rest[-1]
    _barrier([plan])
    pending = []
    if mode == "sum":
        y_ref[...] = _sum(plan, sems, 0, x_ref[...], rbufs, pending)
    else:
        if mode == "reduce":
            own = epilogue(_reduce_scatter(plan, sems, 0, x_ref, rbufs, pending)[...], s_ref)
        else:
            own = x_ref[...]
        _all_gather(plan, sems, 2, gbuf, own, pending)
        if mode == "gather" and len(y_ref.shape) == 3:
            n = math.prod(factors)
            share = own.shape[-1]
            per = y_ref.shape[-1] // share
            for j in range(n):
                y_ref[j // per, :, pl.ds((j % per) * share, share)] = gbuf[_digits(j, factors)]
        else:
            y_ref[...] = gbuf[...]
    for c in pending:
        c.wait_send()


def _digits(j, factors):
    return tuple((j // math.prod(factors[:s])) % factors[s] for s in reversed(range(len(factors))))


def _product_gram_kernel(x_ref, s_ref, y_ref, g_ref, *rest, row_factors, col_factors):
    rows = _Plan("row", row_factors)
    cols = _Plan("col", col_factors)
    rbufs = rest[:rows.stages]
    gbuf = rest[rows.stages]
    cbufs = rest[rows.stages + 1:rows.stages + 1 + cols.stages]
    sems = rest[-1]
    _barrier([rows, cols])
    pending = []
    own = _reduce_scatter(rows, sems, 0, x_ref, rbufs, pending)[...] * s_ref[...]
    _all_gather(rows, sems, 2, gbuf, own, pending)
    y_ref[...] = gbuf[...]
    n = math.prod(row_factors)
    per = y_ref.shape[-2]
    width = g_ref.shape[0]
    gram = None
    for p in range(n * per // width):
        parts = [y_ref[_digits(p * width // per + i, row_factors)] for i in range(width // per)]
        block = jnp.concatenate(parts, axis=0)
        term = lax.dot_general(block, block, (((1,), (1,)), ((), ())), precision=HIGH,
                               preferred_element_type=jnp.float32)
        gram = term if gram is None else gram + term
    g_ref[...] = _sum(cols, sems, 4, gram, cbufs, pending)
    for c in pending:
        c.wait_send()


def product_gram(x, scale, row_factors, col_factors, cid, width):
    n = math.prod(row_factors)
    chunk = x.shape[1:]
    x = x.reshape(tuple(reversed(row_factors)) + chunk)
    scratch = []
    for s in range(len(row_factors)):
        scratch.append(pltpu.VMEM((row_factors[s],) + tuple(reversed(row_factors[s + 1:])) + chunk,
                                  jnp.float32))
    scratch.append(pltpu.VMEM(tuple(reversed(row_factors)) + chunk, jnp.float32))
    for s in range(len(col_factors)):
        scratch.append(pltpu.VMEM((col_factors[s], width, width), jnp.float32))
    scratch.append(pltpu.SemaphoreType.DMA((6, max(len(row_factors), len(col_factors)),
                                            max(row_factors + col_factors))))
    nbytes = n * math.prod(chunk) * 4
    y, g = pl.pallas_call(
        functools.partial(_product_gram_kernel, row_factors=tuple(row_factors),
                          col_factors=tuple(col_factors)),
        out_shape=(jax.ShapeDtypeStruct(tuple(reversed(row_factors)) + chunk, jnp.float32),
                   jax.ShapeDtypeStruct((width, width), jnp.float32)),
        in_specs=[pl.BlockSpec(memory_space=pltpu.VMEM)] * 2,
        out_specs=(pl.BlockSpec(memory_space=pltpu.VMEM), pl.BlockSpec(memory_space=pltpu.VMEM)),
        scratch_shapes=scratch,
        compiler_params=pltpu.CompilerParams(collective_id=cid, has_side_effects=True),
        cost_estimate=pl.CostEstimate(flops=0, transcendentals=0, bytes_accessed=2 * nbytes),
    )(x, scale)
    return y.reshape((n,) + chunk), g


def staged(x, axis, factors, mode, cid, scale=None, epilogue=None, out_dtype=None, tiled=None):
    n = math.prod(factors)
    stages = len(factors)
    out_dtype = out_dtype or x.dtype
    if mode == "reduce":
        chunk = x.shape[1:]
        x = x.reshape(tuple(reversed(factors)) + chunk)
    else:
        chunk = x.shape
    scratch = []
    if mode in ("reduce", "sum"):
        for s in range(stages):
            rest = tuple(reversed(factors[s + 1:])) if mode == "reduce" else ()
            scratch.append(pltpu.VMEM((factors[s],) + rest + chunk, jnp.float32))
    if mode != "sum":
        scratch.append(pltpu.VMEM(tuple(reversed(factors)) + chunk, out_dtype))
    scratch.append(pltpu.SemaphoreType.DMA((4, stages, max(factors))))
    if mode == "sum":
        out_shape = chunk
    elif tiled is not None:
        out_shape = tiled
    else:
        out_shape = tuple(reversed(factors)) + chunk
    args = (x,) if scale is None else (x, scale)
    nbytes = n * math.prod(chunk) * 4
    y = pl.pallas_call(
        functools.partial(_staged_kernel, axis=axis, factors=tuple(factors), mode=mode,
                          has_scale=scale is not None, epilogue=epilogue),
        out_shape=jax.ShapeDtypeStruct(out_shape, out_dtype),
        in_specs=[pl.BlockSpec(memory_space=pltpu.VMEM)] * len(args),
        out_specs=pl.BlockSpec(memory_space=pltpu.VMEM),
        scratch_shapes=scratch,
        compiler_params=pltpu.CompilerParams(collective_id=cid, has_side_effects=True),
        cost_estimate=pl.CostEstimate(flops=0, transcendentals=0, bytes_accessed=2 * nbytes),
    )(*args)
    if mode == "sum" or tiled is not None:
        return y
    return y.reshape((n,) + chunk)


QUERY_FACTORS = (2, 4, 4)
GRAM_FACTORS = (4, 8)
ROW_FACTORS = (4, 4)


def _query_epilogue(total, s_ref):
    return (total * s_ref[...]).astype(jnp.bfloat16)


def _product_epilogue(total, s_ref):
    return total * s_ref[...]


GROUP = 8


def _products_kernel(ids_ref, count_ref, src_ref, tiles_hbm, out_ref, tiles, sems, *, forward):
    slots = tiles.shape[0]
    groups = slots // GROUP

    def fetch(g):
        return pltpu.make_async_copy(
            tiles_hbm.at[pl.ds(g * GROUP, GROUP)], tiles.at[pl.ds(g * GROUP, GROUP)], sems.at[g]
        )

    for g in range(groups):
        fetch(g).start()
    out_ref[...] = jnp.zeros_like(out_ref)
    src_row, dst_row = (1, 0) if forward else (0, 1)
    count = count_ref[0]
    for g in range(groups):
        fetch(g).wait()
        ys = []
        for k in range(g * GROUP, (g + 1) * GROUP):
            x = src_ref[ids_ref[src_row, k]]
            t = tiles[k]
            if forward:
                y = lax.dot_general(x, t, (((1,), (1,)), ((), ())),
                                    preferred_element_type=jnp.float32)
            else:
                y = jnp.dot(x, t, preferred_element_type=jnp.float32)
            ys.append(jnp.where(k < count, y, 0.0))
        for k, y in zip(range(g * GROUP, (g + 1) * GROUP), ys):
            d = ids_ref[dst_row, k]
            out_ref[d] = out_ref[d] + y


def tile_products(slot_ids, live_count, src, tile_set, blocks, forward):
    slots, side, _ = tile_set.shape
    width = src.shape[1]
    return pl.pallas_call(
        functools.partial(_products_kernel, forward=forward),
        out_shape=jax.ShapeDtypeStruct((blocks, width, side), jnp.float32),
        in_specs=[
            pl.BlockSpec(memory_space=pltpu.SMEM),
            pl.BlockSpec(memory_space=pltpu.SMEM),
            pl.BlockSpec(memory_space=pltpu.VMEM),
            pl.BlockSpec(memory_space=pl.ANY),
        ],
        out_specs=pl.BlockSpec(memory_space=pltpu.VMEM),
        scratch_shapes=[
            pltpu.VMEM(tile_set.shape, tile_set.dtype),
            pltpu.SemaphoreType.DMA((slots // GROUP,)),
        ],
        cost_estimate=pl.CostEstimate(
            flops=2 * slots * width * side * side, transcendentals=0,
            bytes_accessed=slots * side * side * 2 + src.size * 2 + blocks * width * side * 4,
        ),
    )(slot_ids, live_count.reshape(1), src, tile_set)


def lower_inverse(gram):
    lower = lax.linalg.cholesky(gram, symmetrize_input=False)
    eye = jnp.eye(gram.shape[0], dtype=gram.dtype)
    return lax.linalg.triangular_solve(lower, eye, left_side=True, lower=True)


def shards(tiles, tile_ids, tile_count, query_degree, product_degree, panel):
    tile_set = tiles[0, 0]
    slot_ids = tile_ids[0, 0]
    live_count = tile_count[0, 0]
    side = tile_set.shape[1]
    width = panel.shape[0]
    query_tiles = query_degree.shape[0] // side
    product_tiles = product_degree.shape[0] // side
    n_row = lax.axis_size("row")
    n_col = lax.axis_size("col")
    qscale = (1.0 / jnp.sqrt(query_degree.astype(jnp.float32))).reshape(query_tiles, 1, side)
    pscale = (1.0 / jnp.sqrt(product_degree.astype(jnp.float32))).reshape(product_tiles, 1, side)
    row_at = lax.axis_index("row")
    col_at = lax.axis_index("col")
    share = panel.shape[1]
    block = product_degree.shape[0]
    q_per_tile = n_col // query_tiles
    p_per_tile = n_row // product_tiles
    my_qscale = lax.dynamic_index_in_dim(qscale, col_at // q_per_tile, keepdims=False)
    my_pscale = lax.dynamic_index_in_dim(pscale, row_at // p_per_tile, keepdims=False)
    root_count = math.sqrt(product_degree.shape[0] * n_col)

    panel_pscale = lax.dynamic_slice_in_dim(pscale.reshape(block), row_at * share, share)
    scaled0 = (panel * panel_pscale[None, :]).astype(jnp.bfloat16)
    scaled_tiles = staged(scaled0, "row", ROW_FACTORS, "gather", 0,
                          tiled=(product_tiles, width, side))
    per_tile = side // share
    for iteration in range(ITERS):
        if iteration:
            current_tiles = jnp.einsum("rs,psi->pri", inverse, lifted_tiles, precision=HIGH)
            scaled_tiles = (current_tiles * pscale).astype(jnp.bfloat16)
        partial_sum = tile_products(slot_ids, live_count, scaled_tiles, tile_set, query_tiles, True)
        query_tiles_panel = staged(
            partial_sum.reshape(n_col, width // q_per_tile, side), "col", QUERY_FACTORS, "reduce", 1,
            scale=my_qscale, epilogue=_query_epilogue, out_dtype=jnp.bfloat16,
        ).reshape(query_tiles, width, side)
        product_partial = tile_products(
            slot_ids, live_count, query_tiles_panel, tile_set, product_tiles, False
        )
        lifted_pieces, gram = product_gram(
            product_partial.reshape(n_row, width // p_per_tile, side), my_pscale, ROW_FACTORS,
            GRAM_FACTORS, 2, width,
        )
        lifted_tiles = lifted_pieces.reshape(product_tiles, width, side)
        inverse = lower_inverse(gram)
    my_tile = lax.dynamic_index_in_dim(lifted_tiles, row_at // per_tile, keepdims=False)
    my_lifted = lax.dynamic_slice_in_dim(my_tile, (row_at % per_tile) * share, share, axis=1)
    return jnp.einsum("rs,si->ri", inverse, my_lifted, precision=HIGH) * root_count


def solution(mesh):
    in_specs = (
        P("row", "col", None, None, None),
        P("row", "col", None, None),
        P("row", "col"),
        P("row"),
        P("col"),
        P(None, ("col", "row")),
    )
    out_specs = P(None, ("col", "row"))
    return jax.shard_map(shards, mesh=mesh, in_specs=in_specs, out_specs=out_specs, check_vma=False)
```

```python
import functools
import math

import jax
import jax.numpy as jnp
from jax import lax
from jax.experimental import pallas as pl
from jax.experimental.pallas import tpu as pltpu
from jax.sharding import PartitionSpec as P

ITERS = 2


HIGH = lax.Precision.HIGHEST

AXES = ("row", "col")


def _device(axis, peer):
    if axis == "row":
        return (peer, lax.axis_index("col"))
    return (lax.axis_index("row"), peer)


class _Plan:
    def __init__(self, axis, factors):
        self.axis = axis
        self.factors = tuple(factors)
        self.stages = len(factors)
        self.me = lax.axis_index(axis)
        self.strides = [math.prod(factors[:s]) for s in range(self.stages)]
        self.mine = [lax.rem(lax.div(self.me, self.strides[s]), factors[s])
                     for s in range(self.stages)]

    def peer(self, s, d):
        return _device(self.axis, self.me + (d - self.mine[s]) * self.strides[s])

    def other(self, s, k):
        return lax.rem(self.mine[s] + k, self.factors[s])

    def peers(self):
        return [self.peer(s, self.other(s, k)) for s in range(self.stages)
                for k in range(1, self.factors[s])]


def _barrier(plans):
    barrier = pltpu.get_barrier_semaphore()
    count = 0
    for plan in plans:
        for dev in plan.peers():
            pl.semaphore_signal(barrier, inc=1, device_id=dev, device_id_type=pl.DeviceIdType.MESH)
            count += 1
    pl.semaphore_wait(barrier, count)


def _exchange(plan, sems, kind, s, src_of, dst_of, pending):
    copies = []
    mine = plan.mine[s]
    for k in range(1, plan.factors[s]):
        d = plan.other(s, k)
        c = pltpu.make_async_remote_copy(
            src_ref=src_of(d), dst_ref=dst_of(mine),
            send_sem=sems.at[kind, s, d], recv_sem=sems.at[kind + 1, s, mine],
            device_id=plan.peer(s, d), device_id_type=pl.DeviceIdType.MESH,
        )
        c.start()
        copies.append((d, c))
    pending.extend(c for _, c in copies)
    for d, c in copies:
        pltpu.make_async_remote_copy(
            src_ref=src_of(d), dst_ref=dst_of(d),
            send_sem=sems.at[kind, s, d], recv_sem=sems.at[kind + 1, s, d],
            device_id=plan.peer(s, d), device_id_type=pl.DeviceIdType.MESH,
        ).wait_recv()


def _reduce_scatter(plan, sems, kind, x_ref, rbufs, pending):
    cur = x_ref
    for s in range(plan.stages):
        lead = plan.stages - 1 - s

        def src_of(d, cur=cur, lead=lead):
            return cur.at[(slice(None),) * lead + (d,)]

        rb = rbufs[s]
        _exchange(plan, sems, kind, s, src_of, lambda d, rb=rb: rb.at[d], pending)
        total = cur[(slice(None),) * lead + (plan.mine[s],)]
        for k in range(1, plan.factors[s]):
            total = total + rb[plan.other(s, k)]
        rb[plan.mine[s]] = total
        cur = rb.at[plan.mine[s]]
    return cur


def _all_gather(plan, sems, kind, gbuf, own, pending):
    mine = plan.mine
    gbuf[tuple(mine[::-1])] = own.astype(gbuf.dtype)
    for s in reversed(range(plan.stages)):
        lead = plan.stages - 1 - s

        def view(d, s=s, lead=lead):
            return gbuf.at[(slice(None),) * lead + (d,) + tuple(mine[s - 1::-1] if s else ())]

        _exchange(plan, sems, kind, s, lambda d, s=s: view(mine[s]), view, pending)


def _sum(plan, sems, kind, value, rbufs, pending):
    for s in range(plan.stages):
        rb = rbufs[s]
        rb[plan.mine[s]] = value
        src = rb.at[plan.mine[s]]
        _exchange(plan, sems, kind, s, lambda d, src=src: src, lambda d, rb=rb: rb.at[d], pending)
        value = rb[0]
        for d in range(1, plan.factors[s]):
            value = value + rb[d]
    return value


def _staged_kernel(*refs, axis, factors, mode, has_scale, epilogue):
    if has_scale:
        x_ref, s_ref, y_ref = refs[:3]
        rest = refs[3:]
    else:
        x_ref, y_ref = refs[:2]
        s_ref = None
        rest = refs[2:]
    plan = _Plan(axis, factors)
    n_rs = plan.stages if mode in ("reduce", "sum") else 0
    rbufs = rest[:n_rs]
    gbuf = rest[n_rs] if mode != "sum" else None
    sems = rest[-1]
    _barrier([plan])
    pending = []
    if mode == "sum":
        y_ref[...] = _sum(plan, sems, 0, x_ref[...], rbufs, pending)
    else:
        if mode == "reduce":
            own = epilogue(_reduce_scatter(plan, sems, 0, x_ref, rbufs, pending)[...], s_ref)
        else:
            own = x_ref[...]
        _all_gather(plan, sems, 2, gbuf, own, pending)
        if mode == "gather" and len(y_ref.shape) == 3:
            n = math.prod(factors)
            share = own.shape[-1]
            per = y_ref.shape[-1] // share
            for j in range(n):
                y_ref[j // per, :, pl.ds((j % per) * share, share)] = gbuf[_digits(j, factors)]
        else:
            y_ref[...] = gbuf[...]
    for c in pending:
        c.wait_send()


def _digits(j, factors):
    return tuple((j // math.prod(factors[:s])) % factors[s] for s in reversed(range(len(factors))))


def _product_gram_kernel(x_ref, s_ref, y_ref, g_ref, *rest, row_factors, col_factors):
    rows = _Plan("row", row_factors)
    cols = _Plan("col", col_factors)
    rbufs = rest[:rows.stages]
    gbuf = rest[rows.stages]
    cbufs = rest[rows.stages + 1:rows.stages + 1 + cols.stages]
    sems = rest[-1]
    _barrier([rows, cols])
    pending = []
    own = _reduce_scatter(rows, sems, 0, x_ref, rbufs, pending)[...] * s_ref[...]
    _all_gather(rows, sems, 2, gbuf, own, pending)
    y_ref[...] = gbuf[...]
    n = math.prod(row_factors)
    per = y_ref.shape[-2]
    width = g_ref.shape[0]
    gram = None
    for p in range(n * per // width):
        parts = [y_ref[_digits(p * width // per + i, row_factors)] for i in range(width // per)]
        block = jnp.concatenate(parts, axis=0)
        term = lax.dot_general(block, block, (((1,), (1,)), ((), ())), precision=HIGH,
                               preferred_element_type=jnp.float32)
        gram = term if gram is None else gram + term
    g_ref[...] = _sum(cols, sems, 4, gram, cbufs, pending)
    for c in pending:
        c.wait_send()


def product_gram(x, scale, row_factors, col_factors, cid, width):
    n = math.prod(row_factors)
    chunk = x.shape[1:]
    x = x.reshape(tuple(reversed(row_factors)) + chunk)
    scratch = []
    for s in range(len(row_factors)):
        scratch.append(pltpu.VMEM((row_factors[s],) + tuple(reversed(row_factors[s + 1:])) + chunk,
                                  jnp.float32))
    scratch.append(pltpu.VMEM(tuple(reversed(row_factors)) + chunk, jnp.float32))
    for s in range(len(col_factors)):
        scratch.append(pltpu.VMEM((col_factors[s], width, width), jnp.float32))
    scratch.append(pltpu.SemaphoreType.DMA((6, max(len(row_factors), len(col_factors)),
                                            max(row_factors + col_factors))))
    nbytes = n * math.prod(chunk) * 4
    y, g = pl.pallas_call(
        functools.partial(_product_gram_kernel, row_factors=tuple(row_factors),
                          col_factors=tuple(col_factors)),
        out_shape=(jax.ShapeDtypeStruct(tuple(reversed(row_factors)) + chunk, jnp.float32),
                   jax.ShapeDtypeStruct((width, width), jnp.float32)),
        in_specs=[pl.BlockSpec(memory_space=pltpu.VMEM)] * 2,
        out_specs=(pl.BlockSpec(memory_space=pltpu.VMEM), pl.BlockSpec(memory_space=pltpu.VMEM)),
        scratch_shapes=scratch,
        compiler_params=pltpu.CompilerParams(collective_id=cid, has_side_effects=True),
        cost_estimate=pl.CostEstimate(flops=0, transcendentals=0, bytes_accessed=2 * nbytes),
    )(x, scale)
    return y.reshape((n,) + chunk), g


def staged(x, axis, factors, mode, cid, scale=None, epilogue=None, out_dtype=None, tiled=None):
    n = math.prod(factors)
    stages = len(factors)
    out_dtype = out_dtype or x.dtype
    if mode == "reduce":
        chunk = x.shape[1:]
        x = x.reshape(tuple(reversed(factors)) + chunk)
    else:
        chunk = x.shape
    scratch = []
    if mode in ("reduce", "sum"):
        for s in range(stages):
            rest = tuple(reversed(factors[s + 1:])) if mode == "reduce" else ()
            scratch.append(pltpu.VMEM((factors[s],) + rest + chunk, jnp.float32))
    if mode != "sum":
        scratch.append(pltpu.VMEM(tuple(reversed(factors)) + chunk, out_dtype))
    scratch.append(pltpu.SemaphoreType.DMA((4, stages, max(factors))))
    if mode == "sum":
        out_shape = chunk
    elif tiled is not None:
        out_shape = tiled
    else:
        out_shape = tuple(reversed(factors)) + chunk
    args = (x,) if scale is None else (x, scale)
    nbytes = n * math.prod(chunk) * 4
    y = pl.pallas_call(
        functools.partial(_staged_kernel, axis=axis, factors=tuple(factors), mode=mode,
                          has_scale=scale is not None, epilogue=epilogue),
        out_shape=jax.ShapeDtypeStruct(out_shape, out_dtype),
        in_specs=[pl.BlockSpec(memory_space=pltpu.VMEM)] * len(args),
        out_specs=pl.BlockSpec(memory_space=pltpu.VMEM),
        scratch_shapes=scratch,
        compiler_params=pltpu.CompilerParams(collective_id=cid, has_side_effects=True),
        cost_estimate=pl.CostEstimate(flops=0, transcendentals=0, bytes_accessed=2 * nbytes),
    )(*args)
    if mode == "sum" or tiled is not None:
        return y
    return y.reshape((n,) + chunk)


QUERY_FACTORS = (2, 4, 4)
GRAM_FACTORS = (4, 8)
ROW_FACTORS = (4, 4)


def _query_epilogue(total, s_ref):
    return (total * s_ref[...]).astype(jnp.bfloat16)


def _product_epilogue(total, s_ref):
    return total * s_ref[...]


GROUP = 8


def _products_kernel(ids_ref, count_ref, src_ref, tiles_hbm, out_ref, tiles, sems, *, forward):
    slots = tiles.shape[0]
    groups = slots // GROUP

    def fetch(g):
        return pltpu.make_async_copy(
            tiles_hbm.at[pl.ds(g * GROUP, GROUP)], tiles.at[pl.ds(g * GROUP, GROUP)], sems.at[g]
        )

    for g in range(groups):
        fetch(g).start()
    out_ref[...] = jnp.zeros_like(out_ref)
    src_row, dst_row = (1, 0) if forward else (0, 1)
    count = count_ref[0]
    for g in range(groups):
        fetch(g).wait()
        ys = []
        for k in range(g * GROUP, (g + 1) * GROUP):
            x = src_ref[ids_ref[src_row, k]]
            t = tiles[k]
            if forward:
                y = lax.dot_general(x, t, (((1,), (1,)), ((), ())),
                                    preferred_element_type=jnp.float32)
            else:
                y = jnp.dot(x, t, preferred_element_type=jnp.float32)
            ys.append(jnp.where(k < count, y, 0.0))
        for k, y in zip(range(g * GROUP, (g + 1) * GROUP), ys):
            d = ids_ref[dst_row, k]
            out_ref[d] = out_ref[d] + y


def tile_products(slot_ids, live_count, src, tile_set, blocks, forward):
    slots, side, _ = tile_set.shape
    width = src.shape[1]
    return pl.pallas_call(
        functools.partial(_products_kernel, forward=forward),
        out_shape=jax.ShapeDtypeStruct((blocks, width, side), jnp.float32),
        in_specs=[
            pl.BlockSpec(memory_space=pltpu.SMEM),
            pl.BlockSpec(memory_space=pltpu.SMEM),
            pl.BlockSpec(memory_space=pltpu.VMEM),
            pl.BlockSpec(memory_space=pl.ANY),
        ],
        out_specs=pl.BlockSpec(memory_space=pltpu.VMEM),
        scratch_shapes=[
            pltpu.VMEM(tile_set.shape, tile_set.dtype),
            pltpu.SemaphoreType.DMA((slots // GROUP,)),
        ],
        cost_estimate=pl.CostEstimate(
            flops=2 * slots * width * side * side, transcendentals=0,
            bytes_accessed=slots * side * side * 2 + src.size * 2 + blocks * width * side * 4,
        ),
    )(slot_ids, live_count.reshape(1), src, tile_set)


def _lower_inverse_kernel(m_ref, out_ref):
    rows, cols = m_ref.shape
    row = lax.broadcasted_iota(jnp.int32, (rows, cols), 0)
    lane = lax.broadcasted_iota(jnp.int32, (rows, cols), 1)

    def step(j, m):
        pivot_row = jnp.sum(jnp.where(row == j, m, 0.0), axis=0, keepdims=True)
        pivot = jnp.sum(jnp.where(lane[:1] == j, pivot_row, 0.0), axis=1, keepdims=True)
        root = jnp.sqrt(pivot)
        scaled_row = pivot_row / root
        column = jnp.sum(jnp.where(lane == j, m, 0.0), axis=1, keepdims=True) / root
        return jnp.where(row == j, scaled_row, jnp.where(row > j, m - column * scaled_row, m))

    out_ref[...] = lax.fori_loop(0, rows, step, m_ref[...])


def lower_inverse(gram):
    width = gram.shape[0]
    augmented = jnp.concatenate([gram, jnp.eye(width, dtype=gram.dtype)], axis=1)
    reduced = pl.pallas_call(
        _lower_inverse_kernel,
        out_shape=jax.ShapeDtypeStruct(augmented.shape, augmented.dtype),
        in_specs=[pl.BlockSpec(memory_space=pltpu.VMEM)],
        out_specs=pl.BlockSpec(memory_space=pltpu.VMEM),
    )(augmented)
    return reduced[:, width:]


def lower_inverse_native(gram):
    lower = lax.linalg.cholesky(gram, symmetrize_input=False)
    eye = jnp.eye(gram.shape[0], dtype=gram.dtype)
    return lax.linalg.triangular_solve(lower, eye, left_side=True, lower=True)


def shards(tiles, tile_ids, tile_count, query_degree, product_degree, panel):
    tile_set = tiles[0, 0]
    slot_ids = tile_ids[0, 0]
    live_count = tile_count[0, 0]
    side = tile_set.shape[1]
    width = panel.shape[0]
    query_tiles = query_degree.shape[0] // side
    product_tiles = product_degree.shape[0] // side
    n_row = lax.axis_size("row")
    n_col = lax.axis_size("col")
    qscale = (1.0 / jnp.sqrt(query_degree.astype(jnp.float32))).reshape(query_tiles, 1, side)
    pscale = (1.0 / jnp.sqrt(product_degree.astype(jnp.float32))).reshape(product_tiles, 1, side)
    row_at = lax.axis_index("row")
    col_at = lax.axis_index("col")
    share = panel.shape[1]
    block = product_degree.shape[0]
    q_per_tile = n_col // query_tiles
    p_per_tile = n_row // product_tiles
    my_qscale = lax.dynamic_index_in_dim(qscale, col_at // q_per_tile, keepdims=False)
    my_pscale = lax.dynamic_index_in_dim(pscale, row_at // p_per_tile, keepdims=False)
    root_count = math.sqrt(product_degree.shape[0] * n_col)

    panel_pscale = lax.dynamic_slice_in_dim(pscale.reshape(block), row_at * share, share)
    scaled0 = (panel * panel_pscale[None, :]).astype(jnp.bfloat16)
    scaled_tiles = staged(scaled0, "row", ROW_FACTORS, "gather", 0,
                          tiled=(product_tiles, width, side))
    per_tile = side // share
    for iteration in range(ITERS):
        if iteration:
            current_tiles = jnp.einsum("rs,psi->pri", inverse, lifted_tiles, precision=HIGH)
            scaled_tiles = (current_tiles * pscale).astype(jnp.bfloat16)
        partial_sum = tile_products(slot_ids, live_count, scaled_tiles, tile_set, query_tiles, True)
        query_tiles_panel = staged(
            partial_sum.reshape(n_col, width // q_per_tile, side), "col", QUERY_FACTORS, "reduce", 1,
            scale=my_qscale, epilogue=_query_epilogue, out_dtype=jnp.bfloat16,
        ).reshape(query_tiles, width, side)
        product_partial = tile_products(
            slot_ids, live_count, query_tiles_panel, tile_set, product_tiles, False
        )
        lifted_pieces, gram = product_gram(
            product_partial.reshape(n_row, width // p_per_tile, side), my_pscale, ROW_FACTORS,
            GRAM_FACTORS, 2, width,
        )
        lifted_tiles = lifted_pieces.reshape(product_tiles, width, side)
        inverse = lower_inverse(gram)
    my_tile = lax.dynamic_index_in_dim(lifted_tiles, row_at // per_tile, keepdims=False)
    my_lifted = lax.dynamic_slice_in_dim(my_tile, (row_at % per_tile) * share, share, axis=1)
    return jnp.einsum("rs,si->ri", inverse, my_lifted, precision=HIGH) * root_count


def solution(mesh):
    in_specs = (
        P("row", "col", None, None, None),
        P("row", "col", None, None),
        P("row", "col"),
        P("row"),
        P("col"),
        P(None, ("col", "row")),
    )
    out_specs = P(None, ("col", "row"))
    return jax.shard_map(shards, mesh=mesh, in_specs=in_specs, out_specs=out_specs, check_vma=False)
```

```python
import functools
import math

import jax
import jax.numpy as jnp
from jax import lax
from jax.experimental import pallas as pl
from jax.experimental.pallas import tpu as pltpu
from jax.sharding import PartitionSpec as P

ITERS = 2


HIGH = lax.Precision.HIGHEST

AXES = ("row", "col")


def _device(axis, peer):
    if axis == "row":
        return (peer, lax.axis_index("col"))
    return (lax.axis_index("row"), peer)


class _Plan:
    def __init__(self, axis, factors):
        self.axis = axis
        self.factors = tuple(factors)
        self.stages = len(factors)
        self.me = lax.axis_index(axis)
        self.strides = [math.prod(factors[:s]) for s in range(self.stages)]
        self.mine = [lax.rem(lax.div(self.me, self.strides[s]), factors[s])
                     for s in range(self.stages)]

    def peer(self, s, d):
        return _device(self.axis, self.me + (d - self.mine[s]) * self.strides[s])

    def other(self, s, k):
        return lax.rem(self.mine[s] + k, self.factors[s])

    def peers(self):
        return [self.peer(s, self.other(s, k)) for s in range(self.stages)
                for k in range(1, self.factors[s])]


def _barrier(plans):
    barrier = pltpu.get_barrier_semaphore()
    count = 0
    for plan in plans:
        for dev in plan.peers():
            pl.semaphore_signal(barrier, inc=1, device_id=dev, device_id_type=pl.DeviceIdType.MESH)
            count += 1
    pl.semaphore_wait(barrier, count)


def _exchange(plan, sems, kind, s, src_of, dst_of, pending):
    copies = []
    mine = plan.mine[s]
    for k in range(1, plan.factors[s]):
        d = plan.other(s, k)
        c = pltpu.make_async_remote_copy(
            src_ref=src_of(d), dst_ref=dst_of(mine),
            send_sem=sems.at[kind, s, d], recv_sem=sems.at[kind + 1, s, mine],
            device_id=plan.peer(s, d), device_id_type=pl.DeviceIdType.MESH,
        )
        c.start()
        copies.append((d, c))
    pending.extend(c for _, c in copies)
    for d, c in copies:
        pltpu.make_async_remote_copy(
            src_ref=src_of(d), dst_ref=dst_of(d),
            send_sem=sems.at[kind, s, d], recv_sem=sems.at[kind + 1, s, d],
            device_id=plan.peer(s, d), device_id_type=pl.DeviceIdType.MESH,
        ).wait_recv()


def _reduce_scatter(plan, sems, kind, x_ref, rbufs, pending):
    cur = x_ref
    for s in range(plan.stages):
        lead = plan.stages - 1 - s

        def src_of(d, cur=cur, lead=lead):
            return cur.at[(slice(None),) * lead + (d,)]

        rb = rbufs[s]
        _exchange(plan, sems, kind, s, src_of, lambda d, rb=rb: rb.at[d], pending)
        total = cur[(slice(None),) * lead + (plan.mine[s],)]
        for k in range(1, plan.factors[s]):
            total = total + rb[plan.other(s, k)]
        rb[plan.mine[s]] = total
        cur = rb.at[plan.mine[s]]
    return cur


def _all_gather(plan, sems, kind, gbuf, own, pending):
    mine = plan.mine
    gbuf[tuple(mine[::-1])] = own.astype(gbuf.dtype)
    for s in reversed(range(plan.stages)):
        lead = plan.stages - 1 - s

        def view(d, s=s, lead=lead):
            return gbuf.at[(slice(None),) * lead + (d,) + tuple(mine[s - 1::-1] if s else ())]

        _exchange(plan, sems, kind, s, lambda d, s=s: view(mine[s]), view, pending)


def _sum(plan, sems, kind, value, rbufs, pending):
    for s in range(plan.stages):
        rb = rbufs[s]
        rb[plan.mine[s]] = value
        src = rb.at[plan.mine[s]]
        _exchange(plan, sems, kind, s, lambda d, src=src: src, lambda d, rb=rb: rb.at[d], pending)
        value = rb[0]
        for d in range(1, plan.factors[s]):
            value = value + rb[d]
    return value


def _staged_kernel(*refs, axis, factors, mode, has_scale, epilogue):
    if has_scale:
        x_ref, s_ref, y_ref = refs[:3]
        rest = refs[3:]
    else:
        x_ref, y_ref = refs[:2]
        s_ref = None
        rest = refs[2:]
    plan = _Plan(axis, factors)
    n_rs = plan.stages if mode in ("reduce", "sum") else 0
    rbufs = rest[:n_rs]
    gbuf = rest[n_rs] if mode != "sum" else None
    sems = rest[-1]
    _barrier([plan])
    pending = []
    if mode == "sum":
        y_ref[...] = _sum(plan, sems, 0, x_ref[...], rbufs, pending)
    else:
        if mode == "reduce":
            own = epilogue(_reduce_scatter(plan, sems, 0, x_ref, rbufs, pending)[...], s_ref)
        else:
            own = x_ref[...]
        _all_gather(plan, sems, 2, gbuf, own, pending)
        if mode == "gather" and len(y_ref.shape) == 3:
            n = math.prod(factors)
            share = own.shape[-1]
            per = y_ref.shape[-1] // share
            for j in range(n):
                y_ref[j // per, :, pl.ds((j % per) * share, share)] = gbuf[_digits(j, factors)]
        else:
            y_ref[...] = gbuf[...]
    for c in pending:
        c.wait_send()


def _digits(j, factors):
    return tuple((j // math.prod(factors[:s])) % factors[s] for s in reversed(range(len(factors))))


def _product_gram_kernel(x_ref, s_ref, y_ref, g_ref, *rest, row_factors, col_factors):
    rows = _Plan("row", row_factors)
    cols = _Plan("col", col_factors)
    rbufs = rest[:rows.stages]
    gbuf = rest[rows.stages]
    cbufs = rest[rows.stages + 1:rows.stages + 1 + cols.stages]
    sems = rest[-1]
    _barrier([rows, cols])
    pending = []
    own = _reduce_scatter(rows, sems, 0, x_ref, rbufs, pending)[...] * s_ref[...]
    _all_gather(rows, sems, 2, gbuf, own, pending)
    y_ref[...] = gbuf[...]
    n = math.prod(row_factors)
    per = y_ref.shape[-2]
    width = g_ref.shape[0]
    gram = None
    for p in range(n * per // width):
        parts = [y_ref[_digits(p * width // per + i, row_factors)] for i in range(width // per)]
        block = jnp.concatenate(parts, axis=0)
        padded = jnp.concatenate([block, jnp.zeros_like(block)], axis=0)
        term = lax.dot_general(block, padded, (((1,), (1,)), ((), ())), precision=HIGH,
                               preferred_element_type=jnp.float32)
        gram = term if gram is None else gram + term
    total = _sum(cols, sems, 4, gram, cbufs, pending)
    row = lax.broadcasted_iota(jnp.int32, total.shape, 0)
    lane = lax.broadcasted_iota(jnp.int32, total.shape, 1)
    g_ref[...] = _eliminate(total + jnp.where(lane == row + width, 1.0, 0.0))
    for c in pending:
        c.wait_send()


def product_gram(x, scale, row_factors, col_factors, cid, width):
    n = math.prod(row_factors)
    chunk = x.shape[1:]
    x = x.reshape(tuple(reversed(row_factors)) + chunk)
    scratch = []
    for s in range(len(row_factors)):
        scratch.append(pltpu.VMEM((row_factors[s],) + tuple(reversed(row_factors[s + 1:])) + chunk,
                                  jnp.float32))
    scratch.append(pltpu.VMEM(tuple(reversed(row_factors)) + chunk, jnp.float32))
    for s in range(len(col_factors)):
        scratch.append(pltpu.VMEM((col_factors[s], width, 2 * width), jnp.float32))
    scratch.append(pltpu.SemaphoreType.DMA((6, max(len(row_factors), len(col_factors)),
                                            max(row_factors + col_factors))))
    nbytes = n * math.prod(chunk) * 4
    y, g = pl.pallas_call(
        functools.partial(_product_gram_kernel, row_factors=tuple(row_factors),
                          col_factors=tuple(col_factors)),
        out_shape=(jax.ShapeDtypeStruct(tuple(reversed(row_factors)) + chunk, jnp.float32),
                   jax.ShapeDtypeStruct((width, 2 * width), jnp.float32)),
        in_specs=[pl.BlockSpec(memory_space=pltpu.VMEM)] * 2,
        out_specs=(pl.BlockSpec(memory_space=pltpu.VMEM), pl.BlockSpec(memory_space=pltpu.VMEM)),
        scratch_shapes=scratch,
        compiler_params=pltpu.CompilerParams(collective_id=cid, has_side_effects=True),
        cost_estimate=pl.CostEstimate(flops=0, transcendentals=0, bytes_accessed=2 * nbytes),
    )(x, scale)
    return y.reshape((n,) + chunk), g[:, width:]


def staged(x, axis, factors, mode, cid, scale=None, epilogue=None, out_dtype=None, tiled=None):
    n = math.prod(factors)
    stages = len(factors)
    out_dtype = out_dtype or x.dtype
    if mode == "reduce":
        chunk = x.shape[1:]
        x = x.reshape(tuple(reversed(factors)) + chunk)
    else:
        chunk = x.shape
    scratch = []
    if mode in ("reduce", "sum"):
        for s in range(stages):
            rest = tuple(reversed(factors[s + 1:])) if mode == "reduce" else ()
            scratch.append(pltpu.VMEM((factors[s],) + rest + chunk, jnp.float32))
    if mode != "sum":
        scratch.append(pltpu.VMEM(tuple(reversed(factors)) + chunk, out_dtype))
    scratch.append(pltpu.SemaphoreType.DMA((4, stages, max(factors))))
    if mode == "sum":
        out_shape = chunk
    elif tiled is not None:
        out_shape = tiled
    else:
        out_shape = tuple(reversed(factors)) + chunk
    args = (x,) if scale is None else (x, scale)
    nbytes = n * math.prod(chunk) * 4
    y = pl.pallas_call(
        functools.partial(_staged_kernel, axis=axis, factors=tuple(factors), mode=mode,
                          has_scale=scale is not None, epilogue=epilogue),
        out_shape=jax.ShapeDtypeStruct(out_shape, out_dtype),
        in_specs=[pl.BlockSpec(memory_space=pltpu.VMEM)] * len(args),
        out_specs=pl.BlockSpec(memory_space=pltpu.VMEM),
        scratch_shapes=scratch,
        compiler_params=pltpu.CompilerParams(collective_id=cid, has_side_effects=True),
        cost_estimate=pl.CostEstimate(flops=0, transcendentals=0, bytes_accessed=2 * nbytes),
    )(*args)
    if mode == "sum" or tiled is not None:
        return y
    return y.reshape((n,) + chunk)


QUERY_FACTORS = (2, 4, 4)
GRAM_FACTORS = (4, 8)
ROW_FACTORS = (4, 4)


def _query_epilogue(total, s_ref):
    return (total * s_ref[...]).astype(jnp.bfloat16)


def _product_epilogue(total, s_ref):
    return total * s_ref[...]


GROUP = 8


def _products_kernel(ids_ref, count_ref, src_ref, tiles_hbm, out_ref, tiles, sems, *, forward):
    slots = tiles.shape[0]
    groups = slots // GROUP

    def fetch(g):
        return pltpu.make_async_copy(
            tiles_hbm.at[pl.ds(g * GROUP, GROUP)], tiles.at[pl.ds(g * GROUP, GROUP)], sems.at[g]
        )

    for g in range(groups):
        fetch(g).start()
    out_ref[...] = jnp.zeros_like(out_ref)
    src_row, dst_row = (1, 0) if forward else (0, 1)
    count = count_ref[0]
    for g in range(groups):
        fetch(g).wait()
        ys = []
        for k in range(g * GROUP, (g + 1) * GROUP):
            x = src_ref[ids_ref[src_row, k]]
            t = tiles[k]
            if forward:
                y = lax.dot_general(x, t, (((1,), (1,)), ((), ())),
                                    preferred_element_type=jnp.float32)
            else:
                y = jnp.dot(x, t, preferred_element_type=jnp.float32)
            ys.append(jnp.where(k < count, y, 0.0))
        for k, y in zip(range(g * GROUP, (g + 1) * GROUP), ys):
            d = ids_ref[dst_row, k]
            out_ref[d] = out_ref[d] + y


def tile_products(slot_ids, live_count, src, tile_set, blocks, forward):
    slots, side, _ = tile_set.shape
    width = src.shape[1]
    return pl.pallas_call(
        functools.partial(_products_kernel, forward=forward),
        out_shape=jax.ShapeDtypeStruct((blocks, width, side), jnp.float32),
        in_specs=[
            pl.BlockSpec(memory_space=pltpu.SMEM),
            pl.BlockSpec(memory_space=pltpu.SMEM),
            pl.BlockSpec(memory_space=pltpu.VMEM),
            pl.BlockSpec(memory_space=pl.ANY),
        ],
        out_specs=pl.BlockSpec(memory_space=pltpu.VMEM),
        scratch_shapes=[
            pltpu.VMEM(tile_set.shape, tile_set.dtype),
            pltpu.SemaphoreType.DMA((slots // GROUP,)),
        ],
        cost_estimate=pl.CostEstimate(
            flops=2 * slots * width * side * side, transcendentals=0,
            bytes_accessed=slots * side * side * 2 + src.size * 2 + blocks * width * side * 4,
        ),
    )(slot_ids, live_count.reshape(1), src, tile_set)


def _eliminate(m):
    rows, cols = m.shape
    row = lax.broadcasted_iota(jnp.int32, (rows, cols), 0)
    lane = lax.broadcasted_iota(jnp.int32, (rows, cols), 1)

    def step(j, m):
        pivot_row = jnp.sum(jnp.where(row == j, m, 0.0), axis=0, keepdims=True)
        pivot = jnp.sum(jnp.where(lane[:1] == j, pivot_row, 0.0), axis=1, keepdims=True)
        inv_root = 1.0 / jnp.sqrt(pivot)
        scaled_row = pivot_row * inv_root
        column = jnp.sum(jnp.where(lane == j, m, 0.0), axis=1, keepdims=True) * inv_root
        return jnp.where(row == j, scaled_row, jnp.where(row > j, m - column * scaled_row, m))

    return lax.fori_loop(0, rows, step, m, unroll=2)


def _lower_inverse_kernel(m_ref, out_ref):
    out_ref[...] = _eliminate(m_ref[...])


def lower_inverse(gram):
    width = gram.shape[0]
    augmented = jnp.concatenate([gram, jnp.eye(width, dtype=gram.dtype)], axis=1)
    reduced = pl.pallas_call(
        _lower_inverse_kernel,
        out_shape=jax.ShapeDtypeStruct(augmented.shape, augmented.dtype),
        in_specs=[pl.BlockSpec(memory_space=pltpu.VMEM)],
        out_specs=pl.BlockSpec(memory_space=pltpu.VMEM),
    )(augmented)
    return reduced[:, width:]


def lower_inverse_native(gram):
    lower = lax.linalg.cholesky(gram, symmetrize_input=False)
    eye = jnp.eye(gram.shape[0], dtype=gram.dtype)
    return lax.linalg.triangular_solve(lower, eye, left_side=True, lower=True)


def shards(tiles, tile_ids, tile_count, query_degree, product_degree, panel):
    tile_set = tiles[0, 0]
    slot_ids = tile_ids[0, 0]
    live_count = tile_count[0, 0]
    side = tile_set.shape[1]
    width = panel.shape[0]
    query_tiles = query_degree.shape[0] // side
    product_tiles = product_degree.shape[0] // side
    n_row = lax.axis_size("row")
    n_col = lax.axis_size("col")
    qscale = (1.0 / jnp.sqrt(query_degree.astype(jnp.float32))).reshape(query_tiles, 1, side)
    pscale = (1.0 / jnp.sqrt(product_degree.astype(jnp.float32))).reshape(product_tiles, 1, side)
    row_at = lax.axis_index("row")
    col_at = lax.axis_index("col")
    share = panel.shape[1]
    block = product_degree.shape[0]
    q_per_tile = n_col // query_tiles
    p_per_tile = n_row // product_tiles
    my_qscale = lax.dynamic_index_in_dim(qscale, col_at // q_per_tile, keepdims=False)
    my_pscale = lax.dynamic_index_in_dim(pscale, row_at // p_per_tile, keepdims=False)
    root_count = math.sqrt(product_degree.shape[0] * n_col)

    panel_pscale = lax.dynamic_slice_in_dim(pscale.reshape(block), row_at * share, share)
    scaled0 = (panel * panel_pscale[None, :]).astype(jnp.bfloat16)
    scaled_tiles = staged(scaled0, "row", ROW_FACTORS, "gather", 0,
                          tiled=(product_tiles, width, side))
    per_tile = side // share
    for iteration in range(ITERS):
        if iteration:
            current_tiles = jnp.einsum("rs,psi->pri", inverse, lifted_tiles, precision=HIGH)
            scaled_tiles = (current_tiles * pscale).astype(jnp.bfloat16)
        partial_sum = tile_products(slot_ids, live_count, scaled_tiles, tile_set, query_tiles, True)
        query_tiles_panel = staged(
            partial_sum.reshape(n_col, width // q_per_tile, side), "col", QUERY_FACTORS, "reduce", 1,
            scale=my_qscale, epilogue=_query_epilogue, out_dtype=jnp.bfloat16,
        ).reshape(query_tiles, width, side)
        product_partial = tile_products(
            slot_ids, live_count, query_tiles_panel, tile_set, product_tiles, False
        )
        lifted_pieces, inverse = product_gram(
            product_partial.reshape(n_row, width // p_per_tile, side), my_pscale, ROW_FACTORS,
            GRAM_FACTORS, 2, width,
        )
        lifted_tiles = lifted_pieces.reshape(product_tiles, width, side)
    my_tile = lax.dynamic_index_in_dim(lifted_tiles, row_at // per_tile, keepdims=False)
    my_lifted = lax.dynamic_slice_in_dim(my_tile, (row_at % per_tile) * share, share, axis=1)
    return jnp.einsum("rs,si->ri", inverse, my_lifted, precision=HIGH) * root_count


def solution(mesh):
    in_specs = (
        P("row", "col", None, None, None),
        P("row", "col", None, None),
        P("row", "col"),
        P("row"),
        P("col"),
        P(None, ("col", "row")),
    )
    out_specs = P(None, ("col", "row"))
    return jax.shard_map(shards, mesh=mesh, in_specs=in_specs, out_specs=out_specs, check_vma=False)
```

```python
import functools
import math

import jax
import jax.numpy as jnp
from jax import lax
from jax.experimental import pallas as pl
from jax.experimental.pallas import tpu as pltpu
from jax.sharding import PartitionSpec as P

ITERS = 2


HIGH = lax.Precision.HIGHEST

AXES = ("row", "col")


def _device(axis, peer):
    if axis == "row":
        return (peer, lax.axis_index("col"))
    return (lax.axis_index("row"), peer)


class _Plan:
    def __init__(self, axis, factors):
        self.axis = axis
        self.factors = tuple(factors)
        self.stages = len(factors)
        self.me = lax.axis_index(axis)
        self.strides = [math.prod(factors[:s]) for s in range(self.stages)]
        self.mine = [lax.rem(lax.div(self.me, self.strides[s]), factors[s])
                     for s in range(self.stages)]

    def peer(self, s, d):
        return _device(self.axis, self.me + (d - self.mine[s]) * self.strides[s])

    def other(self, s, k):
        return lax.rem(self.mine[s] + k, self.factors[s])

    def peers(self):
        return [self.peer(s, self.other(s, k)) for s in range(self.stages)
                for k in range(1, self.factors[s])]


def _barrier(plans):
    barrier = pltpu.get_barrier_semaphore()
    count = 0
    for plan in plans:
        for dev in plan.peers():
            pl.semaphore_signal(barrier, inc=1, device_id=dev, device_id_type=pl.DeviceIdType.MESH)
            count += 1
    pl.semaphore_wait(barrier, count)


def _exchange(plan, sems, kind, s, src_of, dst_of, pending):
    copies = []
    mine = plan.mine[s]
    for k in range(1, plan.factors[s]):
        d = plan.other(s, k)
        c = pltpu.make_async_remote_copy(
            src_ref=src_of(d), dst_ref=dst_of(mine),
            send_sem=sems.at[kind, s, d], recv_sem=sems.at[kind + 1, s, mine],
            device_id=plan.peer(s, d), device_id_type=pl.DeviceIdType.MESH,
        )
        c.start()
        copies.append((d, c))
    pending.extend(c for _, c in copies)
    for d, c in copies:
        pltpu.make_async_remote_copy(
            src_ref=src_of(d), dst_ref=dst_of(d),
            send_sem=sems.at[kind, s, d], recv_sem=sems.at[kind + 1, s, d],
            device_id=plan.peer(s, d), device_id_type=pl.DeviceIdType.MESH,
        ).wait_recv()


def _reduce_scatter(plan, sems, kind, x_ref, rbufs, pending):
    cur = x_ref
    for s in range(plan.stages):
        lead = plan.stages - 1 - s

        def src_of(d, cur=cur, lead=lead):
            return cur.at[(slice(None),) * lead + (d,)]

        rb = rbufs[s]
        _exchange(plan, sems, kind, s, src_of, lambda d, rb=rb: rb.at[d], pending)
        total = cur[(slice(None),) * lead + (plan.mine[s],)]
        for k in range(1, plan.factors[s]):
            total = total + rb[plan.other(s, k)]
        rb[plan.mine[s]] = total
        cur = rb.at[plan.mine[s]]
    return cur


def _all_gather(plan, sems, kind, gbuf, own, pending):
    mine = plan.mine
    gbuf[tuple(mine[::-1])] = own.astype(gbuf.dtype)
    for s in reversed(range(plan.stages)):
        lead = plan.stages - 1 - s

        def view(d, s=s, lead=lead):
            return gbuf.at[(slice(None),) * lead + (d,) + tuple(mine[s - 1::-1] if s else ())]

        _exchange(plan, sems, kind, s, lambda d, s=s: view(mine[s]), view, pending)


def _sum(plan, sems, kind, value, rbufs, pending):
    for s in range(plan.stages):
        rb = rbufs[s]
        rb[plan.mine[s]] = value
        src = rb.at[plan.mine[s]]
        _exchange(plan, sems, kind, s, lambda d, src=src: src, lambda d, rb=rb: rb.at[d], pending)
        value = rb[0]
        for d in range(1, plan.factors[s]):
            value = value + rb[d]
    return value


def _staged_kernel(*refs, axis, factors, mode, has_scale, epilogue):
    if has_scale:
        x_ref, s_ref, y_ref = refs[:3]
        rest = refs[3:]
    else:
        x_ref, y_ref = refs[:2]
        s_ref = None
        rest = refs[2:]
    plan = _Plan(axis, factors)
    n_rs = plan.stages if mode in ("reduce", "sum") else 0
    rbufs = rest[:n_rs]
    gbuf = rest[n_rs] if mode != "sum" else None
    sems = rest[-1]
    _barrier([plan])
    pending = []
    if mode == "sum":
        y_ref[...] = _sum(plan, sems, 0, x_ref[...], rbufs, pending)
    else:
        if mode == "reduce":
            own = epilogue(_reduce_scatter(plan, sems, 0, x_ref, rbufs, pending)[...], s_ref)
        else:
            own = x_ref[...]
        _all_gather(plan, sems, 2, gbuf, own, pending)
        if mode == "gather" and len(y_ref.shape) == 3:
            n = math.prod(factors)
            share = own.shape[-1]
            per = y_ref.shape[-1] // share
            for j in range(n):
                y_ref[j // per, :, pl.ds((j % per) * share, share)] = gbuf[_digits(j, factors)]
        else:
            y_ref[...] = gbuf[...]
    for c in pending:
        c.wait_send()


def _digits(j, factors):
    return tuple((j // math.prod(factors[:s])) % factors[s] for s in reversed(range(len(factors))))


def _product_gram_kernel(x_ref, s_ref, y_ref, g_ref, *rest, row_factors, col_factors):
    rows = _Plan("row", row_factors)
    cols = _Plan("col", col_factors)
    rbufs = rest[:rows.stages]
    gbuf = rest[rows.stages]
    cbufs = rest[rows.stages + 1:rows.stages + 1 + cols.stages]
    sems = rest[-1]
    _barrier([rows, cols])
    pending = []
    own = _reduce_scatter(rows, sems, 0, x_ref, rbufs, pending)[...] * s_ref[...]
    _all_gather(rows, sems, 2, gbuf, own, pending)
    y_ref[...] = gbuf[...]
    n = math.prod(row_factors)
    per = y_ref.shape[-2]
    width = g_ref.shape[0]
    gram = None
    for p in range(n * per // width):
        parts = [y_ref[_digits(p * width // per + i, row_factors)] for i in range(width // per)]
        block = jnp.concatenate(parts, axis=0)
        padded = jnp.concatenate([block, jnp.zeros_like(block)], axis=0)
        term = lax.dot_general(block, padded, (((1,), (1,)), ((), ())), precision=HIGH,
                               preferred_element_type=jnp.float32)
        gram = term if gram is None else gram + term
    total = _sum(cols, sems, 4, gram, cbufs, pending)
    row = lax.broadcasted_iota(jnp.int32, total.shape, 0)
    lane = lax.broadcasted_iota(jnp.int32, total.shape, 1)
    g_ref[...] = _eliminate(total + jnp.where(lane == row + width, 1.0, 0.0))
    for c in pending:
        c.wait_send()


def product_gram(x, scale, row_factors, col_factors, cid, width):
    n = math.prod(row_factors)
    chunk = x.shape[1:]
    x = x.reshape(tuple(reversed(row_factors)) + chunk)
    scratch = []
    for s in range(len(row_factors)):
        scratch.append(pltpu.VMEM((row_factors[s],) + tuple(reversed(row_factors[s + 1:])) + chunk,
                                  jnp.float32))
    scratch.append(pltpu.VMEM(tuple(reversed(row_factors)) + chunk, jnp.float32))
    for s in range(len(col_factors)):
        scratch.append(pltpu.VMEM((col_factors[s], width, 2 * width), jnp.float32))
    scratch.append(pltpu.SemaphoreType.DMA((6, max(len(row_factors), len(col_factors)),
                                            max(row_factors + col_factors))))
    nbytes = n * math.prod(chunk) * 4
    y, g = pl.pallas_call(
        functools.partial(_product_gram_kernel, row_factors=tuple(row_factors),
                          col_factors=tuple(col_factors)),
        out_shape=(jax.ShapeDtypeStruct(tuple(reversed(row_factors)) + chunk, jnp.float32),
                   jax.ShapeDtypeStruct((width, 2 * width), jnp.float32)),
        in_specs=[pl.BlockSpec(memory_space=pltpu.VMEM)] * 2,
        out_specs=(pl.BlockSpec(memory_space=pltpu.VMEM), pl.BlockSpec(memory_space=pltpu.VMEM)),
        scratch_shapes=scratch,
        compiler_params=pltpu.CompilerParams(collective_id=cid, has_side_effects=True),
        cost_estimate=pl.CostEstimate(flops=0, transcendentals=0, bytes_accessed=2 * nbytes),
    )(x, scale)
    return y.reshape((n,) + chunk), g[:, width:]


def staged(x, axis, factors, mode, cid, scale=None, epilogue=None, out_dtype=None, tiled=None):
    n = math.prod(factors)
    stages = len(factors)
    out_dtype = out_dtype or x.dtype
    if mode == "reduce":
        chunk = x.shape[1:]
        x = x.reshape(tuple(reversed(factors)) + chunk)
    else:
        chunk = x.shape
    scratch = []
    if mode in ("reduce", "sum"):
        for s in range(stages):
            rest = tuple(reversed(factors[s + 1:])) if mode == "reduce" else ()
            scratch.append(pltpu.VMEM((factors[s],) + rest + chunk, jnp.float32))
    if mode != "sum":
        scratch.append(pltpu.VMEM(tuple(reversed(factors)) + chunk, out_dtype))
    scratch.append(pltpu.SemaphoreType.DMA((4, stages, max(factors))))
    if mode == "sum":
        out_shape = chunk
    elif tiled is not None:
        out_shape = tiled
    else:
        out_shape = tuple(reversed(factors)) + chunk
    args = (x,) if scale is None else (x, scale)
    nbytes = n * math.prod(chunk) * 4
    y = pl.pallas_call(
        functools.partial(_staged_kernel, axis=axis, factors=tuple(factors), mode=mode,
                          has_scale=scale is not None, epilogue=epilogue),
        out_shape=jax.ShapeDtypeStruct(out_shape, out_dtype),
        in_specs=[pl.BlockSpec(memory_space=pltpu.VMEM)] * len(args),
        out_specs=pl.BlockSpec(memory_space=pltpu.VMEM),
        scratch_shapes=scratch,
        compiler_params=pltpu.CompilerParams(collective_id=cid, has_side_effects=True),
        cost_estimate=pl.CostEstimate(flops=0, transcendentals=0, bytes_accessed=2 * nbytes),
    )(*args)
    if mode == "sum" or tiled is not None:
        return y
    return y.reshape((n,) + chunk)


QUERY_FACTORS = (2, 4, 4)
GRAM_FACTORS = (4, 8)
ROW_FACTORS = (4, 4)


def _query_epilogue(total, s_ref):
    return (total * s_ref[...]).astype(jnp.bfloat16)


def _product_epilogue(total, s_ref):
    return total * s_ref[...]


GROUP = 8


def _products_kernel(*refs, forward, lift):
    if lift:
        ids_ref, count_ref, inv_ref, lifted_ref, scale_ref, tiles_hbm, out_ref, tiles, sems, src_ref = refs
    else:
        ids_ref, count_ref, src_ref, tiles_hbm, out_ref, tiles, sems = refs
    slots = tiles.shape[0]
    groups = slots // GROUP

    def fetch(g):
        return pltpu.make_async_copy(
            tiles_hbm.at[pl.ds(g * GROUP, GROUP)], tiles.at[pl.ds(g * GROUP, GROUP)], sems.at[g]
        )

    for g in range(groups):
        fetch(g).start()
    if lift:
        inv = inv_ref[...]
        for p in range(src_ref.shape[0]):
            current = jnp.dot(inv, lifted_ref[p], precision=HIGH, preferred_element_type=jnp.float32)
            src_ref[p] = (current * scale_ref[p]).astype(src_ref.dtype)
    out_ref[...] = jnp.zeros_like(out_ref)
    src_row, dst_row = (1, 0) if forward else (0, 1)
    count = count_ref[0]
    for g in range(groups):
        fetch(g).wait()
        ys = []
        for k in range(g * GROUP, (g + 1) * GROUP):
            x = src_ref[ids_ref[src_row, k]]
            t = tiles[k]
            if forward:
                y = lax.dot_general(x, t, (((1,), (1,)), ((), ())),
                                    preferred_element_type=jnp.float32)
            else:
                y = jnp.dot(x, t, preferred_element_type=jnp.float32)
            ys.append(jnp.where(k < count, y, 0.0))
        for k, y in zip(range(g * GROUP, (g + 1) * GROUP), ys):
            d = ids_ref[dst_row, k]
            out_ref[d] = out_ref[d] + y


def tile_products(slot_ids, live_count, src, tile_set, blocks, forward, lift=None):
    slots, side, _ = tile_set.shape
    width = src.shape[1] if lift is None else lift[1].shape[1]
    scratch = [pltpu.VMEM(tile_set.shape, tile_set.dtype), pltpu.SemaphoreType.DMA((slots // GROUP,))]
    if lift is None:
        operands = (src,)
    else:
        operands = lift
        scratch.append(pltpu.VMEM(lift[1].shape, jnp.bfloat16))
    vmem = pl.BlockSpec(memory_space=pltpu.VMEM)
    smem = pl.BlockSpec(memory_space=pltpu.SMEM)
    return pl.pallas_call(
        functools.partial(_products_kernel, forward=forward, lift=lift is not None),
        out_shape=jax.ShapeDtypeStruct((blocks, width, side), jnp.float32),
        in_specs=[smem, smem] + [vmem] * len(operands) + [pl.BlockSpec(memory_space=pl.ANY)],
        out_specs=vmem,
        scratch_shapes=scratch,
        cost_estimate=pl.CostEstimate(
            flops=2 * slots * width * side * side, transcendentals=0,
            bytes_accessed=slots * side * side * 2 + blocks * width * side * 6,
        ),
    )(slot_ids, live_count.reshape(1), *operands, tile_set)


def _eliminate(m):
    rows, cols = m.shape
    row = lax.broadcasted_iota(jnp.int32, (rows, cols), 0)
    lane = lax.broadcasted_iota(jnp.int32, (rows, cols), 1)

    def step(j, m):
        pivot_row = jnp.sum(jnp.where(row == j, m, 0.0), axis=0, keepdims=True)
        pivot = jnp.sum(jnp.where(lane[:1] == j, pivot_row, 0.0), axis=1, keepdims=True)
        inv_root = 1.0 / jnp.sqrt(pivot)
        scaled_row = pivot_row * inv_root
        column = jnp.sum(jnp.where(lane == j, m, 0.0), axis=1, keepdims=True) * inv_root
        return jnp.where(row == j, scaled_row, jnp.where(row > j, m - column * scaled_row, m))

    return lax.fori_loop(0, rows, step, m, unroll=2)


def _lower_inverse_kernel(m_ref, out_ref):
    out_ref[...] = _eliminate(m_ref[...])


def lower_inverse(gram):
    width = gram.shape[0]
    augmented = jnp.concatenate([gram, jnp.eye(width, dtype=gram.dtype)], axis=1)
    reduced = pl.pallas_call(
        _lower_inverse_kernel,
        out_shape=jax.ShapeDtypeStruct(augmented.shape, augmented.dtype),
        in_specs=[pl.BlockSpec(memory_space=pltpu.VMEM)],
        out_specs=pl.BlockSpec(memory_space=pltpu.VMEM),
    )(augmented)
    return reduced[:, width:]


def lower_inverse_native(gram):
    lower = lax.linalg.cholesky(gram, symmetrize_input=False)
    eye = jnp.eye(gram.shape[0], dtype=gram.dtype)
    return lax.linalg.triangular_solve(lower, eye, left_side=True, lower=True)


def shards(tiles, tile_ids, tile_count, query_degree, product_degree, panel):
    tile_set = tiles[0, 0]
    slot_ids = tile_ids[0, 0]
    live_count = tile_count[0, 0]
    side = tile_set.shape[1]
    width = panel.shape[0]
    query_tiles = query_degree.shape[0] // side
    product_tiles = product_degree.shape[0] // side
    n_row = lax.axis_size("row")
    n_col = lax.axis_size("col")
    qscale = (1.0 / jnp.sqrt(query_degree.astype(jnp.float32))).reshape(query_tiles, 1, side)
    pscale = (1.0 / jnp.sqrt(product_degree.astype(jnp.float32))).reshape(product_tiles, 1, side)
    row_at = lax.axis_index("row")
    col_at = lax.axis_index("col")
    share = panel.shape[1]
    block = product_degree.shape[0]
    q_per_tile = n_col // query_tiles
    p_per_tile = n_row // product_tiles
    my_qscale = lax.dynamic_index_in_dim(qscale, col_at // q_per_tile, keepdims=False)
    my_pscale = lax.dynamic_index_in_dim(pscale, row_at // p_per_tile, keepdims=False)
    root_count = math.sqrt(product_degree.shape[0] * n_col)

    panel_pscale = lax.dynamic_slice_in_dim(pscale.reshape(block), row_at * share, share)
    scaled0 = (panel * panel_pscale[None, :]).astype(jnp.bfloat16)
    scaled_tiles = staged(scaled0, "row", ROW_FACTORS, "gather", 0,
                          tiled=(product_tiles, width, side))
    per_tile = side // share
    for iteration in range(ITERS):
        if iteration:
            partial_sum = tile_products(slot_ids, live_count, None, tile_set, query_tiles, True,
                                        lift=(inverse, lifted_tiles, pscale))
        else:
            partial_sum = tile_products(slot_ids, live_count, scaled_tiles, tile_set, query_tiles, True)
        query_tiles_panel = staged(
            partial_sum.reshape(n_col, width // q_per_tile, side), "col", QUERY_FACTORS, "reduce", 1,
            scale=my_qscale, epilogue=_query_epilogue, out_dtype=jnp.bfloat16,
        ).reshape(query_tiles, width, side)
        product_partial = tile_products(
            slot_ids, live_count, query_tiles_panel, tile_set, product_tiles, False
        )
        lifted_pieces, inverse = product_gram(
            product_partial.reshape(n_row, width // p_per_tile, side), my_pscale, ROW_FACTORS,
            GRAM_FACTORS, 2, width,
        )
        lifted_tiles = lifted_pieces.reshape(product_tiles, width, side)
    my_tile = lax.dynamic_index_in_dim(lifted_tiles, row_at // per_tile, keepdims=False)
    my_lifted = lax.dynamic_slice_in_dim(my_tile, (row_at % per_tile) * share, share, axis=1)
    return jnp.einsum("rs,si->ri", inverse, my_lifted, precision=HIGH) * root_count


def solution(mesh):
    in_specs = (
        P("row", "col", None, None, None),
        P("row", "col", None, None),
        P("row", "col"),
        P("row"),
        P("col"),
        P(None, ("col", "row")),
    )
    out_specs = P(None, ("col", "row"))
    return jax.shard_map(shards, mesh=mesh, in_specs=in_specs, out_specs=out_specs, check_vma=False)
```

```python
import functools
import math

import jax
import jax.numpy as jnp
from jax import lax
from jax.experimental import pallas as pl
from jax.experimental.pallas import tpu as pltpu
from jax.sharding import PartitionSpec as P

ITERS = 2


HIGH = lax.Precision.HIGHEST

AXES = ("row", "col")


def _device(axis, peer):
    if axis == "row":
        return (peer, lax.axis_index("col"))
    return (lax.axis_index("row"), peer)


class _Plan:
    def __init__(self, axis, factors):
        self.axis = axis
        self.factors = tuple(factors)
        self.stages = len(factors)
        self.me = lax.axis_index(axis)
        self.strides = [math.prod(factors[:s]) for s in range(self.stages)]
        self.mine = [lax.rem(lax.div(self.me, self.strides[s]), factors[s])
                     for s in range(self.stages)]

    def peer(self, s, d):
        return _device(self.axis, self.me + (d - self.mine[s]) * self.strides[s])

    def other(self, s, k):
        return lax.rem(self.mine[s] + k, self.factors[s])

    def peers(self):
        return [self.peer(s, self.other(s, k)) for s in range(self.stages)
                for k in range(1, self.factors[s])]


def _barrier(plans):
    barrier = pltpu.get_barrier_semaphore()
    count = 0
    for plan in plans:
        for dev in plan.peers():
            pl.semaphore_signal(barrier, inc=1, device_id=dev, device_id_type=pl.DeviceIdType.MESH)
            count += 1
    pl.semaphore_wait(barrier, count)


def _exchange(plan, sems, kind, s, src_of, dst_of, pending):
    copies = []
    mine = plan.mine[s]
    for k in range(1, plan.factors[s]):
        d = plan.other(s, k)
        c = pltpu.make_async_remote_copy(
            src_ref=src_of(d), dst_ref=dst_of(mine),
            send_sem=sems.at[kind, s, d], recv_sem=sems.at[kind + 1, s, mine],
            device_id=plan.peer(s, d), device_id_type=pl.DeviceIdType.MESH,
        )
        c.start()
        copies.append((d, c))
    pending.extend(c for _, c in copies)
    for d, c in copies:
        pltpu.make_async_remote_copy(
            src_ref=src_of(d), dst_ref=dst_of(d),
            send_sem=sems.at[kind, s, d], recv_sem=sems.at[kind + 1, s, d],
            device_id=plan.peer(s, d), device_id_type=pl.DeviceIdType.MESH,
        ).wait_recv()


def _reduce_scatter(plan, sems, kind, x_ref, rbufs, pending):
    cur = x_ref
    for s in range(plan.stages):
        lead = plan.stages - 1 - s

        def src_of(d, cur=cur, lead=lead):
            return cur.at[(slice(None),) * lead + (d,)]

        rb = rbufs[s]
        _exchange(plan, sems, kind, s, src_of, lambda d, rb=rb: rb.at[d], pending)
        total = cur[(slice(None),) * lead + (plan.mine[s],)]
        for k in range(1, plan.factors[s]):
            total = total + rb[plan.other(s, k)]
        rb[plan.mine[s]] = total
        cur = rb.at[plan.mine[s]]
    return cur


def _all_gather(plan, sems, kind, gbuf, own, pending):
    mine = plan.mine
    gbuf[tuple(mine[::-1])] = own.astype(gbuf.dtype)
    for s in reversed(range(plan.stages)):
        lead = plan.stages - 1 - s

        def view(d, s=s, lead=lead):
            return gbuf.at[(slice(None),) * lead + (d,) + tuple(mine[s - 1::-1] if s else ())]

        _exchange(plan, sems, kind, s, lambda d, s=s: view(mine[s]), view, pending)


def _sum(plan, sems, kind, value, rbufs, pending):
    for s in range(plan.stages):
        rb = rbufs[s]
        rb[plan.mine[s]] = value
        src = rb.at[plan.mine[s]]
        _exchange(plan, sems, kind, s, lambda d, src=src: src, lambda d, rb=rb: rb.at[d], pending)
        value = rb[0]
        for d in range(1, plan.factors[s]):
            value = value + rb[d]
    return value


def _staged_kernel(*refs, axis, factors, mode, has_scale, epilogue):
    if has_scale:
        x_ref, s_ref, y_ref = refs[:3]
        rest = refs[3:]
    else:
        x_ref, y_ref = refs[:2]
        s_ref = None
        rest = refs[2:]
    plan = _Plan(axis, factors)
    n_rs = plan.stages if mode in ("reduce", "sum") else 0
    rbufs = rest[:n_rs]
    gbuf = rest[n_rs] if mode != "sum" else None
    sems = rest[-1]
    _barrier([plan])
    pending = []
    if mode == "sum":
        y_ref[...] = _sum(plan, sems, 0, x_ref[...], rbufs, pending)
    else:
        if mode == "reduce":
            own = epilogue(_reduce_scatter(plan, sems, 0, x_ref, rbufs, pending)[...], s_ref)
        else:
            own = x_ref[...]
        _all_gather(plan, sems, 2, gbuf, own, pending)
        if mode == "gather" and len(y_ref.shape) == 3:
            n = math.prod(factors)
            share = own.shape[-1]
            per = y_ref.shape[-1] // share
            for j in range(n):
                y_ref[j // per, :, pl.ds((j % per) * share, share)] = gbuf[_digits(j, factors)]
        else:
            y_ref[...] = gbuf[...]
    for c in pending:
        c.wait_send()


def _digits(j, factors):
    return tuple((j // math.prod(factors[:s])) % factors[s] for s in reversed(range(len(factors))))


def _product_gram_kernel(x_ref, s_ref, y_ref, g_ref, *rest, row_factors, col_factors):
    rows = _Plan("row", row_factors)
    cols = _Plan("col", col_factors)
    rbufs = rest[:rows.stages]
    gbuf = rest[rows.stages]
    cbufs = rest[rows.stages + 1:rows.stages + 1 + cols.stages]
    sems = rest[-1]
    _barrier([rows, cols])
    pending = []
    own = _reduce_scatter(rows, sems, 0, x_ref, rbufs, pending)[...] * s_ref[...]
    _all_gather(rows, sems, 2, gbuf, own, pending)
    y_ref[...] = gbuf[...]
    n = math.prod(row_factors)
    per = y_ref.shape[-2]
    width = g_ref.shape[0]
    gram = None
    for p in range(n * per // width):
        parts = [y_ref[_digits(p * width // per + i, row_factors)] for i in range(width // per)]
        block = jnp.concatenate(parts, axis=0)
        padded = jnp.concatenate([block, jnp.zeros_like(block)], axis=0)
        term = lax.dot_general(block, padded, (((1,), (1,)), ((), ())), precision=HIGH,
                               preferred_element_type=jnp.float32)
        gram = term if gram is None else gram + term
    total = _sum(cols, sems, 4, gram, cbufs, pending)
    row = lax.broadcasted_iota(jnp.int32, total.shape, 0)
    lane = lax.broadcasted_iota(jnp.int32, total.shape, 1)
    g_ref[...] = _eliminate(total + jnp.where(lane == row + width, 1.0, 0.0))
    for c in pending:
        c.wait_send()


def product_gram(x, scale, row_factors, col_factors, cid, width):
    n = math.prod(row_factors)
    chunk = x.shape[1:]
    x = x.reshape(tuple(reversed(row_factors)) + chunk)
    scratch = []
    for s in range(len(row_factors)):
        scratch.append(pltpu.VMEM((row_factors[s],) + tuple(reversed(row_factors[s + 1:])) + chunk,
                                  jnp.float32))
    scratch.append(pltpu.VMEM(tuple(reversed(row_factors)) + chunk, jnp.float32))
    for s in range(len(col_factors)):
        scratch.append(pltpu.VMEM((col_factors[s], width, 2 * width), jnp.float32))
    scratch.append(pltpu.SemaphoreType.DMA((6, max(len(row_factors), len(col_factors)),
                                            max(row_factors + col_factors))))
    nbytes = n * math.prod(chunk) * 4
    y, g = pl.pallas_call(
        functools.partial(_product_gram_kernel, row_factors=tuple(row_factors),
                          col_factors=tuple(col_factors)),
        out_shape=(jax.ShapeDtypeStruct(tuple(reversed(row_factors)) + chunk, jnp.float32),
                   jax.ShapeDtypeStruct((width, 2 * width), jnp.float32)),
        in_specs=[pl.BlockSpec(memory_space=pltpu.VMEM)] * 2,
        out_specs=(pl.BlockSpec(memory_space=pltpu.VMEM), pl.BlockSpec(memory_space=pltpu.VMEM)),
        scratch_shapes=scratch,
        compiler_params=pltpu.CompilerParams(collective_id=cid, has_side_effects=True),
        cost_estimate=pl.CostEstimate(flops=0, transcendentals=0, bytes_accessed=2 * nbytes),
    )(x, scale)
    return y.reshape((n,) + chunk), g[:, width:]


def staged(x, axis, factors, mode, cid, scale=None, epilogue=None, out_dtype=None, tiled=None):
    n = math.prod(factors)
    stages = len(factors)
    out_dtype = out_dtype or x.dtype
    if mode == "reduce":
        chunk = x.shape[1:]
        x = x.reshape(tuple(reversed(factors)) + chunk)
    else:
        chunk = x.shape
    scratch = []
    if mode in ("reduce", "sum"):
        for s in range(stages):
            rest = tuple(reversed(factors[s + 1:])) if mode == "reduce" else ()
            scratch.append(pltpu.VMEM((factors[s],) + rest + chunk, jnp.float32))
    if mode != "sum":
        scratch.append(pltpu.VMEM(tuple(reversed(factors)) + chunk, out_dtype))
    scratch.append(pltpu.SemaphoreType.DMA((4, stages, max(factors))))
    if mode == "sum":
        out_shape = chunk
    elif tiled is not None:
        out_shape = tiled
    else:
        out_shape = tuple(reversed(factors)) + chunk
    args = (x,) if scale is None else (x, scale)
    nbytes = n * math.prod(chunk) * 4
    y = pl.pallas_call(
        functools.partial(_staged_kernel, axis=axis, factors=tuple(factors), mode=mode,
                          has_scale=scale is not None, epilogue=epilogue),
        out_shape=jax.ShapeDtypeStruct(out_shape, out_dtype),
        in_specs=[pl.BlockSpec(memory_space=pltpu.VMEM)] * len(args),
        out_specs=pl.BlockSpec(memory_space=pltpu.VMEM),
        scratch_shapes=scratch,
        compiler_params=pltpu.CompilerParams(collective_id=cid, has_side_effects=True),
        cost_estimate=pl.CostEstimate(flops=0, transcendentals=0, bytes_accessed=2 * nbytes),
    )(*args)
    if mode == "sum" or tiled is not None:
        return y
    return y.reshape((n,) + chunk)


QUERY_FACTORS = (2, 4, 4)
GRAM_FACTORS = (4, 8)
ROW_FACTORS = (4, 4)


def _query_epilogue(total, s_ref):
    return (total * s_ref[...]).astype(jnp.bfloat16)


def _product_epilogue(total, s_ref):
    return total * s_ref[...]


GROUP = 8


def _products_kernel(*refs, forward, lift):
    if lift:
        ids_ref, count_ref, inv_ref, lifted_ref, scale_ref, tiles_hbm, out_ref, tiles, sems, src_ref = refs
    else:
        ids_ref, count_ref, src_ref, tiles_hbm, out_ref, tiles, sems = refs
    slots = tiles.shape[0]
    groups = slots // GROUP

    def fetch(g):
        return pltpu.make_async_copy(
            tiles_hbm.at[pl.ds(g * GROUP, GROUP)], tiles.at[pl.ds(g * GROUP, GROUP)], sems.at[g]
        )

    for g in range(groups):
        fetch(g).start()
    if lift:
        inv = inv_ref[...]
        for p in range(src_ref.shape[0]):
            current = jnp.dot(inv, lifted_ref[p], precision=HIGH, preferred_element_type=jnp.float32)
            src_ref[p] = (current * scale_ref[p]).astype(src_ref.dtype)
    out_ref[...] = jnp.zeros_like(out_ref)
    src_row, dst_row = (1, 0) if forward else (0, 1)
    count = count_ref[0]
    for g in range(groups):
        fetch(g).wait()
        ys = []
        for k in range(g * GROUP, (g + 1) * GROUP):
            x = src_ref[ids_ref[src_row, k]]
            t = tiles[k]
            if forward:
                y = lax.dot_general(x, t, (((1,), (1,)), ((), ())),
                                    preferred_element_type=jnp.float32)
            else:
                y = jnp.dot(x, t, preferred_element_type=jnp.float32)
            ys.append(jnp.where(k < count, y, 0.0))
        for k, y in zip(range(g * GROUP, (g + 1) * GROUP), ys):
            d = ids_ref[dst_row, k]
            out_ref[d] = out_ref[d] + y


def tile_products(slot_ids, live_count, src, tile_set, blocks, forward, lift=None):
    slots, side, _ = tile_set.shape
    width = src.shape[1] if lift is None else lift[1].shape[1]
    scratch = [pltpu.VMEM(tile_set.shape, tile_set.dtype), pltpu.SemaphoreType.DMA((slots // GROUP,))]
    if lift is None:
        operands = (src,)
    else:
        operands = lift
        scratch.append(pltpu.VMEM(lift[1].shape, jnp.bfloat16))
    vmem = pl.BlockSpec(memory_space=pltpu.VMEM)
    smem = pl.BlockSpec(memory_space=pltpu.SMEM)
    return pl.pallas_call(
        functools.partial(_products_kernel, forward=forward, lift=lift is not None),
        out_shape=jax.ShapeDtypeStruct((blocks, width, side), jnp.float32),
        in_specs=[smem, smem] + [vmem] * len(operands) + [pl.BlockSpec(memory_space=pl.ANY)],
        out_specs=vmem,
        scratch_shapes=scratch,
        cost_estimate=pl.CostEstimate(
            flops=2 * slots * width * side * side, transcendentals=0,
            bytes_accessed=slots * side * side * 2 + blocks * width * side * 6,
        ),
    )(slot_ids, live_count.reshape(1), *operands, tile_set)


def _eliminate(m):
    rows, cols = m.shape
    row = lax.broadcasted_iota(jnp.int32, (rows, cols), 0)
    lane = lax.broadcasted_iota(jnp.int32, (rows, cols), 1)

    def step(j, m):
        pivot_row = jnp.sum(jnp.where(row == j, m, 0.0), axis=0, keepdims=True)
        pivot = jnp.sum(jnp.where(lane[:1] == j, pivot_row, 0.0), axis=1, keepdims=True)
        inv_root = 1.0 / jnp.sqrt(pivot)
        scaled_row = pivot_row * inv_root
        column = jnp.sum(jnp.where(lane == j, m, 0.0), axis=1, keepdims=True) * inv_root
        return jnp.where(row == j, scaled_row, jnp.where(row > j, m - column * scaled_row, m))

    return lax.fori_loop(0, rows, step, m, unroll=4)


def _lower_inverse_kernel(m_ref, out_ref):
    out_ref[...] = _eliminate(m_ref[...])


def lower_inverse(gram):
    width = gram.shape[0]
    augmented = jnp.concatenate([gram, jnp.eye(width, dtype=gram.dtype)], axis=1)
    reduced = pl.pallas_call(
        _lower_inverse_kernel,
        out_shape=jax.ShapeDtypeStruct(augmented.shape, augmented.dtype),
        in_specs=[pl.BlockSpec(memory_space=pltpu.VMEM)],
        out_specs=pl.BlockSpec(memory_space=pltpu.VMEM),
    )(augmented)
    return reduced[:, width:]


def lower_inverse_native(gram):
    lower = lax.linalg.cholesky(gram, symmetrize_input=False)
    eye = jnp.eye(gram.shape[0], dtype=gram.dtype)
    return lax.linalg.triangular_solve(lower, eye, left_side=True, lower=True)


def shards(tiles, tile_ids, tile_count, query_degree, product_degree, panel):
    tile_set = tiles[0, 0]
    slot_ids = tile_ids[0, 0]
    live_count = tile_count[0, 0]
    side = tile_set.shape[1]
    width = panel.shape[0]
    query_tiles = query_degree.shape[0] // side
    product_tiles = product_degree.shape[0] // side
    n_row = lax.axis_size("row")
    n_col = lax.axis_size("col")
    qscale = (1.0 / jnp.sqrt(query_degree.astype(jnp.float32))).reshape(query_tiles, 1, side)
    pscale = (1.0 / jnp.sqrt(product_degree.astype(jnp.float32))).reshape(product_tiles, 1, side)
    row_at = lax.axis_index("row")
    col_at = lax.axis_index("col")
    share = panel.shape[1]
    block = product_degree.shape[0]
    q_per_tile = n_col // query_tiles
    p_per_tile = n_row // product_tiles
    my_qscale = lax.dynamic_index_in_dim(qscale, col_at // q_per_tile, keepdims=False)
    my_pscale = lax.dynamic_index_in_dim(pscale, row_at // p_per_tile, keepdims=False)
    root_count = math.sqrt(product_degree.shape[0] * n_col)

    panel_pscale = lax.dynamic_slice_in_dim(pscale.reshape(block), row_at * share, share)
    scaled0 = (panel * panel_pscale[None, :]).astype(jnp.bfloat16)
    scaled_tiles = staged(scaled0, "row", ROW_FACTORS, "gather", 0,
                          tiled=(product_tiles, width, side))
    per_tile = side // share
    for iteration in range(ITERS):
        if iteration:
            partial_sum = tile_products(slot_ids, live_count, None, tile_set, query_tiles, True,
                                        lift=(inverse, lifted_tiles, pscale))
        else:
            partial_sum = tile_products(slot_ids, live_count, scaled_tiles, tile_set, query_tiles, True)
        query_tiles_panel = staged(
            partial_sum.reshape(n_col, width // q_per_tile, side), "col", QUERY_FACTORS, "reduce", 1,
            scale=my_qscale, epilogue=_query_epilogue, out_dtype=jnp.bfloat16,
        ).reshape(query_tiles, width, side)
        product_partial = tile_products(
            slot_ids, live_count, query_tiles_panel, tile_set, product_tiles, False
        )
        lifted_pieces, inverse = product_gram(
            product_partial.reshape(n_row, width // p_per_tile, side), my_pscale, ROW_FACTORS,
            GRAM_FACTORS, 2, width,
        )
        lifted_tiles = lifted_pieces.reshape(product_tiles, width, side)
    my_tile = lax.dynamic_index_in_dim(lifted_tiles, row_at // per_tile, keepdims=False)
    my_lifted = lax.dynamic_slice_in_dim(my_tile, (row_at % per_tile) * share, share, axis=1)
    return jnp.einsum("rs,si->ri", inverse, my_lifted, precision=HIGH) * root_count


def solution(mesh):
    in_specs = (
        P("row", "col", None, None, None),
        P("row", "col", None, None),
        P("row", "col"),
        P("row"),
        P("col"),
        P(None, ("col", "row")),
    )
    out_specs = P(None, ("col", "row"))
    return jax.shard_map(shards, mesh=mesh, in_specs=in_specs, out_specs=out_specs, check_vma=False)
```

```python
import functools
import math

import jax
import jax.numpy as jnp
from jax import lax
from jax.experimental import pallas as pl
from jax.experimental.pallas import tpu as pltpu
from jax.sharding import PartitionSpec as P

ITERS = 2


HIGH = lax.Precision.HIGHEST

AXES = ("row", "col")


def _device(axis, peer):
    if axis == "row":
        return (peer, lax.axis_index("col"))
    return (lax.axis_index("row"), peer)


class _Plan:
    def __init__(self, axis, factors):
        self.axis = axis
        self.factors = tuple(factors)
        self.stages = len(factors)
        self.me = lax.axis_index(axis)
        self.strides = [math.prod(factors[:s]) for s in range(self.stages)]
        self.mine = [lax.rem(lax.div(self.me, self.strides[s]), factors[s])
                     for s in range(self.stages)]

    def peer(self, s, d):
        return _device(self.axis, self.me + (d - self.mine[s]) * self.strides[s])

    def other(self, s, k):
        return lax.rem(self.mine[s] + k, self.factors[s])

    def peers(self):
        return [self.peer(s, self.other(s, k)) for s in range(self.stages)
                for k in range(1, self.factors[s])]


def _barrier(plans):
    barrier = pltpu.get_barrier_semaphore()
    count = 0
    for plan in plans:
        for dev in plan.peers():
            pl.semaphore_signal(barrier, inc=1, device_id=dev, device_id_type=pl.DeviceIdType.MESH)
            count += 1
    pl.semaphore_wait(barrier, count)


def _exchange(plan, sems, kind, s, src_of, dst_of, pending):
    copies = []
    mine = plan.mine[s]
    for k in range(1, plan.factors[s]):
        d = plan.other(s, k)
        c = pltpu.make_async_remote_copy(
            src_ref=src_of(d), dst_ref=dst_of(mine),
            send_sem=sems.at[kind, s, d], recv_sem=sems.at[kind + 1, s, mine],
            device_id=plan.peer(s, d), device_id_type=pl.DeviceIdType.MESH,
        )
        c.start()
        copies.append((d, c))
    pending.extend(c for _, c in copies)
    for d, c in copies:
        pltpu.make_async_remote_copy(
            src_ref=src_of(d), dst_ref=dst_of(d),
            send_sem=sems.at[kind, s, d], recv_sem=sems.at[kind + 1, s, d],
            device_id=plan.peer(s, d), device_id_type=pl.DeviceIdType.MESH,
        ).wait_recv()


def _reduce_scatter(plan, sems, kind, x_ref, rbufs, pending):
    cur = x_ref
    for s in range(plan.stages):
        lead = plan.stages - 1 - s

        def src_of(d, cur=cur, lead=lead):
            return cur.at[(slice(None),) * lead + (d,)]

        rb = rbufs[s]
        _exchange(plan, sems, kind, s, src_of, lambda d, rb=rb: rb.at[d], pending)
        total = cur[(slice(None),) * lead + (plan.mine[s],)]
        for k in range(1, plan.factors[s]):
            total = total + rb[plan.other(s, k)]
        rb[plan.mine[s]] = total
        cur = rb.at[plan.mine[s]]
    return cur


def _all_gather(plan, sems, kind, gbuf, own, pending):
    mine = plan.mine
    gbuf[tuple(mine[::-1])] = own.astype(gbuf.dtype)
    for s in reversed(range(plan.stages)):
        lead = plan.stages - 1 - s

        def view(d, s=s, lead=lead):
            return gbuf.at[(slice(None),) * lead + (d,) + tuple(mine[s - 1::-1] if s else ())]

        _exchange(plan, sems, kind, s, lambda d, s=s: view(mine[s]), view, pending)


def _sum(plan, sems, kind, value, rbufs, pending):
    for s in range(plan.stages):
        rb = rbufs[s]
        rb[plan.mine[s]] = value
        src = rb.at[plan.mine[s]]
        _exchange(plan, sems, kind, s, lambda d, src=src: src, lambda d, rb=rb: rb.at[d], pending)
        value = rb[0]
        for d in range(1, plan.factors[s]):
            value = value + rb[d]
    return value


def _staged_kernel(*refs, axis, factors, mode, has_scale, epilogue):
    if has_scale:
        x_ref, s_ref, y_ref = refs[:3]
        rest = refs[3:]
    else:
        x_ref, y_ref = refs[:2]
        s_ref = None
        rest = refs[2:]
    plan = _Plan(axis, factors)
    n_rs = plan.stages if mode in ("reduce", "sum") else 0
    rbufs = rest[:n_rs]
    gbuf = rest[n_rs] if mode != "sum" else None
    sems = rest[-1]
    _barrier([plan])
    pending = []
    if mode == "sum":
        y_ref[...] = _sum(plan, sems, 0, x_ref[...], rbufs, pending)
    else:
        if mode == "reduce":
            own = epilogue(_reduce_scatter(plan, sems, 0, x_ref, rbufs, pending)[...], s_ref)
        elif epilogue is not None:
            own = epilogue(x_ref[...], s_ref.at[pl.ds(plan.me, 1)])
        else:
            own = x_ref[...]
        _all_gather(plan, sems, 2, gbuf, own, pending)
        if mode == "gather" and len(y_ref.shape) == 3:
            n = math.prod(factors)
            share = own.shape[-1]
            per = y_ref.shape[-1] // share
            for j in range(n):
                y_ref[j // per, :, pl.ds((j % per) * share, share)] = gbuf[_digits(j, factors)]
        else:
            y_ref[...] = gbuf[...]
    for c in pending:
        c.wait_send()


def _digits(j, factors):
    return tuple((j // math.prod(factors[:s])) % factors[s] for s in reversed(range(len(factors))))


def _product_gram_kernel(x_ref, s_ref, y_ref, g_ref, *rest, row_factors, col_factors):
    rows = _Plan("row", row_factors)
    cols = _Plan("col", col_factors)
    rbufs = rest[:rows.stages]
    gbuf = rest[rows.stages]
    cbufs = rest[rows.stages + 1:rows.stages + 1 + cols.stages]
    sems = rest[-1]
    _barrier([rows, cols])
    pending = []
    own = _reduce_scatter(rows, sems, 0, x_ref, rbufs, pending)[...] * s_ref[...]
    _all_gather(rows, sems, 2, gbuf, own, pending)
    y_ref[...] = gbuf[...]
    n = math.prod(row_factors)
    per = y_ref.shape[-2]
    width = g_ref.shape[0]
    gram = None
    for p in range(n * per // width):
        parts = [y_ref[_digits(p * width // per + i, row_factors)] for i in range(width // per)]
        block = jnp.concatenate(parts, axis=0)
        padded = jnp.concatenate([block, jnp.zeros_like(block)], axis=0)
        term = lax.dot_general(block, padded, (((1,), (1,)), ((), ())), precision=HIGH,
                               preferred_element_type=jnp.float32)
        gram = term if gram is None else gram + term
    total = _sum(cols, sems, 4, gram, cbufs, pending)
    row = lax.broadcasted_iota(jnp.int32, total.shape, 0)
    lane = lax.broadcasted_iota(jnp.int32, total.shape, 1)
    g_ref[...] = _eliminate(total + jnp.where(lane == row + width, 1.0, 0.0))
    for c in pending:
        c.wait_send()


def product_gram(x, scale, row_factors, col_factors, cid, width):
    n = math.prod(row_factors)
    chunk = x.shape[1:]
    x = x.reshape(tuple(reversed(row_factors)) + chunk)
    scratch = []
    for s in range(len(row_factors)):
        scratch.append(pltpu.VMEM((row_factors[s],) + tuple(reversed(row_factors[s + 1:])) + chunk,
                                  jnp.float32))
    scratch.append(pltpu.VMEM(tuple(reversed(row_factors)) + chunk, jnp.float32))
    for s in range(len(col_factors)):
        scratch.append(pltpu.VMEM((col_factors[s], width, 2 * width), jnp.float32))
    scratch.append(pltpu.SemaphoreType.DMA((6, max(len(row_factors), len(col_factors)),
                                            max(row_factors + col_factors))))
    nbytes = n * math.prod(chunk) * 4
    y, g = pl.pallas_call(
        functools.partial(_product_gram_kernel, row_factors=tuple(row_factors),
                          col_factors=tuple(col_factors)),
        out_shape=(jax.ShapeDtypeStruct(tuple(reversed(row_factors)) + chunk, jnp.float32),
                   jax.ShapeDtypeStruct((width, 2 * width), jnp.float32)),
        in_specs=[pl.BlockSpec(memory_space=pltpu.VMEM)] * 2,
        out_specs=(pl.BlockSpec(memory_space=pltpu.VMEM), pl.BlockSpec(memory_space=pltpu.VMEM)),
        scratch_shapes=scratch,
        compiler_params=pltpu.CompilerParams(collective_id=cid, has_side_effects=True),
        cost_estimate=pl.CostEstimate(flops=0, transcendentals=0, bytes_accessed=2 * nbytes),
    )(x, scale)
    return y.reshape((n,) + chunk), g[:, width:]


def staged(x, axis, factors, mode, cid, scale=None, epilogue=None, out_dtype=None, tiled=None):
    n = math.prod(factors)
    stages = len(factors)
    out_dtype = out_dtype or x.dtype
    if mode == "reduce":
        chunk = x.shape[1:]
        x = x.reshape(tuple(reversed(factors)) + chunk)
    else:
        chunk = x.shape
    scratch = []
    if mode in ("reduce", "sum"):
        for s in range(stages):
            rest = tuple(reversed(factors[s + 1:])) if mode == "reduce" else ()
            scratch.append(pltpu.VMEM((factors[s],) + rest + chunk, jnp.float32))
    if mode != "sum":
        scratch.append(pltpu.VMEM(tuple(reversed(factors)) + chunk, out_dtype))
    scratch.append(pltpu.SemaphoreType.DMA((4, stages, max(factors))))
    if mode == "sum":
        out_shape = chunk
    elif tiled is not None:
        out_shape = tiled
    else:
        out_shape = tuple(reversed(factors)) + chunk
    args = (x,) if scale is None else (x, scale)
    nbytes = n * math.prod(chunk) * 4
    y = pl.pallas_call(
        functools.partial(_staged_kernel, axis=axis, factors=tuple(factors), mode=mode,
                          has_scale=scale is not None, epilogue=epilogue),
        out_shape=jax.ShapeDtypeStruct(out_shape, out_dtype),
        in_specs=[pl.BlockSpec(memory_space=pltpu.VMEM)] * len(args),
        out_specs=pl.BlockSpec(memory_space=pltpu.VMEM),
        scratch_shapes=scratch,
        compiler_params=pltpu.CompilerParams(collective_id=cid, has_side_effects=True),
        cost_estimate=pl.CostEstimate(flops=0, transcendentals=0, bytes_accessed=2 * nbytes),
    )(*args)
    if mode == "sum" or tiled is not None:
        return y
    return y.reshape((n,) + chunk)


QUERY_FACTORS = (2, 4, 4)
GRAM_FACTORS = (4, 8)
ROW_FACTORS = (4, 4)


def _query_epilogue(total, s_ref):
    return (total * s_ref[...]).astype(jnp.bfloat16)


def _panel_epilogue(panel, degree_ref):
    scale = 1.0 / jnp.sqrt(degree_ref[...].astype(jnp.float32))
    return (panel * scale).astype(jnp.bfloat16)


def _product_epilogue(total, s_ref):
    return total * s_ref[...]


GROUP = 8


def _products_kernel(*refs, forward, lift):
    if lift:
        ids_ref, count_ref, inv_ref, lifted_ref, scale_ref, tiles_hbm, out_ref, tiles, sems, src_ref = refs
    else:
        ids_ref, count_ref, src_ref, tiles_hbm, out_ref, tiles, sems = refs
    slots = tiles.shape[0]
    groups = slots // GROUP

    def fetch(g):
        return pltpu.make_async_copy(
            tiles_hbm.at[pl.ds(g * GROUP, GROUP)], tiles.at[pl.ds(g * GROUP, GROUP)], sems.at[g]
        )

    for g in range(groups):
        fetch(g).start()
    if lift:
        inv = inv_ref[...]
        for p in range(src_ref.shape[0]):
            current = jnp.dot(inv, lifted_ref[p], precision=HIGH, preferred_element_type=jnp.float32)
            src_ref[p] = (current * scale_ref[p]).astype(src_ref.dtype)
    out_ref[...] = jnp.zeros_like(out_ref)
    src_row, dst_row = (1, 0) if forward else (0, 1)
    count = count_ref[0]
    for g in range(groups):
        fetch(g).wait()
        ys = []
        for k in range(g * GROUP, (g + 1) * GROUP):
            x = src_ref[ids_ref[src_row, k]]
            t = tiles[k]
            if forward:
                y = lax.dot_general(x, t, (((1,), (1,)), ((), ())),
                                    preferred_element_type=jnp.float32)
            else:
                y = jnp.dot(x, t, preferred_element_type=jnp.float32)
            ys.append(jnp.where(k < count, y, 0.0))
        for k, y in zip(range(g * GROUP, (g + 1) * GROUP), ys):
            d = ids_ref[dst_row, k]
            out_ref[d] = out_ref[d] + y


def tile_products(slot_ids, live_count, src, tile_set, blocks, forward, lift=None):
    slots, side, _ = tile_set.shape
    width = src.shape[1] if lift is None else lift[1].shape[1]
    scratch = [pltpu.VMEM(tile_set.shape, tile_set.dtype), pltpu.SemaphoreType.DMA((slots // GROUP,))]
    if lift is None:
        operands = (src,)
    else:
        operands = lift
        scratch.append(pltpu.VMEM(lift[1].shape, jnp.bfloat16))
    vmem = pl.BlockSpec(memory_space=pltpu.VMEM)
    smem = pl.BlockSpec(memory_space=pltpu.SMEM)
    return pl.pallas_call(
        functools.partial(_products_kernel, forward=forward, lift=lift is not None),
        out_shape=jax.ShapeDtypeStruct((blocks, width, side), jnp.float32),
        in_specs=[smem, smem] + [vmem] * len(operands) + [pl.BlockSpec(memory_space=pl.ANY)],
        out_specs=vmem,
        scratch_shapes=scratch,
        cost_estimate=pl.CostEstimate(
            flops=2 * slots * width * side * side, transcendentals=0,
            bytes_accessed=slots * side * side * 2 + blocks * width * side * 6,
        ),
    )(slot_ids, live_count.reshape(1), *operands, tile_set)


def _eliminate(m):
    rows, cols = m.shape
    row = lax.broadcasted_iota(jnp.int32, (rows, cols), 0)
    lane = lax.broadcasted_iota(jnp.int32, (rows, cols), 1)

    def step(j, m):
        pivot_row = jnp.sum(jnp.where(row == j, m, 0.0), axis=0, keepdims=True)
        pivot = jnp.sum(jnp.where(lane[:1] == j, pivot_row, 0.0), axis=1, keepdims=True)
        inv_root = 1.0 / jnp.sqrt(pivot)
        scaled_row = pivot_row * inv_root
        column = jnp.sum(jnp.where(lane == j, m, 0.0), axis=1, keepdims=True) * inv_root
        return jnp.where(row == j, scaled_row, jnp.where(row > j, m - column * scaled_row, m))

    return lax.fori_loop(0, rows, step, m, unroll=2)


def _lower_inverse_kernel(m_ref, out_ref):
    out_ref[...] = _eliminate(m_ref[...])


def lower_inverse(gram):
    width = gram.shape[0]
    augmented = jnp.concatenate([gram, jnp.eye(width, dtype=gram.dtype)], axis=1)
    reduced = pl.pallas_call(
        _lower_inverse_kernel,
        out_shape=jax.ShapeDtypeStruct(augmented.shape, augmented.dtype),
        in_specs=[pl.BlockSpec(memory_space=pltpu.VMEM)],
        out_specs=pl.BlockSpec(memory_space=pltpu.VMEM),
    )(augmented)
    return reduced[:, width:]


def lower_inverse_native(gram):
    lower = lax.linalg.cholesky(gram, symmetrize_input=False)
    eye = jnp.eye(gram.shape[0], dtype=gram.dtype)
    return lax.linalg.triangular_solve(lower, eye, left_side=True, lower=True)


def shards(tiles, tile_ids, tile_count, query_degree, product_degree, panel):
    tile_set = tiles[0, 0]
    slot_ids = tile_ids[0, 0]
    live_count = tile_count[0, 0]
    side = tile_set.shape[1]
    width = panel.shape[0]
    query_tiles = query_degree.shape[0] // side
    product_tiles = product_degree.shape[0] // side
    n_row = lax.axis_size("row")
    n_col = lax.axis_size("col")
    qscale = (1.0 / jnp.sqrt(query_degree.astype(jnp.float32))).reshape(query_tiles, 1, side)
    pscale = (1.0 / jnp.sqrt(product_degree.astype(jnp.float32))).reshape(product_tiles, 1, side)
    row_at = lax.axis_index("row")
    col_at = lax.axis_index("col")
    share = panel.shape[1]
    block = product_degree.shape[0]
    q_per_tile = n_col // query_tiles
    p_per_tile = n_row // product_tiles
    my_qscale = lax.dynamic_index_in_dim(qscale, col_at // q_per_tile, keepdims=False)
    my_pscale = lax.dynamic_index_in_dim(pscale, row_at // p_per_tile, keepdims=False)
    root_count = math.sqrt(product_degree.shape[0] * n_col)

    scaled_tiles = staged(panel, "row", ROW_FACTORS, "gather", 0,
                          scale=product_degree.reshape(n_row, share), epilogue=_panel_epilogue,
                          out_dtype=jnp.bfloat16, tiled=(product_tiles, width, side))
    per_tile = side // share
    for iteration in range(ITERS):
        if iteration:
            partial_sum = tile_products(slot_ids, live_count, None, tile_set, query_tiles, True,
                                        lift=(inverse, lifted_tiles, pscale))
        else:
            partial_sum = tile_products(slot_ids, live_count, scaled_tiles, tile_set, query_tiles, True)
        query_tiles_panel = staged(
            partial_sum.reshape(n_col, width // q_per_tile, side), "col", QUERY_FACTORS, "reduce", 1,
            scale=my_qscale, epilogue=_query_epilogue, out_dtype=jnp.bfloat16,
        ).reshape(query_tiles, width, side)
        product_partial = tile_products(
            slot_ids, live_count, query_tiles_panel, tile_set, product_tiles, False
        )
        lifted_pieces, inverse = product_gram(
            product_partial.reshape(n_row, width // p_per_tile, side), my_pscale, ROW_FACTORS,
            GRAM_FACTORS, 2, width,
        )
        lifted_tiles = lifted_pieces.reshape(product_tiles, width, side)
    my_tile = lax.dynamic_index_in_dim(lifted_tiles, row_at // per_tile, keepdims=False)
    my_lifted = lax.dynamic_slice_in_dim(my_tile, (row_at % per_tile) * share, share, axis=1)
    return jnp.einsum("rs,si->ri", inverse, my_lifted, precision=HIGH) * root_count


def solution(mesh):
    in_specs = (
        P("row", "col", None, None, None),
        P("row", "col", None, None),
        P("row", "col"),
        P("row"),
        P("col"),
        P(None, ("col", "row")),
    )
    out_specs = P(None, ("col", "row"))
    return jax.shard_map(shards, mesh=mesh, in_specs=in_specs, out_specs=out_specs, check_vma=False)
```

```python
import functools
import math

import jax
import jax.numpy as jnp
from jax import lax
from jax.experimental import pallas as pl
from jax.experimental.pallas import tpu as pltpu
from jax.sharding import PartitionSpec as P

ITERS = 2


HIGH = lax.Precision.HIGHEST

AXES = ("row", "col")


def _device(axis, peer):
    if axis == "row":
        return (peer, lax.axis_index("col"))
    return (lax.axis_index("row"), peer)


class _Plan:
    def __init__(self, axis, factors):
        self.axis = axis
        self.factors = tuple(factors)
        self.stages = len(factors)
        self.me = lax.axis_index(axis)
        self.strides = [math.prod(factors[:s]) for s in range(self.stages)]
        self.mine = [lax.rem(lax.div(self.me, self.strides[s]), factors[s])
                     for s in range(self.stages)]

    def peer(self, s, d):
        return _device(self.axis, self.me + (d - self.mine[s]) * self.strides[s])

    def other(self, s, k):
        return lax.rem(self.mine[s] + k, self.factors[s])

    def peers(self):
        return [self.peer(s, self.other(s, k)) for s in range(self.stages)
                for k in range(1, self.factors[s])]


def _barrier(plans):
    barrier = pltpu.get_barrier_semaphore()
    count = 0
    for plan in plans:
        for dev in plan.peers():
            pl.semaphore_signal(barrier, inc=1, device_id=dev, device_id_type=pl.DeviceIdType.MESH)
            count += 1
    pl.semaphore_wait(barrier, count)


def _exchange(plan, sems, kind, s, src_of, dst_of, pending):
    copies = []
    mine = plan.mine[s]
    for k in range(1, plan.factors[s]):
        d = plan.other(s, k)
        c = pltpu.make_async_remote_copy(
            src_ref=src_of(d), dst_ref=dst_of(mine),
            send_sem=sems.at[kind, s, d], recv_sem=sems.at[kind + 1, s, mine],
            device_id=plan.peer(s, d), device_id_type=pl.DeviceIdType.MESH,
        )
        c.start()
        copies.append((d, c))
    pending.extend(c for _, c in copies)
    for d, c in copies:
        pltpu.make_async_remote_copy(
            src_ref=src_of(d), dst_ref=dst_of(d),
            send_sem=sems.at[kind, s, d], recv_sem=sems.at[kind + 1, s, d],
            device_id=plan.peer(s, d), device_id_type=pl.DeviceIdType.MESH,
        ).wait_recv()


def _reduce_scatter(plan, sems, kind, x_ref, rbufs, pending):
    cur = x_ref
    for s in range(plan.stages):
        lead = plan.stages - 1 - s

        def src_of(d, cur=cur, lead=lead):
            return cur.at[(slice(None),) * lead + (d,)]

        rb = rbufs[s]
        _exchange(plan, sems, kind, s, src_of, lambda d, rb=rb: rb.at[d], pending)
        total = cur[(slice(None),) * lead + (plan.mine[s],)]
        for k in range(1, plan.factors[s]):
            total = total + rb[plan.other(s, k)]
        rb[plan.mine[s]] = total
        cur = rb.at[plan.mine[s]]
    return cur


def _all_gather(plan, sems, kind, gbuf, own, pending):
    mine = plan.mine
    gbuf[tuple(mine[::-1])] = own.astype(gbuf.dtype)
    for s in reversed(range(plan.stages)):
        lead = plan.stages - 1 - s

        def view(d, s=s, lead=lead):
            return gbuf.at[(slice(None),) * lead + (d,) + tuple(mine[s - 1::-1] if s else ())]

        _exchange(plan, sems, kind, s, lambda d, s=s: view(mine[s]), view, pending)


def _sum(plan, sems, kind, value, rbufs, pending):
    for s in range(plan.stages):
        rb = rbufs[s]
        rb[plan.mine[s]] = value
        src = rb.at[plan.mine[s]]
        _exchange(plan, sems, kind, s, lambda d, src=src: src, lambda d, rb=rb: rb.at[d], pending)
        value = rb[0]
        for d in range(1, plan.factors[s]):
            value = value + rb[d]
    return value


def _staged_kernel(*refs, axis, factors, mode, has_scale, epilogue):
    if has_scale:
        x_ref, s_ref, y_ref = refs[:3]
        rest = refs[3:]
    else:
        x_ref, y_ref = refs[:2]
        s_ref = None
        rest = refs[2:]
    plan = _Plan(axis, factors)
    n_rs = plan.stages if mode in ("reduce", "sum") else 0
    rbufs = rest[:n_rs]
    gbuf = rest[n_rs] if mode != "sum" else None
    sems = rest[-1]
    _barrier([plan])
    pending = []
    if mode == "sum":
        y_ref[...] = _sum(plan, sems, 0, x_ref[...], rbufs, pending)
    else:
        if mode == "reduce":
            if s_ref.shape[0] > 1:
                s_ref = s_ref.at[pl.ds(plan.me // (math.prod(factors) // s_ref.shape[0]), 1)]
            own = epilogue(_reduce_scatter(plan, sems, 0, x_ref, rbufs, pending)[...], s_ref)
        elif epilogue is not None:
            own = epilogue(x_ref[...], s_ref.at[pl.ds(plan.me, 1)])
        else:
            own = x_ref[...]
        _all_gather(plan, sems, 2, gbuf, own, pending)
        if mode == "gather" and len(y_ref.shape) == 3:
            n = math.prod(factors)
            share = own.shape[-1]
            per = y_ref.shape[-1] // share
            for j in range(n):
                y_ref[j // per, :, pl.ds((j % per) * share, share)] = gbuf[_digits(j, factors)]
        else:
            y_ref[...] = gbuf[...]
    for c in pending:
        c.wait_send()


def _digits(j, factors):
    return tuple((j // math.prod(factors[:s])) % factors[s] for s in reversed(range(len(factors))))


def _product_gram_kernel(x_ref, s_ref, y_ref, g_ref, *rest, row_factors, col_factors):
    rows = _Plan("row", row_factors)
    cols = _Plan("col", col_factors)
    rbufs = rest[:rows.stages]
    gbuf = rest[rows.stages]
    cbufs = rest[rows.stages + 1:rows.stages + 1 + cols.stages]
    sems = rest[-1]
    _barrier([rows, cols])
    pending = []
    own = _reduce_scatter(rows, sems, 0, x_ref, rbufs, pending)[...] * s_ref[...]
    _all_gather(rows, sems, 2, gbuf, own, pending)
    y_ref[...] = gbuf[...]
    n = math.prod(row_factors)
    per = y_ref.shape[-2]
    width = g_ref.shape[0]
    gram = None
    for p in range(n * per // width):
        parts = [y_ref[_digits(p * width // per + i, row_factors)] for i in range(width // per)]
        block = jnp.concatenate(parts, axis=0)
        padded = jnp.concatenate([block, jnp.zeros_like(block)], axis=0)
        term = lax.dot_general(block, padded, (((1,), (1,)), ((), ())), precision=HIGH,
                               preferred_element_type=jnp.float32)
        gram = term if gram is None else gram + term
    total = _sum(cols, sems, 4, gram, cbufs, pending)
    row = lax.broadcasted_iota(jnp.int32, total.shape, 0)
    lane = lax.broadcasted_iota(jnp.int32, total.shape, 1)
    g_ref[...] = _eliminate(total + jnp.where(lane == row + width, 1.0, 0.0))
    for c in pending:
        c.wait_send()


def product_gram(x, scale, row_factors, col_factors, cid, width):
    n = math.prod(row_factors)
    chunk = x.shape[1:]
    x = x.reshape(tuple(reversed(row_factors)) + chunk)
    scratch = []
    for s in range(len(row_factors)):
        scratch.append(pltpu.VMEM((row_factors[s],) + tuple(reversed(row_factors[s + 1:])) + chunk,
                                  jnp.float32))
    scratch.append(pltpu.VMEM(tuple(reversed(row_factors)) + chunk, jnp.float32))
    for s in range(len(col_factors)):
        scratch.append(pltpu.VMEM((col_factors[s], width, 2 * width), jnp.float32))
    scratch.append(pltpu.SemaphoreType.DMA((6, max(len(row_factors), len(col_factors)),
                                            max(row_factors + col_factors))))
    nbytes = n * math.prod(chunk) * 4
    y, g = pl.pallas_call(
        functools.partial(_product_gram_kernel, row_factors=tuple(row_factors),
                          col_factors=tuple(col_factors)),
        out_shape=(jax.ShapeDtypeStruct(tuple(reversed(row_factors)) + chunk, jnp.float32),
                   jax.ShapeDtypeStruct((width, 2 * width), jnp.float32)),
        in_specs=[pl.BlockSpec(memory_space=pltpu.VMEM)] * 2,
        out_specs=(pl.BlockSpec(memory_space=pltpu.VMEM), pl.BlockSpec(memory_space=pltpu.VMEM)),
        scratch_shapes=scratch,
        compiler_params=pltpu.CompilerParams(collective_id=cid, has_side_effects=True),
        cost_estimate=pl.CostEstimate(flops=0, transcendentals=0, bytes_accessed=2 * nbytes),
    )(x, scale)
    return y.reshape((n,) + chunk), g[:, width:]


def staged(x, axis, factors, mode, cid, scale=None, epilogue=None, out_dtype=None, tiled=None):
    n = math.prod(factors)
    stages = len(factors)
    out_dtype = out_dtype or x.dtype
    if mode == "reduce":
        chunk = x.shape[1:]
        x = x.reshape(tuple(reversed(factors)) + chunk)
    else:
        chunk = x.shape
    scratch = []
    if mode in ("reduce", "sum"):
        for s in range(stages):
            rest = tuple(reversed(factors[s + 1:])) if mode == "reduce" else ()
            scratch.append(pltpu.VMEM((factors[s],) + rest + chunk, jnp.float32))
    if mode != "sum":
        scratch.append(pltpu.VMEM(tuple(reversed(factors)) + chunk, out_dtype))
    scratch.append(pltpu.SemaphoreType.DMA((4, stages, max(factors))))
    if mode == "sum":
        out_shape = chunk
    elif tiled is not None:
        out_shape = tiled
    else:
        out_shape = tuple(reversed(factors)) + chunk
    args = (x,) if scale is None else (x, scale)
    nbytes = n * math.prod(chunk) * 4
    y = pl.pallas_call(
        functools.partial(_staged_kernel, axis=axis, factors=tuple(factors), mode=mode,
                          has_scale=scale is not None, epilogue=epilogue),
        out_shape=jax.ShapeDtypeStruct(out_shape, out_dtype),
        in_specs=[pl.BlockSpec(memory_space=pltpu.VMEM)] * len(args),
        out_specs=pl.BlockSpec(memory_space=pltpu.VMEM),
        scratch_shapes=scratch,
        compiler_params=pltpu.CompilerParams(collective_id=cid, has_side_effects=True),
        cost_estimate=pl.CostEstimate(flops=0, transcendentals=0, bytes_accessed=2 * nbytes),
    )(*args)
    if mode == "sum" or tiled is not None:
        return y
    return y.reshape((n,) + chunk)


QUERY_FACTORS = (2, 4, 4)
GRAM_FACTORS = (4, 8)
ROW_FACTORS = (4, 4)


def _query_epilogue(total, degree_ref):
    return (total * (1.0 / jnp.sqrt(degree_ref[...].astype(jnp.float32)))).astype(jnp.bfloat16)


def _panel_epilogue(panel, degree_ref):
    scale = 1.0 / jnp.sqrt(degree_ref[...].astype(jnp.float32))
    return (panel * scale).astype(jnp.bfloat16)


def _product_epilogue(total, s_ref):
    return total * s_ref[...]


GROUP = 8


def _products_kernel(*refs, forward, lift):
    if lift:
        ids_ref, count_ref, inv_ref, lifted_ref, scale_ref, tiles_hbm, out_ref, tiles, sems, src_ref = refs
    else:
        ids_ref, count_ref, src_ref, tiles_hbm, out_ref, tiles, sems = refs
    slots = tiles.shape[0]
    groups = slots // GROUP

    def fetch(g):
        return pltpu.make_async_copy(
            tiles_hbm.at[pl.ds(g * GROUP, GROUP)], tiles.at[pl.ds(g * GROUP, GROUP)], sems.at[g]
        )

    for g in range(groups):
        fetch(g).start()
    if lift:
        inv = inv_ref[...]
        for p in range(src_ref.shape[0]):
            current = jnp.dot(inv, lifted_ref[p], precision=HIGH, preferred_element_type=jnp.float32)
            src_ref[p] = (current * scale_ref[p]).astype(src_ref.dtype)
    out_ref[...] = jnp.zeros_like(out_ref)
    src_row, dst_row = (1, 0) if forward else (0, 1)
    count = count_ref[0]
    for g in range(groups):
        fetch(g).wait()
        ys = []
        for k in range(g * GROUP, (g + 1) * GROUP):
            x = src_ref[ids_ref[src_row, k]]
            t = tiles[k]
            if forward:
                y = lax.dot_general(x, t, (((1,), (1,)), ((), ())),
                                    preferred_element_type=jnp.float32)
            else:
                y = jnp.dot(x, t, preferred_element_type=jnp.float32)
            ys.append(jnp.where(k < count, y, 0.0))
        for k, y in zip(range(g * GROUP, (g + 1) * GROUP), ys):
            d = ids_ref[dst_row, k]
            out_ref[d] = out_ref[d] + y


def tile_products(slot_ids, live_count, src, tile_set, blocks, forward, lift=None):
    slots, side, _ = tile_set.shape
    width = src.shape[1] if lift is None else lift[1].shape[1]
    scratch = [pltpu.VMEM(tile_set.shape, tile_set.dtype), pltpu.SemaphoreType.DMA((slots // GROUP,))]
    if lift is None:
        operands = (src,)
    else:
        operands = lift
        scratch.append(pltpu.VMEM(lift[1].shape, jnp.bfloat16))
    vmem = pl.BlockSpec(memory_space=pltpu.VMEM)
    smem = pl.BlockSpec(memory_space=pltpu.SMEM)
    return pl.pallas_call(
        functools.partial(_products_kernel, forward=forward, lift=lift is not None),
        out_shape=jax.ShapeDtypeStruct((blocks, width, side), jnp.float32),
        in_specs=[smem, smem] + [vmem] * len(operands) + [pl.BlockSpec(memory_space=pl.ANY)],
        out_specs=vmem,
        scratch_shapes=scratch,
        cost_estimate=pl.CostEstimate(
            flops=2 * slots * width * side * side, transcendentals=0,
            bytes_accessed=slots * side * side * 2 + blocks * width * side * 6,
        ),
    )(slot_ids, live_count.reshape(1), *operands, tile_set)


def _eliminate(m):
    rows, cols = m.shape
    row = lax.broadcasted_iota(jnp.int32, (rows, cols), 0)
    lane = lax.broadcasted_iota(jnp.int32, (rows, cols), 1)

    def step(j, m):
        pivot_row = jnp.sum(jnp.where(row == j, m, 0.0), axis=0, keepdims=True)
        pivot = jnp.sum(jnp.where(lane[:1] == j, pivot_row, 0.0), axis=1, keepdims=True)
        inv_root = 1.0 / jnp.sqrt(pivot)
        scaled_row = pivot_row * inv_root
        column = jnp.sum(jnp.where(lane == j, m, 0.0), axis=1, keepdims=True) * inv_root
        return jnp.where(row == j, scaled_row, jnp.where(row > j, m - column * scaled_row, m))

    return lax.fori_loop(0, rows, step, m, unroll=2)


def _lower_inverse_kernel(m_ref, out_ref):
    out_ref[...] = _eliminate(m_ref[...])


def lower_inverse(gram):
    width = gram.shape[0]
    augmented = jnp.concatenate([gram, jnp.eye(width, dtype=gram.dtype)], axis=1)
    reduced = pl.pallas_call(
        _lower_inverse_kernel,
        out_shape=jax.ShapeDtypeStruct(augmented.shape, augmented.dtype),
        in_specs=[pl.BlockSpec(memory_space=pltpu.VMEM)],
        out_specs=pl.BlockSpec(memory_space=pltpu.VMEM),
    )(augmented)
    return reduced[:, width:]


def lower_inverse_native(gram):
    lower = lax.linalg.cholesky(gram, symmetrize_input=False)
    eye = jnp.eye(gram.shape[0], dtype=gram.dtype)
    return lax.linalg.triangular_solve(lower, eye, left_side=True, lower=True)


def shards(tiles, tile_ids, tile_count, query_degree, product_degree, panel):
    tile_set = tiles[0, 0]
    slot_ids = tile_ids[0, 0]
    live_count = tile_count[0, 0]
    side = tile_set.shape[1]
    width = panel.shape[0]
    query_tiles = query_degree.shape[0] // side
    product_tiles = product_degree.shape[0] // side
    n_row = lax.axis_size("row")
    n_col = lax.axis_size("col")
    qscale = (1.0 / jnp.sqrt(query_degree.astype(jnp.float32))).reshape(query_tiles, 1, side)
    pscale = (1.0 / jnp.sqrt(product_degree.astype(jnp.float32))).reshape(product_tiles, 1, side)
    row_at = lax.axis_index("row")
    col_at = lax.axis_index("col")
    share = panel.shape[1]
    block = product_degree.shape[0]
    q_per_tile = n_col // query_tiles
    p_per_tile = n_row // product_tiles
    my_qscale = lax.dynamic_index_in_dim(qscale, col_at // q_per_tile, keepdims=False)
    my_pscale = lax.dynamic_index_in_dim(pscale, row_at // p_per_tile, keepdims=False)
    root_count = math.sqrt(product_degree.shape[0] * n_col)

    scaled_tiles = staged(panel, "row", ROW_FACTORS, "gather", 0,
                          scale=product_degree.reshape(n_row, share), epilogue=_panel_epilogue,
                          out_dtype=jnp.bfloat16, tiled=(product_tiles, width, side))
    per_tile = side // share
    for iteration in range(ITERS):
        if iteration:
            partial_sum = tile_products(slot_ids, live_count, None, tile_set, query_tiles, True,
                                        lift=(inverse, lifted_tiles, pscale))
        else:
            partial_sum = tile_products(slot_ids, live_count, scaled_tiles, tile_set, query_tiles, True)
        query_tiles_panel = staged(
            partial_sum.reshape(n_col, width // q_per_tile, side), "col", QUERY_FACTORS, "reduce", 1,
            scale=query_degree.reshape(query_tiles, side), epilogue=_query_epilogue,
            out_dtype=jnp.bfloat16,
        ).reshape(query_tiles, width, side)
        product_partial = tile_products(
            slot_ids, live_count, query_tiles_panel, tile_set, product_tiles, False
        )
        lifted_pieces, inverse = product_gram(
            product_partial.reshape(n_row, width // p_per_tile, side), my_pscale, ROW_FACTORS,
            GRAM_FACTORS, 2, width,
        )
        lifted_tiles = lifted_pieces.reshape(product_tiles, width, side)
    my_tile = lax.dynamic_index_in_dim(lifted_tiles, row_at // per_tile, keepdims=False)
    my_lifted = lax.dynamic_slice_in_dim(my_tile, (row_at % per_tile) * share, share, axis=1)
    return jnp.einsum("rs,si->ri", inverse, my_lifted, precision=HIGH) * root_count


def solution(mesh):
    in_specs = (
        P("row", "col", None, None, None),
        P("row", "col", None, None),
        P("row", "col"),
        P("row"),
        P("col"),
        P(None, ("col", "row")),
    )
    out_specs = P(None, ("col", "row"))
    return jax.shard_map(shards, mesh=mesh, in_specs=in_specs, out_specs=out_specs, check_vma=False)
```

```python
import functools
import math

import jax
import jax.numpy as jnp
from jax import lax
from jax.experimental import pallas as pl
from jax.experimental.pallas import tpu as pltpu
from jax.sharding import PartitionSpec as P

ITERS = 2


HIGH = lax.Precision.HIGHEST

AXES = ("row", "col")


def _device(axis, peer):
    if axis == "row":
        return (peer, lax.axis_index("col"))
    return (lax.axis_index("row"), peer)


class _Plan:
    def __init__(self, axis, factors):
        self.axis = axis
        self.factors = tuple(factors)
        self.stages = len(factors)
        self.me = lax.axis_index(axis)
        self.strides = [math.prod(factors[:s]) for s in range(self.stages)]
        self.mine = [lax.rem(lax.div(self.me, self.strides[s]), factors[s])
                     for s in range(self.stages)]

    def peer(self, s, d):
        return _device(self.axis, self.me + (d - self.mine[s]) * self.strides[s])

    def other(self, s, k):
        return lax.rem(self.mine[s] + k, self.factors[s])

    def peers(self):
        return [self.peer(s, self.other(s, k)) for s in range(self.stages)
                for k in range(1, self.factors[s])]


def _barrier(plans):
    barrier = pltpu.get_barrier_semaphore()
    count = 0
    for plan in plans:
        for dev in plan.peers():
            pl.semaphore_signal(barrier, inc=1, device_id=dev, device_id_type=pl.DeviceIdType.MESH)
            count += 1
    pl.semaphore_wait(barrier, count)


def _exchange(plan, sems, kind, s, src_of, dst_of, pending):
    copies = []
    mine = plan.mine[s]
    for k in range(1, plan.factors[s]):
        d = plan.other(s, k)
        c = pltpu.make_async_remote_copy(
            src_ref=src_of(d), dst_ref=dst_of(mine),
            send_sem=sems.at[kind, s, d], recv_sem=sems.at[kind + 1, s, mine],
            device_id=plan.peer(s, d), device_id_type=pl.DeviceIdType.MESH,
        )
        c.start()
        copies.append((d, c))
    pending.extend(c for _, c in copies)
    for d, c in copies:
        pltpu.make_async_remote_copy(
            src_ref=src_of(d), dst_ref=dst_of(d),
            send_sem=sems.at[kind, s, d], recv_sem=sems.at[kind + 1, s, d],
            device_id=plan.peer(s, d), device_id_type=pl.DeviceIdType.MESH,
        ).wait_recv()


def _reduce_scatter(plan, sems, kind, x_ref, rbufs, pending):
    cur = x_ref
    for s in range(plan.stages):
        lead = plan.stages - 1 - s

        def src_of(d, cur=cur, lead=lead):
            return cur.at[(slice(None),) * lead + (d,)]

        rb = rbufs[s]
        _exchange(plan, sems, kind, s, src_of, lambda d, rb=rb: rb.at[d], pending)
        total = cur[(slice(None),) * lead + (plan.mine[s],)]
        for k in range(1, plan.factors[s]):
            total = total + rb[plan.other(s, k)]
        rb[plan.mine[s]] = total
        cur = rb.at[plan.mine[s]]
    return cur


def _all_gather(plan, sems, kind, gbuf, own, pending):
    mine = plan.mine
    gbuf[tuple(mine[::-1])] = own.astype(gbuf.dtype)
    for s in reversed(range(plan.stages)):
        lead = plan.stages - 1 - s

        def view(d, s=s, lead=lead):
            return gbuf.at[(slice(None),) * lead + (d,) + tuple(mine[s - 1::-1] if s else ())]

        _exchange(plan, sems, kind, s, lambda d, s=s: view(mine[s]), view, pending)


def _sum(plan, sems, kind, value, rbufs, pending):
    for s in range(plan.stages):
        rb = rbufs[s]
        rb[plan.mine[s]] = value
        src = rb.at[plan.mine[s]]
        _exchange(plan, sems, kind, s, lambda d, src=src: src, lambda d, rb=rb: rb.at[d], pending)
        value = rb[0]
        for d in range(1, plan.factors[s]):
            value = value + rb[d]
    return value


def _staged_kernel(*refs, axis, factors, mode, has_scale, epilogue):
    if has_scale:
        x_ref, s_ref, y_ref = refs[:3]
        rest = refs[3:]
    else:
        x_ref, y_ref = refs[:2]
        s_ref = None
        rest = refs[2:]
    plan = _Plan(axis, factors)
    n_rs = plan.stages if mode in ("reduce", "sum") else 0
    rbufs = rest[:n_rs]
    gbuf = rest[n_rs] if mode != "sum" else None
    sems = rest[-1]
    _barrier([plan])
    pending = []
    if mode == "sum":
        y_ref[...] = _sum(plan, sems, 0, x_ref[...], rbufs, pending)
    else:
        if mode == "reduce":
            if s_ref.shape[0] > 1:
                s_ref = s_ref.at[pl.ds(plan.me // (math.prod(factors) // s_ref.shape[0]), 1)]
            own = epilogue(_reduce_scatter(plan, sems, 0, x_ref, rbufs, pending)[...], s_ref)
        elif epilogue is not None:
            own = epilogue(x_ref[...], s_ref.at[pl.ds(plan.me, 1)])
        else:
            own = x_ref[...]
        _all_gather(plan, sems, 2, gbuf, own, pending)
        if mode == "gather" and len(y_ref.shape) == 3:
            n = math.prod(factors)
            share = own.shape[-1]
            per = y_ref.shape[-1] // share
            for j in range(n):
                y_ref[j // per, :, pl.ds((j % per) * share, share)] = gbuf[_digits(j, factors)]
        else:
            y_ref[...] = gbuf[...]
    for c in pending:
        c.wait_send()


def _digits(j, factors):
    return tuple((j // math.prod(factors[:s])) % factors[s] for s in reversed(range(len(factors))))


def _product_gram_kernel(x_ref, s_ref, y_ref, g_ref, *rest, row_factors, col_factors):
    rows = _Plan("row", row_factors)
    cols = _Plan("col", col_factors)
    rbufs = rest[:rows.stages]
    gbuf = rest[rows.stages]
    cbufs = rest[rows.stages + 1:rows.stages + 1 + cols.stages]
    sems = rest[-1]
    _barrier([rows, cols])
    pending = []
    degree = s_ref[pl.ds(rows.me // (math.prod(row_factors) // s_ref.shape[0]), 1)]
    scale = 1.0 / jnp.sqrt(degree.astype(jnp.float32))
    own = _reduce_scatter(rows, sems, 0, x_ref, rbufs, pending)[...] * scale
    _all_gather(rows, sems, 2, gbuf, own, pending)
    y_ref[...] = gbuf[...]
    n = math.prod(row_factors)
    per = y_ref.shape[-2]
    width = g_ref.shape[0]
    gram = None
    for p in range(n * per // width):
        parts = [y_ref[_digits(p * width // per + i, row_factors)] for i in range(width // per)]
        block = jnp.concatenate(parts, axis=0)
        padded = jnp.concatenate([block, jnp.zeros_like(block)], axis=0)
        term = lax.dot_general(block, padded, (((1,), (1,)), ((), ())), precision=HIGH,
                               preferred_element_type=jnp.float32)
        gram = term if gram is None else gram + term
    total = _sum(cols, sems, 4, gram, cbufs, pending)
    row = lax.broadcasted_iota(jnp.int32, total.shape, 0)
    lane = lax.broadcasted_iota(jnp.int32, total.shape, 1)
    g_ref[...] = _eliminate(total + jnp.where(lane == row + width, 1.0, 0.0))
    for c in pending:
        c.wait_send()


def product_gram(x, scale, row_factors, col_factors, cid, width):
    n = math.prod(row_factors)
    chunk = x.shape[1:]
    x = x.reshape(tuple(reversed(row_factors)) + chunk)
    scratch = []
    for s in range(len(row_factors)):
        scratch.append(pltpu.VMEM((row_factors[s],) + tuple(reversed(row_factors[s + 1:])) + chunk,
                                  jnp.float32))
    scratch.append(pltpu.VMEM(tuple(reversed(row_factors)) + chunk, jnp.float32))
    for s in range(len(col_factors)):
        scratch.append(pltpu.VMEM((col_factors[s], width, 2 * width), jnp.float32))
    scratch.append(pltpu.SemaphoreType.DMA((6, max(len(row_factors), len(col_factors)),
                                            max(row_factors + col_factors))))
    nbytes = n * math.prod(chunk) * 4
    y, g = pl.pallas_call(
        functools.partial(_product_gram_kernel, row_factors=tuple(row_factors),
                          col_factors=tuple(col_factors)),
        out_shape=(jax.ShapeDtypeStruct(tuple(reversed(row_factors)) + chunk, jnp.float32),
                   jax.ShapeDtypeStruct((width, 2 * width), jnp.float32)),
        in_specs=[pl.BlockSpec(memory_space=pltpu.VMEM)] * 2,
        out_specs=(pl.BlockSpec(memory_space=pltpu.VMEM), pl.BlockSpec(memory_space=pltpu.VMEM)),
        scratch_shapes=scratch,
        compiler_params=pltpu.CompilerParams(collective_id=cid, has_side_effects=True),
        cost_estimate=pl.CostEstimate(flops=0, transcendentals=0, bytes_accessed=2 * nbytes),
    )(x, scale)
    return y.reshape((n,) + chunk), g[:, width:]


def staged(x, axis, factors, mode, cid, scale=None, epilogue=None, out_dtype=None, tiled=None):
    n = math.prod(factors)
    stages = len(factors)
    out_dtype = out_dtype or x.dtype
    if mode == "reduce":
        chunk = x.shape[1:]
        x = x.reshape(tuple(reversed(factors)) + chunk)
    else:
        chunk = x.shape
    scratch = []
    if mode in ("reduce", "sum"):
        for s in range(stages):
            rest = tuple(reversed(factors[s + 1:])) if mode == "reduce" else ()
            scratch.append(pltpu.VMEM((factors[s],) + rest + chunk, jnp.float32))
    if mode != "sum":
        scratch.append(pltpu.VMEM(tuple(reversed(factors)) + chunk, out_dtype))
    scratch.append(pltpu.SemaphoreType.DMA((4, stages, max(factors))))
    if mode == "sum":
        out_shape = chunk
    elif tiled is not None:
        out_shape = tiled
    else:
        out_shape = tuple(reversed(factors)) + chunk
    args = (x,) if scale is None else (x, scale)
    nbytes = n * math.prod(chunk) * 4
    y = pl.pallas_call(
        functools.partial(_staged_kernel, axis=axis, factors=tuple(factors), mode=mode,
                          has_scale=scale is not None, epilogue=epilogue),
        out_shape=jax.ShapeDtypeStruct(out_shape, out_dtype),
        in_specs=[pl.BlockSpec(memory_space=pltpu.VMEM)] * len(args),
        out_specs=pl.BlockSpec(memory_space=pltpu.VMEM),
        scratch_shapes=scratch,
        compiler_params=pltpu.CompilerParams(collective_id=cid, has_side_effects=True),
        cost_estimate=pl.CostEstimate(flops=0, transcendentals=0, bytes_accessed=2 * nbytes),
    )(*args)
    if mode == "sum" or tiled is not None:
        return y
    return y.reshape((n,) + chunk)


QUERY_FACTORS = (2, 4, 4)
GRAM_FACTORS = (4, 8)
ROW_FACTORS = (4, 4)


def _query_epilogue(total, degree_ref):
    return (total * (1.0 / jnp.sqrt(degree_ref[...].astype(jnp.float32)))).astype(jnp.bfloat16)


def _panel_epilogue(panel, degree_ref):
    scale = 1.0 / jnp.sqrt(degree_ref[...].astype(jnp.float32))
    return (panel * scale).astype(jnp.bfloat16)


def _product_epilogue(total, s_ref):
    return total * s_ref[...]


GROUP = 8


def _products_kernel(*refs, forward, lift):
    if lift:
        ids_ref, count_ref, inv_ref, lifted_ref, scale_ref, tiles_hbm, out_ref, tiles, sems, src_ref = refs
    else:
        ids_ref, count_ref, src_ref, tiles_hbm, out_ref, tiles, sems = refs
    slots = tiles.shape[0]
    groups = slots // GROUP

    def fetch(g):
        return pltpu.make_async_copy(
            tiles_hbm.at[pl.ds(g * GROUP, GROUP)], tiles.at[pl.ds(g * GROUP, GROUP)], sems.at[g]
        )

    for g in range(groups):
        fetch(g).start()
    if lift:
        inv = inv_ref[...]
        for p in range(src_ref.shape[0]):
            current = jnp.dot(inv, lifted_ref[p], precision=HIGH, preferred_element_type=jnp.float32)
            src_ref[p] = (current * scale_ref[p]).astype(src_ref.dtype)
    out_ref[...] = jnp.zeros_like(out_ref)
    src_row, dst_row = (1, 0) if forward else (0, 1)
    count = count_ref[0]
    for g in range(groups):
        fetch(g).wait()
        ys = []
        for k in range(g * GROUP, (g + 1) * GROUP):
            x = src_ref[ids_ref[src_row, k]]
            t = tiles[k]
            if forward:
                y = lax.dot_general(x, t, (((1,), (1,)), ((), ())),
                                    preferred_element_type=jnp.float32)
            else:
                y = jnp.dot(x, t, preferred_element_type=jnp.float32)
            ys.append(jnp.where(k < count, y, 0.0))
        for k, y in zip(range(g * GROUP, (g + 1) * GROUP), ys):
            d = ids_ref[dst_row, k]
            out_ref[d] = out_ref[d] + y


def tile_products(slot_ids, live_count, src, tile_set, blocks, forward, lift=None):
    slots, side, _ = tile_set.shape
    width = src.shape[1] if lift is None else lift[1].shape[1]
    scratch = [pltpu.VMEM(tile_set.shape, tile_set.dtype), pltpu.SemaphoreType.DMA((slots // GROUP,))]
    if lift is None:
        operands = (src,)
    else:
        operands = lift
        scratch.append(pltpu.VMEM(lift[1].shape, jnp.bfloat16))
    vmem = pl.BlockSpec(memory_space=pltpu.VMEM)
    smem = pl.BlockSpec(memory_space=pltpu.SMEM)
    return pl.pallas_call(
        functools.partial(_products_kernel, forward=forward, lift=lift is not None),
        out_shape=jax.ShapeDtypeStruct((blocks, width, side), jnp.float32),
        in_specs=[smem, smem] + [vmem] * len(operands) + [pl.BlockSpec(memory_space=pl.ANY)],
        out_specs=vmem,
        scratch_shapes=scratch,
        cost_estimate=pl.CostEstimate(
            flops=2 * slots * width * side * side, transcendentals=0,
            bytes_accessed=slots * side * side * 2 + blocks * width * side * 6,
        ),
    )(slot_ids, live_count.reshape(1), *operands, tile_set)


def _eliminate(m):
    rows, cols = m.shape
    row = lax.broadcasted_iota(jnp.int32, (rows, cols), 0)
    lane = lax.broadcasted_iota(jnp.int32, (rows, cols), 1)

    def step(j, m):
        pivot_row = jnp.sum(jnp.where(row == j, m, 0.0), axis=0, keepdims=True)
        pivot = jnp.sum(jnp.where(lane[:1] == j, pivot_row, 0.0), axis=1, keepdims=True)
        inv_root = 1.0 / jnp.sqrt(pivot)
        scaled_row = pivot_row * inv_root
        column = jnp.sum(jnp.where(lane == j, m, 0.0), axis=1, keepdims=True) * inv_root
        return jnp.where(row == j, scaled_row, jnp.where(row > j, m - column * scaled_row, m))

    return lax.fori_loop(0, rows, step, m, unroll=2)


def _lower_inverse_kernel(m_ref, out_ref):
    out_ref[...] = _eliminate(m_ref[...])


def lower_inverse(gram):
    width = gram.shape[0]
    augmented = jnp.concatenate([gram, jnp.eye(width, dtype=gram.dtype)], axis=1)
    reduced = pl.pallas_call(
        _lower_inverse_kernel,
        out_shape=jax.ShapeDtypeStruct(augmented.shape, augmented.dtype),
        in_specs=[pl.BlockSpec(memory_space=pltpu.VMEM)],
        out_specs=pl.BlockSpec(memory_space=pltpu.VMEM),
    )(augmented)
    return reduced[:, width:]


def lower_inverse_native(gram):
    lower = lax.linalg.cholesky(gram, symmetrize_input=False)
    eye = jnp.eye(gram.shape[0], dtype=gram.dtype)
    return lax.linalg.triangular_solve(lower, eye, left_side=True, lower=True)


def shards(tiles, tile_ids, tile_count, query_degree, product_degree, panel):
    tile_set = tiles[0, 0]
    slot_ids = tile_ids[0, 0]
    live_count = tile_count[0, 0]
    side = tile_set.shape[1]
    width = panel.shape[0]
    query_tiles = query_degree.shape[0] // side
    product_tiles = product_degree.shape[0] // side
    n_row = lax.axis_size("row")
    n_col = lax.axis_size("col")
    qscale = (1.0 / jnp.sqrt(query_degree.astype(jnp.float32))).reshape(query_tiles, 1, side)
    pscale = (1.0 / jnp.sqrt(product_degree.astype(jnp.float32))).reshape(product_tiles, 1, side)
    row_at = lax.axis_index("row")
    col_at = lax.axis_index("col")
    share = panel.shape[1]
    block = product_degree.shape[0]
    q_per_tile = n_col // query_tiles
    p_per_tile = n_row // product_tiles
    my_qscale = lax.dynamic_index_in_dim(qscale, col_at // q_per_tile, keepdims=False)
    my_pscale = lax.dynamic_index_in_dim(pscale, row_at // p_per_tile, keepdims=False)
    root_count = math.sqrt(product_degree.shape[0] * n_col)

    scaled_tiles = staged(panel, "row", ROW_FACTORS, "gather", 0,
                          scale=product_degree.reshape(n_row, share), epilogue=_panel_epilogue,
                          out_dtype=jnp.bfloat16, tiled=(product_tiles, width, side))
    per_tile = side // share
    for iteration in range(ITERS):
        if iteration:
            partial_sum = tile_products(slot_ids, live_count, None, tile_set, query_tiles, True,
                                        lift=(inverse, lifted_tiles, pscale))
        else:
            partial_sum = tile_products(slot_ids, live_count, scaled_tiles, tile_set, query_tiles, True)
        query_tiles_panel = staged(
            partial_sum.reshape(n_col, width // q_per_tile, side), "col", QUERY_FACTORS, "reduce", 1,
            scale=query_degree.reshape(query_tiles, side), epilogue=_query_epilogue,
            out_dtype=jnp.bfloat16,
        ).reshape(query_tiles, width, side)
        product_partial = tile_products(
            slot_ids, live_count, query_tiles_panel, tile_set, product_tiles, False
        )
        lifted_pieces, inverse = product_gram(
            product_partial.reshape(n_row, width // p_per_tile, side),
            product_degree.reshape(product_tiles, side), ROW_FACTORS,
            GRAM_FACTORS, 2, width,
        )
        lifted_tiles = lifted_pieces.reshape(product_tiles, width, side)
    my_tile = lax.dynamic_index_in_dim(lifted_tiles, row_at // per_tile, keepdims=False)
    my_lifted = lax.dynamic_slice_in_dim(my_tile, (row_at % per_tile) * share, share, axis=1)
    return jnp.einsum("rs,si->ri", inverse, my_lifted, precision=HIGH) * root_count


def solution(mesh):
    in_specs = (
        P("row", "col", None, None, None),
        P("row", "col", None, None),
        P("row", "col"),
        P("row"),
        P("col"),
        P(None, ("col", "row")),
    )
    out_specs = P(None, ("col", "row"))
    return jax.shard_map(shards, mesh=mesh, in_specs=in_specs, out_specs=out_specs, check_vma=False)
```

```python
import functools
import math

import jax
import jax.numpy as jnp
from jax import lax
from jax.experimental import pallas as pl
from jax.experimental.pallas import tpu as pltpu
from jax.sharding import PartitionSpec as P

ITERS = 2


HIGH = lax.Precision.HIGHEST

AXES = ("row", "col")


def _device(axis, peer):
    if axis == "row":
        return (peer, lax.axis_index("col"))
    return (lax.axis_index("row"), peer)


class _Plan:
    def __init__(self, axis, factors):
        self.axis = axis
        self.factors = tuple(factors)
        self.stages = len(factors)
        self.me = lax.axis_index(axis)
        self.strides = [math.prod(factors[:s]) for s in range(self.stages)]
        self.mine = [lax.rem(lax.div(self.me, self.strides[s]), factors[s])
                     for s in range(self.stages)]

    def peer(self, s, d):
        return _device(self.axis, self.me + (d - self.mine[s]) * self.strides[s])

    def other(self, s, k):
        return lax.rem(self.mine[s] + k, self.factors[s])

    def peers(self):
        return [self.peer(s, self.other(s, k)) for s in range(self.stages)
                for k in range(1, self.factors[s])]


def _barrier(plans):
    barrier = pltpu.get_barrier_semaphore()
    count = 0
    for plan in plans:
        for dev in plan.peers():
            pl.semaphore_signal(barrier, inc=1, device_id=dev, device_id_type=pl.DeviceIdType.MESH)
            count += 1
    pl.semaphore_wait(barrier, count)


def _exchange(plan, sems, kind, s, src_of, dst_of, pending):
    copies = []
    mine = plan.mine[s]
    for k in range(1, plan.factors[s]):
        d = plan.other(s, k)
        c = pltpu.make_async_remote_copy(
            src_ref=src_of(d), dst_ref=dst_of(mine),
            send_sem=sems.at[kind, s, d], recv_sem=sems.at[kind + 1, s, mine],
            device_id=plan.peer(s, d), device_id_type=pl.DeviceIdType.MESH,
        )
        c.start()
        copies.append((d, c))
    pending.extend(c for _, c in copies)
    for d, c in copies:
        pltpu.make_async_remote_copy(
            src_ref=src_of(d), dst_ref=dst_of(d),
            send_sem=sems.at[kind, s, d], recv_sem=sems.at[kind + 1, s, d],
            device_id=plan.peer(s, d), device_id_type=pl.DeviceIdType.MESH,
        ).wait_recv()


def _reduce_scatter(plan, sems, kind, x_ref, rbufs, pending):
    cur = x_ref
    for s in range(plan.stages):
        lead = plan.stages - 1 - s

        def src_of(d, cur=cur, lead=lead):
            return cur.at[(slice(None),) * lead + (d,)]

        rb = rbufs[s]
        _exchange(plan, sems, kind, s, src_of, lambda d, rb=rb: rb.at[d], pending)
        total = cur[(slice(None),) * lead + (plan.mine[s],)]
        for k in range(1, plan.factors[s]):
            total = total + rb[plan.other(s, k)]
        rb[plan.mine[s]] = total
        cur = rb.at[plan.mine[s]]
    return cur


def _all_gather(plan, sems, kind, gbuf, own, pending):
    mine = plan.mine
    gbuf[tuple(mine[::-1])] = own.astype(gbuf.dtype)
    for s in reversed(range(plan.stages)):
        lead = plan.stages - 1 - s

        def view(d, s=s, lead=lead):
            return gbuf.at[(slice(None),) * lead + (d,) + tuple(mine[s - 1::-1] if s else ())]

        _exchange(plan, sems, kind, s, lambda d, s=s: view(mine[s]), view, pending)


def _sum(plan, sems, kind, value, rbufs, pending):
    for s in range(plan.stages):
        rb = rbufs[s]
        rb[plan.mine[s]] = value
        src = rb.at[plan.mine[s]]
        _exchange(plan, sems, kind, s, lambda d, src=src: src, lambda d, rb=rb: rb.at[d], pending)
        value = rb[0]
        for d in range(1, plan.factors[s]):
            value = value + rb[d]
    return value


def _staged_kernel(*refs, axis, factors, mode, has_scale, epilogue):
    if has_scale:
        x_ref, s_ref, y_ref = refs[:3]
        rest = refs[3:]
    else:
        x_ref, y_ref = refs[:2]
        s_ref = None
        rest = refs[2:]
    plan = _Plan(axis, factors)
    n_rs = plan.stages if mode in ("reduce", "sum") else 0
    rbufs = rest[:n_rs]
    gbuf = rest[n_rs] if mode != "sum" else None
    sems = rest[-1]
    _barrier([plan])
    pending = []
    if mode == "sum":
        y_ref[...] = _sum(plan, sems, 0, x_ref[...], rbufs, pending)
    else:
        if mode == "reduce":
            if s_ref.shape[0] > 1:
                s_ref = s_ref.at[pl.ds(plan.me // (math.prod(factors) // s_ref.shape[0]), 1)]
            own = epilogue(_reduce_scatter(plan, sems, 0, x_ref, rbufs, pending)[...], s_ref)
        elif epilogue is not None:
            own = epilogue(x_ref[...], s_ref.at[pl.ds(plan.me, 1)])
        else:
            own = x_ref[...]
        _all_gather(plan, sems, 2, gbuf, own, pending)
        if mode == "gather" and len(y_ref.shape) == 3:
            n = math.prod(factors)
            share = own.shape[-1]
            per = y_ref.shape[-1] // share
            for j in range(n):
                y_ref[j // per, :, pl.ds((j % per) * share, share)] = gbuf[_digits(j, factors)]
        else:
            y_ref[...] = gbuf[...]
    for c in pending:
        c.wait_send()


def _digits(j, factors):
    return tuple((j // math.prod(factors[:s])) % factors[s] for s in reversed(range(len(factors))))


def _product_gram_kernel(x_ref, s_ref, y_ref, g_ref, *rest, row_factors, col_factors):
    rows = _Plan("row", row_factors)
    cols = _Plan("col", col_factors)
    rbufs = rest[:rows.stages]
    gbuf = rest[rows.stages]
    cbufs = rest[rows.stages + 1:rows.stages + 1 + cols.stages]
    sems = rest[-1]
    _barrier([rows, cols])
    pending = []
    degree = s_ref[pl.ds(rows.me // (math.prod(row_factors) // s_ref.shape[0]), 1)]
    scale = 1.0 / jnp.sqrt(degree.astype(jnp.float32))
    own = _reduce_scatter(rows, sems, 0, x_ref, rbufs, pending)[...] * scale
    _all_gather(rows, sems, 2, gbuf, own, pending)
    y_ref[...] = gbuf[...]
    n = math.prod(row_factors)
    per = y_ref.shape[-2]
    width = g_ref.shape[0]
    gram = None
    for p in range(n * per // width):
        parts = [y_ref[_digits(p * width // per + i, row_factors)] for i in range(width // per)]
        block = jnp.concatenate(parts, axis=0)
        padded = jnp.concatenate([block, jnp.zeros_like(block)], axis=0)
        term = lax.dot_general(block, padded, (((1,), (1,)), ((), ())), precision=HIGH,
                               preferred_element_type=jnp.float32)
        gram = term if gram is None else gram + term
    total = _sum(cols, sems, 4, gram, cbufs, pending)
    row = lax.broadcasted_iota(jnp.int32, total.shape, 0)
    lane = lax.broadcasted_iota(jnp.int32, total.shape, 1)
    g_ref[...] = _eliminate(total + jnp.where(lane == row + width, 1.0, 0.0))
    for c in pending:
        c.wait_send()


def product_gram(x, scale, row_factors, col_factors, cid, width):
    n = math.prod(row_factors)
    chunk = x.shape[1:]
    x = x.reshape(tuple(reversed(row_factors)) + chunk)
    scratch = []
    for s in range(len(row_factors)):
        scratch.append(pltpu.VMEM((row_factors[s],) + tuple(reversed(row_factors[s + 1:])) + chunk,
                                  jnp.float32))
    scratch.append(pltpu.VMEM(tuple(reversed(row_factors)) + chunk, jnp.float32))
    for s in range(len(col_factors)):
        scratch.append(pltpu.VMEM((col_factors[s], width, 2 * width), jnp.float32))
    scratch.append(pltpu.SemaphoreType.DMA((6, max(len(row_factors), len(col_factors)),
                                            max(row_factors + col_factors))))
    nbytes = n * math.prod(chunk) * 4
    y, g = pl.pallas_call(
        functools.partial(_product_gram_kernel, row_factors=tuple(row_factors),
                          col_factors=tuple(col_factors)),
        out_shape=(jax.ShapeDtypeStruct(tuple(reversed(row_factors)) + chunk, jnp.float32),
                   jax.ShapeDtypeStruct((width, 2 * width), jnp.float32)),
        in_specs=[pl.BlockSpec(memory_space=pltpu.VMEM)] * 2,
        out_specs=(pl.BlockSpec(memory_space=pltpu.VMEM), pl.BlockSpec(memory_space=pltpu.VMEM)),
        scratch_shapes=scratch,
        compiler_params=pltpu.CompilerParams(collective_id=cid, has_side_effects=True),
        cost_estimate=pl.CostEstimate(flops=0, transcendentals=0, bytes_accessed=2 * nbytes),
    )(x, scale)
    return y.reshape((n,) + chunk), g[:, width:]


def staged(x, axis, factors, mode, cid, scale=None, epilogue=None, out_dtype=None, tiled=None):
    n = math.prod(factors)
    stages = len(factors)
    out_dtype = out_dtype or x.dtype
    if mode == "reduce":
        chunk = x.shape[1:]
        x = x.reshape(tuple(reversed(factors)) + chunk)
    else:
        chunk = x.shape
    scratch = []
    if mode in ("reduce", "sum"):
        for s in range(stages):
            rest = tuple(reversed(factors[s + 1:])) if mode == "reduce" else ()
            scratch.append(pltpu.VMEM((factors[s],) + rest + chunk, jnp.float32))
    if mode != "sum":
        scratch.append(pltpu.VMEM(tuple(reversed(factors)) + chunk, out_dtype))
    scratch.append(pltpu.SemaphoreType.DMA((4, stages, max(factors))))
    if mode == "sum":
        out_shape = chunk
    elif tiled is not None:
        out_shape = tiled
    else:
        out_shape = tuple(reversed(factors)) + chunk
    args = (x,) if scale is None else (x, scale)
    nbytes = n * math.prod(chunk) * 4
    y = pl.pallas_call(
        functools.partial(_staged_kernel, axis=axis, factors=tuple(factors), mode=mode,
                          has_scale=scale is not None, epilogue=epilogue),
        out_shape=jax.ShapeDtypeStruct(out_shape, out_dtype),
        in_specs=[pl.BlockSpec(memory_space=pltpu.VMEM)] * len(args),
        out_specs=pl.BlockSpec(memory_space=pltpu.VMEM),
        scratch_shapes=scratch,
        compiler_params=pltpu.CompilerParams(collective_id=cid, has_side_effects=True),
        cost_estimate=pl.CostEstimate(flops=0, transcendentals=0, bytes_accessed=2 * nbytes),
    )(*args)
    if mode == "sum" or tiled is not None:
        return y
    return y.reshape((n,) + chunk)


QUERY_FACTORS = (2, 4, 4)
GRAM_FACTORS = (4, 8)
ROW_FACTORS = (4, 4)


def _query_epilogue(total, degree_ref):
    return (total * (1.0 / jnp.sqrt(degree_ref[...].astype(jnp.float32)))).astype(jnp.bfloat16)


def _panel_epilogue(panel, degree_ref):
    scale = 1.0 / jnp.sqrt(degree_ref[...].astype(jnp.float32))
    return (panel * scale).astype(jnp.bfloat16)


def _product_epilogue(total, s_ref):
    return total * s_ref[...]


GROUP = 8


def _products_kernel(*refs, forward, lift):
    if lift:
        ids_ref, count_ref, inv_ref, lifted_ref, scale_ref, tiles_hbm, out_ref, tiles, sems, src_ref = refs
    else:
        ids_ref, count_ref, src_ref, tiles_hbm, out_ref, tiles, sems = refs
    slots = tiles.shape[0]
    groups = slots // GROUP

    def fetch(g):
        return pltpu.make_async_copy(
            tiles_hbm.at[pl.ds(g * GROUP, GROUP)], tiles.at[pl.ds(g * GROUP, GROUP)], sems.at[g]
        )

    for g in range(groups):
        fetch(g).start()
    if lift:
        inv = inv_ref[...]
        for p in range(src_ref.shape[0]):
            current = jnp.dot(inv, lifted_ref[p], precision=HIGH, preferred_element_type=jnp.float32)
            scale = 1.0 / jnp.sqrt(scale_ref[p].astype(jnp.float32))
            src_ref[p] = (current * scale).astype(src_ref.dtype)
    out_ref[...] = jnp.zeros_like(out_ref)
    src_row, dst_row = (1, 0) if forward else (0, 1)
    count = count_ref[0]
    for g in range(groups):
        fetch(g).wait()
        ys = []
        for k in range(g * GROUP, (g + 1) * GROUP):
            x = src_ref[ids_ref[src_row, k]]
            t = tiles[k]
            if forward:
                y = lax.dot_general(x, t, (((1,), (1,)), ((), ())),
                                    preferred_element_type=jnp.float32)
            else:
                y = jnp.dot(x, t, preferred_element_type=jnp.float32)
            ys.append(jnp.where(k < count, y, 0.0))
        for k, y in zip(range(g * GROUP, (g + 1) * GROUP), ys):
            d = ids_ref[dst_row, k]
            out_ref[d] = out_ref[d] + y


def tile_products(slot_ids, live_count, src, tile_set, blocks, forward, lift=None):
    slots, side, _ = tile_set.shape
    width = src.shape[1] if lift is None else lift[1].shape[1]
    scratch = [pltpu.VMEM(tile_set.shape, tile_set.dtype), pltpu.SemaphoreType.DMA((slots // GROUP,))]
    if lift is None:
        operands = (src,)
    else:
        operands = lift
        scratch.append(pltpu.VMEM(lift[1].shape, jnp.bfloat16))
    vmem = pl.BlockSpec(memory_space=pltpu.VMEM)
    smem = pl.BlockSpec(memory_space=pltpu.SMEM)
    return pl.pallas_call(
        functools.partial(_products_kernel, forward=forward, lift=lift is not None),
        out_shape=jax.ShapeDtypeStruct((blocks, width, side), jnp.float32),
        in_specs=[smem, smem] + [vmem] * len(operands) + [pl.BlockSpec(memory_space=pl.ANY)],
        out_specs=vmem,
        scratch_shapes=scratch,
        cost_estimate=pl.CostEstimate(
            flops=2 * slots * width * side * side, transcendentals=0,
            bytes_accessed=slots * side * side * 2 + blocks * width * side * 6,
        ),
    )(slot_ids, live_count.reshape(1), *operands, tile_set)


def _eliminate(m):
    rows, cols = m.shape
    row = lax.broadcasted_iota(jnp.int32, (rows, cols), 0)
    lane = lax.broadcasted_iota(jnp.int32, (rows, cols), 1)

    def step(j, m):
        pivot_row = jnp.sum(jnp.where(row == j, m, 0.0), axis=0, keepdims=True)
        pivot = jnp.sum(jnp.where(lane[:1] == j, pivot_row, 0.0), axis=1, keepdims=True)
        inv_root = 1.0 / jnp.sqrt(pivot)
        scaled_row = pivot_row * inv_root
        column = jnp.sum(jnp.where(lane == j, m, 0.0), axis=1, keepdims=True) * inv_root
        return jnp.where(row == j, scaled_row, jnp.where(row > j, m - column * scaled_row, m))

    return lax.fori_loop(0, rows, step, m, unroll=2)


def _lower_inverse_kernel(m_ref, out_ref):
    out_ref[...] = _eliminate(m_ref[...])


def lower_inverse(gram):
    width = gram.shape[0]
    augmented = jnp.concatenate([gram, jnp.eye(width, dtype=gram.dtype)], axis=1)
    reduced = pl.pallas_call(
        _lower_inverse_kernel,
        out_shape=jax.ShapeDtypeStruct(augmented.shape, augmented.dtype),
        in_specs=[pl.BlockSpec(memory_space=pltpu.VMEM)],
        out_specs=pl.BlockSpec(memory_space=pltpu.VMEM),
    )(augmented)
    return reduced[:, width:]


def lower_inverse_native(gram):
    lower = lax.linalg.cholesky(gram, symmetrize_input=False)
    eye = jnp.eye(gram.shape[0], dtype=gram.dtype)
    return lax.linalg.triangular_solve(lower, eye, left_side=True, lower=True)


def shards(tiles, tile_ids, tile_count, query_degree, product_degree, panel):
    tile_set = tiles[0, 0]
    slot_ids = tile_ids[0, 0]
    live_count = tile_count[0, 0]
    side = tile_set.shape[1]
    width = panel.shape[0]
    query_tiles = query_degree.shape[0] // side
    product_tiles = product_degree.shape[0] // side
    n_row = lax.axis_size("row")
    n_col = lax.axis_size("col")
    qscale = (1.0 / jnp.sqrt(query_degree.astype(jnp.float32))).reshape(query_tiles, 1, side)
    pscale = (1.0 / jnp.sqrt(product_degree.astype(jnp.float32))).reshape(product_tiles, 1, side)
    row_at = lax.axis_index("row")
    col_at = lax.axis_index("col")
    share = panel.shape[1]
    block = product_degree.shape[0]
    q_per_tile = n_col // query_tiles
    p_per_tile = n_row // product_tiles
    my_qscale = lax.dynamic_index_in_dim(qscale, col_at // q_per_tile, keepdims=False)
    my_pscale = lax.dynamic_index_in_dim(pscale, row_at // p_per_tile, keepdims=False)
    root_count = math.sqrt(product_degree.shape[0] * n_col)

    scaled_tiles = staged(panel, "row", ROW_FACTORS, "gather", 0,
                          scale=product_degree.reshape(n_row, share), epilogue=_panel_epilogue,
                          out_dtype=jnp.bfloat16, tiled=(product_tiles, width, side))
    per_tile = side // share
    for iteration in range(ITERS):
        if iteration:
            partial_sum = tile_products(slot_ids, live_count, None, tile_set, query_tiles, True,
                                        lift=(inverse, lifted_tiles,
                                              product_degree.reshape(product_tiles, 1, side)))
        else:
            partial_sum = tile_products(slot_ids, live_count, scaled_tiles, tile_set, query_tiles, True)
        query_tiles_panel = staged(
            partial_sum.reshape(n_col, width // q_per_tile, side), "col", QUERY_FACTORS, "reduce", 1,
            scale=query_degree.reshape(query_tiles, side), epilogue=_query_epilogue,
            out_dtype=jnp.bfloat16,
        ).reshape(query_tiles, width, side)
        product_partial = tile_products(
            slot_ids, live_count, query_tiles_panel, tile_set, product_tiles, False
        )
        lifted_pieces, inverse = product_gram(
            product_partial.reshape(n_row, width // p_per_tile, side),
            product_degree.reshape(product_tiles, side), ROW_FACTORS,
            GRAM_FACTORS, 2, width,
        )
        lifted_tiles = lifted_pieces.reshape(product_tiles, width, side)
    my_tile = lax.dynamic_index_in_dim(lifted_tiles, row_at // per_tile, keepdims=False)
    my_lifted = lax.dynamic_slice_in_dim(my_tile, (row_at % per_tile) * share, share, axis=1)
    return jnp.einsum("rs,si->ri", inverse, my_lifted, precision=HIGH) * root_count


def solution(mesh):
    in_specs = (
        P("row", "col", None, None, None),
        P("row", "col", None, None),
        P("row", "col"),
        P("row"),
        P("col"),
        P(None, ("col", "row")),
    )
    out_specs = P(None, ("col", "row"))
    return jax.shard_map(shards, mesh=mesh, in_specs=in_specs, out_specs=out_specs, check_vma=False)
```
